32 devices in a mesh: row: 2 (over x), col: 16 (over z, y, core).
Axes of the slice: x: 2, y: 2, z: 4, core: 2. Of those that a mesh axis runs over, the one named last changes fastest.
Arguments:
- hidden_in: bfloat16 [8192, 768], P('col', 'row'), may hold values from -6 to 6
- cotangent: bfloat16 [8192, 768], P('col', 'row'), may hold values from -6 to 6
- lengths: int32 [2], replicated, may hold values from 1024 to 4096, as said below
- w_query: bfloat16 [768, 768], P('col', 'row'), may hold values from -0.21875 to 0.21875
- w_key: bfloat16 [768, 768], P('col', 'row'), may hold values from -0.21875 to 0.21875
- w_value: bfloat16 [768, 768], P('col', 'row'), may hold values from -0.21875 to 0.21875
- w_output: bfloat16 [768, 768], P('row', 'col'), may hold values from -1.75 to 1.75
- w_inner: bfloat16 [768, 3072], P('col', 'row'), may hold values from -0.21875 to 0.21875
- w_outer: bfloat16 [3072, 768], P('row', 'col'), may hold values from -0.109375 to 0.109375
- b_query: bfloat16 [768], P(('row', 'col')), may hold values from -1.796875 to 1.796875
- b_value: bfloat16 [768], P(('row', 'col')), may hold values from -0.29882812 to 0.29882812
- b_output: bfloat16 [768], P(('row', 'col')), may hold values from -1.796875 to 1.796875
- b_inner: bfloat16 [3072], P(('row', 'col')), may hold values from -1.796875 to 1.796875
- b_outer: bfloat16 [768], P(('row', 'col')), may hold values from -1.796875 to 1.796875
- gain_one: bfloat16 [768], P(('row', 'col')), may hold values from 0.099609375 to 1.8984375
- shift_one: bfloat16 [768], P(('row', 'col')), may hold values from -1.796875 to 1.796875
- gain_two: bfloat16 [768], P(('row', 'col')), may hold values from 0.099609375 to 1.8984375
- shift_two: bfloat16 [768], P(('row', 'col')), may hold values from -1.796875 to 1.796875
Outputs:
- layer_out: bfloat16 [8192, 768], P('col', 'row')
- grad_in: float32 [8192, 768], P('col', 'row')
- grad_w_query: float32 [768, 768], P('col', 'row')
- grad_w_key: float32 [768, 768], P('col', 'row')
- grad_w_value: float32 [768, 768], P('col', 'row')
- grad_w_output: float32 [768, 768], P('row', 'col')
- grad_w_inner: float32 [768, 3072], P('col', 'row')
- grad_w_outer: float32 [3072, 768], P('row', 'col')
- grad_b_query: float32 [768], P(('row', 'col'))
- grad_b_value: float32 [768], P(('row', 'col'))
- grad_b_output: float32 [768], P(('row', 'col'))
- grad_b_inner: float32 [3072], P(('row', 'col'))
- grad_b_outer: float32 [768], P(('row', 'col'))
- grad_gain_one: float32 [768], P(('row', 'col'))
- grad_shift_one: float32 [768], P(('row', 'col'))
- grad_gain_two: float32 [768], P(('row', 'col'))
- grad_shift_two: float32 [768], P(('row', 'col'))
The draws below stay inside these ranges and needn't reach their ends.
Inputs may be any that keep to these rules, and one draw needn't show every extreme that they name: Sequence s occupies token slots s * 4096 to s * 4096 + lengths[s] - 1; the last sequence has exactly 4096 tokens in every draw.
All inputs are finite; a program needn't handle non-finite values.
Results may differ from the reference program's by a relative error of at most 0.014.
The reference program's roundings to bfloat16 on the way count: a program that leaves them out, or rounds other values in their place, can miss the bound.
Values may be sent and summed in bfloat16 or wider, within the bound.
A program may use at most 128 MiB of HBM per device.

```python
import jax
import jax.numpy as jnp
from jax import lax

D = 768
HEADS = 12
HEAD_DIM = 64
FF = 3072
TOK_DEV = 512
SEQ_CAP = 4096
LEN_MIN = 1024
SLOTS = 2
TOKENS = 8192


def draw_lengths(key, part):
    drawn = jax.random.randint(key, (SLOTS,), LEN_MIN, SEQ_CAP + 1, dtype=jnp.int32)
    return jnp.where(jnp.arange(SLOTS, dtype=jnp.int32) == SLOTS - 1, SEQ_CAP, drawn).astype(jnp.int32)


def block_levels(key, shape, split, low, high):
    level, own = 1.0, jax.random.fold_in(key, 6)
    for axis_at, shards_of in split:
        draws = jnp.exp(jax.random.uniform(jax.random.fold_in(own, axis_at), (shards_of,), jnp.float32, low / len(split), high / len(split)))
        level = level * jnp.repeat(draws, shape[axis_at] // shards_of).reshape([-1 if axis == axis_at else 1 for axis in range(len(shape))])
    return level


def normal_values(rng, shape, scale, reach, cuts=(), held_as=jnp.bfloat16):
    loudness = block_levels(rng, shape, cuts, -0.22, 0.18) if cuts else 1.0
    result = jax.random.normal(rng, shape, jnp.float32) * scale * loudness
    return jnp.minimum(jnp.maximum(result, -reach), reach).astype(held_as)


def setup_inputs(seed: int = 0) -> dict:
    streams_of = jax.random.split(jax.random.key(seed), 19)
    hidden_in = normal_values(streams_of[0], (TOKENS, D), 1.0, 6.0, ((0, 16), (1, 2)))
    cotangent = normal_values(streams_of[1], (TOKENS, D), 1.0, 6.0, ((0, 16), (1, 2)))
    lengths = draw_lengths(jax.random.fold_in(streams_of[18], 71), 0)
    w_query = normal_values(streams_of[3], (D, D), D ** -0.5, 0.21875, ((0, 16), (1, 2)))
    w_key = normal_values(streams_of[4], (D, D), D ** -0.5, 0.21875, ((0, 16), (1, 2)))
    w_value = normal_values(streams_of[5], (D, D), D ** -0.5, 0.21875, ((0, 16), (1, 2)))
    w_output = normal_values(streams_of[6], (D, D), (max(1, D * 64 // SEQ_CAP)) ** -0.5, 1.75, ((0, 2), (1, 16)))
    w_inner = normal_values(streams_of[7], (D, FF), D ** -0.5, 0.21875, ((0, 16), (1, 2)))
    w_outer = normal_values(streams_of[8], (FF, D), FF ** -0.5, 0.109375, ((0, 2), (1, 16)))
    b_query = normal_values(streams_of[9], (D,), 0.3, 1.796875, ((0, 32),))
    b_value = normal_values(streams_of[10], (D,), 0.05, 0.29882812, ((0, 32),))
    b_output = normal_values(streams_of[11], (D,), 0.3, 1.796875, ((0, 32),))
    b_inner = normal_values(streams_of[12], (FF,), 0.3, 1.796875, ((0, 32),))
    b_outer = normal_values(streams_of[13], (D,), 0.3, 1.796875, ((0, 32),))
    gain_one = jnp.clip(1.0 + 0.18 * jax.random.normal(streams_of[14], (D,), jnp.float32), 0.099609375, 1.8984375).astype(jnp.bfloat16)
    shift_one = normal_values(streams_of[15], (D,), 0.3, 1.796875, ((0, 32),))
    gain_two = jnp.clip(1.0 + 0.18 * jax.random.normal(streams_of[16], (D,), jnp.float32), 0.099609375, 1.8984375).astype(jnp.bfloat16)
    shift_two = normal_values(streams_of[17], (D,), 0.3, 1.796875, ((0, 32),))
    return {"hidden_in": hidden_in, "cotangent": cotangent, "lengths": lengths, "w_query": w_query, "w_key": w_key, "w_value": w_value, "w_output": w_output, "w_inner": w_inner, "w_outer": w_outer, "b_query": b_query, "b_value": b_value, "b_output": b_output, "b_inner": b_inner, "b_outer": b_outer, "gain_one": gain_one, "shift_one": shift_one, "gain_two": gain_two, "shift_two": shift_two}


EPSILON = 1e-12
HIGH = lax.Precision.HIGHEST

@jax.custom_vjp
def low(v):
    return lax.optimization_barrier(v.astype(jnp.bfloat16)).astype(jnp.float32)

@jax.custom_vjp
def low_back(v):
    return v

def low_keep(v):
    return (low(v), None)

def low_pass(kept, grad):
    return (grad,)

def back_keep(v):
    return (v, None)

def back_low(kept, grad):
    return (low(grad),)
low.defvjp(low_keep, low_pass)
low_back.defvjp(back_keep, back_low)

def matmul(left, right):
    return jnp.dot(left, right, precision=HIGH, preferred_element_type=jnp.float32)

def layer_norm(resid, gain, shift):
    center = resid - lax.optimization_barrier(jnp.mean(resid, axis=-1, keepdims=True))
    spread = lax.optimization_barrier(jnp.mean(center * center, axis=-1, keepdims=True))
    return center * lax.rsqrt(spread + EPSILON) * gain + shift

def gelu(argument):
    return 0.5 * argument * (1.0 + jax.scipy.special.erf(argument * 0.7071067811865476))

def attend_slot(operands):
    queries, keys, values, allowed = operands
    key_heads = keys.reshape(SEQ_CAP, HEADS, HEAD_DIM)
    value_heads = values.reshape(SEQ_CAP, HEADS, HEAD_DIM)

    def block(query_block):
        scores = jnp.einsum('qhd,khd->hqk', query_block, key_heads, precision=HIGH) * 0.125
        scores = low_back(scores)
        scores = jnp.where(allowed[None, None, :] > 0.5, scores, -1e+30)
        highest = lax.optimization_barrier(jnp.max(scores, axis=2, keepdims=True))
        weights = jnp.exp(scores - highest)
        probs = weights / lax.optimization_barrier(jnp.sum(weights, axis=2, keepdims=True))
        return jnp.einsum('hqk,khd->qhd', low(probs), value_heads, precision=HIGH)
    query_blocks = queries.reshape(SEQ_CAP // TOK_DEV, TOK_DEV, HEADS, HEAD_DIM)
    context = lax.map(jax.checkpoint(block), query_blocks)
    return context.reshape(SEQ_CAP, D)

def forward(hidden, w_query, w_key, w_value, w_output, w_inner, w_outer, b_query, b_value, b_output, b_inner, b_outer, gain_one, shift_one, gain_two, shift_two, keep_mask):
    queries = low(low_back(matmul(hidden, w_query) + b_query))
    keys = low(low_back(matmul(hidden, w_key)))
    values = low(low_back(matmul(hidden, w_value) + b_value))
    slot_count = TOKENS // SEQ_CAP
    operands = (queries.reshape(slot_count, SEQ_CAP, D), keys.reshape(slot_count, SEQ_CAP, D), values.reshape(slot_count, SEQ_CAP, D), keep_mask.reshape(slot_count, SEQ_CAP))
    context = lax.map(attend_slot, operands).reshape(TOKENS, D)
    context = low(low_back(context * keep_mask[:, None]))
    attn = low_back(matmul(context, w_output) + b_output)
    normed = layer_norm(hidden + attn, gain_one, shift_one)
    inner = low_back(matmul(low(normed), w_inner) + b_inner)
    outer = low_back(matmul(low(gelu(inner)), w_outer) + b_outer)
    return layer_norm(normed + outer, gain_two, shift_two)

def reference(hidden_in, cotangent, lengths, w_query, w_key, w_value, w_output, w_inner, w_outer, b_query, b_value, b_output, b_inner, b_outer, gain_one, shift_one, gain_two, shift_two):
    places = jnp.arange(TOKENS, dtype=jnp.int32)
    owners = (places // SEQ_CAP).astype(jnp.int32)
    keep_mask = (places % SEQ_CAP < lengths[owners]).astype(jnp.float32)
    floats = [argument.astype(jnp.float32) for argument in (hidden_in, w_query, w_key, w_value, w_output, w_inner, w_outer, b_query, b_value, b_output, b_inner, b_outer, gain_one, shift_one, gain_two, shift_two)]

    def closed(*params):
        return forward(*params, keep_mask)
    output, pull = jax.vjp(closed, *floats)
    grads = pull(cotangent.astype(jnp.float32) * keep_mask[:, None])
    return (output.astype(jnp.bfloat16), grads[0], grads[1], grads[2], grads[3], grads[4], grads[5], grads[6], grads[7], grads[8], grads[9], grads[10], grads[11], grads[12], grads[13], grads[14], grads[15])
```

```python
import functools

import jax
import jax.numpy as jnp
from jax import lax
from jax.experimental import pallas as pl
from jax.experimental.pallas import tpu as pltpu
from jax.sharding import PartitionSpec as P

D = 768
HALF = 384
HEAD_DIM = 64
FF_HALF = 1536
PAIRS = 3
SPAN = 8
EPSILON = 1e-12
MASKED = -1e30
MESH = pl.DeviceIdType.MESH
F32 = jnp.float32
BF16 = jnp.bfloat16
REST = HALF + 2 * FF_HALF
WIDE = REST + 128
QKV = 3 * HALF


def dot(left, right, contract):
    return lax.dot_general(left, right, (contract, ((), ())), preferred_element_type=F32)


NN = ((1,), (0,))
NT = ((1,), (1,))
TN = ((0,), (0,))


class Place:
    def __init__(self, size):
        self.size = size
        self.planes = size // 4
        self.r = lax.axis_index("row")
        col = lax.axis_index("col")
        self.base = lax.div(col, size) * size
        inner = lax.rem(col, size)
        self.slot = lax.div(col, SPAN)
        self.block = lax.rem(col, SPAN)
        self.z = lax.div(inner, 4)
        self.y = lax.rem(lax.div(inner, 2), 2)
        self.j = lax.rem(inner, 2)
        self.zl = lax.rem(self.z, 2)

    def plane(self, step):
        return lax.rem(self.z + step + self.planes, self.planes)

    def device(self, r, z, y, j):
        return (r, self.base + z * 4 + y * 2 + j)

    def to_z(self, step):
        return self.device(self.r, self.plane(step), self.y, self.j)

    def to_z_near(self):
        return self.device(self.r, self.z - self.zl + (1 - self.zl), self.y, self.j)

    def to_y(self):
        return self.device(self.r, self.z, 1 - self.y, self.j)

    def to_x(self):
        return self.device(1 - self.r, self.z, self.y, self.j)

    def to_core(self):
        return self.device(self.r, self.z, self.y, 1 - self.j)

    def col_block(self, z, y, j):
        return z * 4 + y * 2 + j

    def any_block(self, r, z, y, j):
        return r * self.size + z * 4 + y * 2 + j

    def near_block(self, dz, dy, j):
        return lax.rem(self.zl + dz, 2) * 4 + lax.rem(self.y + dy, 2) * 2 + j


def meet(place):
    barrier = pltpu.get_barrier_semaphore()
    peers = [place.to_z(step) for step in range(1, place.planes)]
    peers += [place.to_y(), place.to_x(), place.to_core()]
    for peer in peers:
        pl.semaphore_signal(barrier, inc=1, device_id=peer, device_id_type=MESH)
    pl.semaphore_wait(barrier, len(peers))


def send(src, dst, sems, index, peer):
    return pltpu.make_async_remote_copy(
        src_ref=src,
        dst_ref=dst,
        send_sem=sems[0].at[index],
        recv_sem=sems[1].at[index],
        device_id=peer,
        device_id_type=MESH,
    )


class Gather:
    def __init__(self, place, own, full, sems, with_rows):
        self.place, self.own, self.full, self.sems = place, own, full, sems
        self.rows = 2 if with_rows else 1
        self.with_rows = with_rows
        n = place.planes
        self.at_y = n - 1
        self.at_x = self.at_y + n
        self.at_c = self.at_x + (2 * n if with_rows else 0)
        self.total = self.at_c + 2 * n * self.rows

    def index(self, n, k, m, j):
        p = self.place
        z, y = p.plane(-k), lax.rem(p.y + m, 2)
        if self.with_rows:
            return p.any_block(lax.rem(p.r + n, 2), z, y, j)
        return p.col_block(z, y, j)

    def move(self, number, peer, n, k, m, j, local):
        where = self.index(n, k, m, j)
        src = self.own if local else self.full.at[where]
        return send(src, self.full.at[where], self.sems, number, peer)

    def z_sends(self):
        p = self.place
        for step in range(1, p.planes):
            self.move(step - 1, p.to_z(step), 0, 0, 0, p.j, True).start()

    def z_done(self, k):
        p = self.place
        self.move(k - 1, p.to_z(k), 0, k, 0, p.j, False).wait_recv()

    def y_send(self, k):
        p = self.place
        self.move(self.at_y + k, p.to_y(), 0, k, 0, p.j, k == 0).start()

    def y_done(self, k):
        p = self.place
        self.move(self.at_y + k, p.to_y(), 0, k, 1, p.j, False).wait_recv()

    def x_send(self, k, m):
        p = self.place
        self.move(self.at_x + 2 * k + m, p.to_x(), 0, k, m, p.j, k + m == 0).start()

    def x_done(self, k, m):
        p = self.place
        self.move(self.at_x + 2 * k + m, p.to_x(), 1, k, m, p.j, False).wait_recv()

    def c_number(self, n, k, m):
        return self.at_c + (2 * k + m) * self.rows + n

    def c_send(self, n, k, m):
        p = self.place
        number = self.c_number(n, k, m)
        self.move(number, p.to_core(), n, k, m, p.j, n + k + m == 0).start()

    def c_done(self, n, k, m):
        p = self.place
        self.move(self.c_number(n, k, m), p.to_core(), n, k, m, 1 - p.j, False).wait_recv()

    def all_sent(self):
        for number in range(self.total):
            send(self.own, self.own, self.sems, number, self.place.to_core()).wait_send()


def kernel_a(
    size,
    lengths,
    hid,
    wq_in,
    bq_in,
    wr_in,
    cot,
    hid_out,
    wq_out,
    q_out,
    kv_out,
    p_out,
    m_out,
    lse_out,
    ctxt_out,
    ctx_out,
    cot_out,
    wr_all,
    hid_all,
    wq_all,
    bq_all,
    kv,
    qs,
    qm,
    acc,
    high,
    low,
    pbuf,
    ctx_tp,
    wr_send,
    wr_recv,
    wq_send,
    wq_recv,
    bq_send,
    bq_recv,
    kv_send,
    kv_recv,
    one_send,
    one_recv,
    local,
    p_sem,
):
    place = Place(size)
    rows = hid.shape[0]
    part = rows // 2
    n = place.planes
    r, y, j = place.r, place.y, place.j
    meet(place)

    single = (one_send, one_recv)
    own_rows = pl.ds(pl.multiple_of(r * part, part), part)
    other_rows = pl.ds(pl.multiple_of((1 - r) * part, part), part)
    to_hid = send(hid, hid_all.at[r], single, 0, place.to_x())
    to_hid.start()
    wq = Gather(place, wq_in, wq_all, (wq_send, wq_recv), False)
    bq = Gather(place, bq_in, bq_all, (bq_send, bq_recv), False)
    rest = Gather(place, wr_in, wr_all, (wr_send, wr_recv), True)
    for gather in (wq, bq):
        gather.z_sends()
        gather.y_send(0)
        gather.c_send(0, 0, 0)
    to_cot = send(cot.at[other_rows], cot_out.at[r], single, 1, place.to_x())
    to_cot.start()
    rest_local = pltpu.make_async_copy(
        wr_in, wr_all.at[place.any_block(r, place.z, y, j)], local.at[0]
    )
    rest_local.start()
    cot_local = pltpu.make_async_copy(cot.at[own_rows], cot_out.at[r], local.at[1])
    cot_local.start()
    hid_all[r] = hid[...]
    wq_all[place.col_block(place.z, y, j)] = wq_in[...]
    bq_all[place.col_block(place.z, y, j)] = bq_in[...]
    for k in range(1, n):
        for gather in (wq, bq):
            gather.z_done(k)
            gather.y_send(k)
            gather.c_send(0, k, 0)
    for k in range(n):
        for gather in (wq, bq):
            gather.y_done(k)
            gather.c_send(0, k, 1)
    rest.z_sends()
    rest.y_send(0)
    rest.x_send(0, 0)
    rest.c_send(0, 0, 0)
    for k in range(n):
        for m in range(2):
            for gather in (wq, bq):
                gather.c_done(0, k, m)
    send(hid, hid_all.at[1 - r], single, 0, place.to_x()).wait_recv()

    hid_local = pltpu.make_async_copy(hid_all, hid_out, local.at[2])
    hid_local.start()
    wq_local = pltpu.make_async_copy(wq_all, wq_out, local.at[3])
    wq_local.start()

    biases = jnp.sum(bq_all[...].astype(F32), axis=0)
    own = place.near_block(0, 0, j)
    half = size // 2
    for which in (1, 2, 0):
        columns = slice(which * HALF, (which + 1) * HALF)
        total = dot(hid_all[0], wq_all[:half, :, columns].reshape(HALF, HALF), NN)
        total += dot(hid_all[1], wq_all[half:, :, columns].reshape(HALF, HALF), NN)
        if which == 0:
            total += biases[0:1]
        if which == 2:
            total += biases[1:2]
        total = total.astype(BF16)
        for p in range(PAIRS):
            piece = total[:, p * 128 : (p + 1) * 128]
            if which == 0:
                lane = lax.broadcasted_iota(jnp.int32, (rows, 128), 1)
                piece = piece * jnp.asarray(0.125, BF16)
                qs[p] = piece
                qm[2 * p] = jnp.where(lane < HEAD_DIM, piece, jnp.zeros_like(piece))
                qm[2 * p + 1] = jnp.where(lane >= HEAD_DIM, piece, jnp.zeros_like(piece))
            else:
                kv[own, (which - 1) * PAIRS + p] = piece
    acc[...] = jnp.zeros_like(acc)
    high[...] = jnp.full_like(high, MASKED)
    low[...] = jnp.zeros_like(low)

    n_one = place.device(r, place.z - place.zl + lax.rem(place.zl + 1 - j, 2), lax.rem(y + j, 2), j)
    n_two = place.device(r, place.z - place.zl + lax.rem(place.zl + j, 2), lax.rem(y + 1 - j, 2), j)
    kvs = (kv_send, kv_recv)

    def kv_block(i):
        pair, core = lax.div(i, 2), lax.rem(j + lax.rem(i, 2), 2)
        b0, b1 = lax.rem(pair, 2), lax.div(pair, 2)
        return place.near_block(b0 * (1 - core) + b1 * core, b0 * core + b1 * (1 - core), core)

    def kv_move(number, what, peer):
        where = kv_block(what)
        return send(kv.at[where], kv.at[where], kvs, number, peer)

    kv_move(1, 0, place.to_core()).start()
    kv_move(2, 0, n_one).start()
    q_local = pltpu.make_async_copy(qs, q_out, local.at[4])
    q_local.start()

    def arrived(number):
        kv_move(number, number, n_one).wait_recv()

    def at_5():
        kv_move(2, 0, n_one).wait_send()
        kv_move(4, 0, n_two).start()
        arrived(2)
        kv_move(3, 2, place.to_core()).start()

    def at_11():
        kv_move(4, 0, n_two).wait_send()
        kv_move(6, 2, n_two).start()
        arrived(4)
        kv_move(5, 4, place.to_core()).start()

    def at_18():
        arrived(6)
        kv_move(7, 6, place.to_core()).start()

    def rest_y(k):
        rest.z_done(k)
        rest.y_send(k)
        rest.x_send(k, 0)
        rest.c_send(0, k, 0)

    def rest_x(k):
        rest.y_done(k)
        rest.x_send(k, 1)
        rest.c_send(0, k, 1)

    def rest_c(k, m):
        rest.x_done(k, m)
        rest.c_send(1, k, m)

    events = {
        3: [lambda: arrived(1)],
        5: [at_5],
        9: [lambda: arrived(3)],
        11: [at_11],
        15: [lambda: arrived(5)],
        18: [at_18],
        21: [lambda: arrived(7)],
    }

    def add(step, *what):
        events.setdefault(step, []).extend(what)

    spots = [6, 8, 10]
    for k in range(1, n):
        add(spots[k - 1], functools.partial(rest_y, k))
    for k in range(n):
        add(12 + k, functools.partial(rest_x, k))
    for k in range(n):
        add(16 + 2 * k, functools.partial(rest_c, k, 0))
        add(17 + 2 * k, functools.partial(rest_c, k, 1))

    length = lengths[place.slot]

    def p_copy(t, slot):
        i, p = lax.div(t, PAIRS), lax.rem(t, PAIRS)
        return pltpu.make_async_copy(
            pbuf.at[slot], p_out.at[kv_block(i), pl.ds(2 * p, 2)], p_sem.at[slot]
        )

    def kv_copy(i):
        where = kv_block(i)
        return pltpu.make_async_copy(kv.at[where], kv_out.at[where], local.at[8 + i])

    steps = SPAN * PAIRS

    def attend(t, carry):
        i, p = lax.div(t, PAIRS), lax.rem(t, PAIRS)
        for step, calls in sorted(events.items()):

            @pl.when(t == step)
            def _(calls=calls):
                for call in calls:
                    call()

        @pl.when(p == 0)
        def _():
            kv_copy(i).start()

        slot = lax.rem(t, 2)

        @pl.when(t >= 2)
        def _():
            p_copy(t - 2, slot).wait()

        where = kv_block(i)
        place_of = lax.broadcasted_iota(jnp.int32, (rows, 128), 0) + where * rows
        bias = jnp.where(place_of < length, 0.0, MASKED)
        bias = jnp.concatenate([bias] * (rows // 128), axis=1)
        key = kv[where, p]
        value_t = kv[where, PAIRS + p].T
        for h in range(2):
            g = 2 * p + h
            scores = dot(key, qm[g], NT) + bias
            top = jnp.max(scores, axis=0, keepdims=True)
            weights = jnp.exp(scores - top)
            below = jnp.sum(weights, axis=0, keepdims=True)
            rounded = weights.astype(BF16)
            pbuf[slot, h] = rounded
            term = dot(value_t[h * HEAD_DIM : (h + 1) * HEAD_DIM], rounded, NN)
            old = high[g]
            new = jnp.maximum(old, top)
            keep_old, keep_new = jnp.exp(old - new), jnp.exp(top - new)
            high[g] = new
            low[g] = low[g] * keep_old + below * keep_new
            acc[g] = acc[g] * keep_old + term * keep_new
            m_out[where, g] = top
        p_copy(t, slot).start()
        return carry

    lax.fori_loop(0, steps, attend, jnp.int32(0))

    column = lax.broadcasted_iota(jnp.int32, (1, rows), 1) + place.block * rows
    keep = jnp.where(column < length, 1.0, 0.0)
    for p in range(PAIRS):
        parts = []
        for h in range(2):
            g = 2 * p + h
            lse_out[g] = high[g] + jnp.log(low[g])
            parts.append(acc[g] / low[g])
        both = jnp.concatenate(parts, axis=0)
        ctxt_out[p] = both
        ctx_tp[:, p * 128 : (p + 1) * 128] = (both * keep).T.astype(BF16)
    for t in (steps - 2, steps - 1):
        p_copy(jnp.int32(t), t % 2).wait()
    to_ctx = send(ctx_tp.at[other_rows], ctx_out.at[r], single, 2, place.to_x())
    to_ctx.start()
    ctx_local = pltpu.make_async_copy(ctx_tp.at[own_rows], ctx_out.at[r], local.at[5])
    ctx_local.start()
    for n_at in range(2):
        for k in range(n):
            for m in range(2):
                rest.c_done(n_at, k, m)
    for gather in (wq, bq, rest):
        gather.all_sent()
    for number in (1, 3, 4, 5, 6, 7):
        if number != 4:
            kv_move(number, 0, n_one).wait_send()
    for number, ref in ((0, hid_all), (1, cot_out), (2, ctx_out)):
        if number:
            send(ref.at[1 - r], ref.at[1 - r], single, number, place.to_x()).wait_recv()
        send(ref.at[1 - r], ref.at[1 - r], single, number, place.to_x()).wait_send()
    for copy in (rest_local, cot_local, hid_local, wq_local, q_local, ctx_local):
        copy.wait()
    for i in range(SPAN):
        kv_copy(jnp.int32(i)).wait()


def forward_attention(size, lengths, hid, wq_in, bq_in, wr_in, cot):
    rows = hid.shape[0]
    part = rows // 2
    blk = wq_in.shape[0]
    n = size // 4
    any_space = pl.BlockSpec(memory_space=pl.ANY)
    vmem = pl.BlockSpec(memory_space=pltpu.VMEM)
    shape = jax.ShapeDtypeStruct
    n_col, n_all = (n - 1) + n + 2 * n, (n - 1) + n + 2 * n + 4 * n
    dma = pltpu.SemaphoreType.DMA
    return pl.pallas_call(
        functools.partial(kernel_a, size),
        out_shape=(
            shape((2, rows, HALF), BF16),
            shape((size, blk, QKV), BF16),
            shape((PAIRS, rows, 128), BF16),
            shape((SPAN, 2 * PAIRS, rows, 128), BF16),
            shape((SPAN, 2 * PAIRS, rows, rows), BF16),
            shape((SPAN, 2 * PAIRS, 1, rows), F32),
            shape((2 * PAIRS, 1, rows), F32),
            shape((PAIRS, 128, rows), F32),
            shape((2, part, HALF), BF16),
            shape((2, part, HALF), BF16),
            shape((2 * size, blk, WIDE), BF16),
        ),
        in_specs=[pl.BlockSpec(memory_space=pltpu.SMEM)] + [vmem] * 5,
        out_specs=[any_space] * 5 + [vmem] * 3 + [any_space] * 3,
        scratch_shapes=[
            pltpu.VMEM((2, rows, HALF), BF16),
            pltpu.VMEM((size, blk, QKV), BF16),
            pltpu.VMEM((size, 16, HALF), BF16),
            pltpu.VMEM((SPAN, 2 * PAIRS, rows, 128), BF16),
            pltpu.VMEM((PAIRS, rows, 128), BF16),
            pltpu.VMEM((2 * PAIRS, rows, 128), BF16),
            pltpu.VMEM((2 * PAIRS, HEAD_DIM, rows), F32),
            pltpu.VMEM((2 * PAIRS, 1, rows), F32),
            pltpu.VMEM((2 * PAIRS, 1, rows), F32),
            pltpu.VMEM((2, 2, rows, rows), BF16),
            pltpu.VMEM((rows, HALF), BF16),
            dma((n_all,)),
            dma((n_all,)),
            dma((n_col,)),
            dma((n_col,)),
            dma((n_col,)),
            dma((n_col,)),
            dma((8,)),
            dma((8,)),
            dma((3,)),
            dma((3,)),
            dma((16,)),
            dma((2,)),
        ],
        compiler_params=pltpu.CompilerParams(
            collective_id=0, has_side_effects=True, vmem_limit_bytes=60 * 2**20
        ),
        name="forward_attention",
    )(lengths, hid, wq_in, bq_in, wr_in, cot)


def kernel_c(
    size,
    dctx,
    qs,
    m_in,
    lse_in,
    ctxt,
    hid_all,
    wq_all,
    lay,
    dres_low,
    dres_own,
    kv_in,
    p_in,
    g_in,
    rest_out,
    qkv_out,
    bias_out,
    grad_out,
    lay_out,
    d_ctx,
    dtot,
    delta,
    qm,
    acc,
    kv,
    pbuf,
    big,
    cb,
    rb,
    st,
    b1,
    b2,
    b3,
    b4,
    d_all,
    gq,
    q1,
    q2,
    q3,
    near,
    dres_far,
    bias_own,
    bias_got,
    one_send,
    one_recv,
    kv_send,
    kv_recv,
    g_send,
    g_recv,
    q_send,
    q_recv,
    s_send,
    s_recv,
    load,
    p_sem,
):
    place = Place(size)
    rows = qs.shape[1]
    part = rows // 2
    n = place.planes
    r, y, j = place.r, place.y, place.j
    meet(place)
    single = (one_send, one_recv)
    gs = (g_send, g_recv)
    ks = (kv_send, kv_recv)
    at_x, at_y, at_z = 4 * n, 6 * n, 7 * n

    own_rows = pl.ds(pl.multiple_of(r * part, part), part)
    other_rows = pl.ds(pl.multiple_of((1 - r) * part, part), part)
    send(dctx.at[1 - r], d_ctx.at[own_rows], single, 0, place.to_x()).start()

    def g_block(index, core):
        n_at, m, k = lax.div(index, 2 * n), lax.rem(lax.div(index, n), 2), lax.rem(index, n)
        return place.any_block(
            lax.rem(r + 1 + n_at, 2), place.plane(k), lax.rem(y + 1 + m, 2), core
        )

    def c_move(index):
        return send(g_in.at[g_block(index, 1 - j)], b1.at[index], gs, index, place.to_core())

    def g_load(index):
        return pltpu.make_async_copy(g_in.at[g_block(index, j)], st.at[index], load.at[8 + index])

    def loop(count, body):
        def step(index, carry):
            body(index)
            return carry

        lax.fori_loop(0, count, step, jnp.int32(0))

    loop(4 * n, lambda index: c_move(index).start())
    loop(4 * n, lambda index: g_load(index).start())

    def b_block(i):
        pair, core = lax.div(i, 2), lax.rem(j + 1 + lax.rem(i, 2), 2)
        return place.near_block(1 - lax.div(pair, 2), 1 - lax.rem(pair, 2), core)

    def kv_load(i):
        return pltpu.make_async_copy(kv_in.at[b_block(i)], kv.at[i], load.at[i])

    def p_load(t, slot):
        i, p = lax.div(t, PAIRS), lax.rem(t, PAIRS)
        return pltpu.make_async_copy(
            p_in.at[b_block(i), pl.ds(2 * p, 2)], pbuf.at[slot], p_sem.at[slot]
        )

    p_load(jnp.int32(0), 0).start()
    loop(SPAN, lambda i: kv_load(i).start())

    lane = lax.broadcasted_iota(jnp.int32, (rows, 128), 1)
    for p in range(PAIRS):
        piece = qs[p]
        qm[2 * p] = jnp.where(lane < HEAD_DIM, piece, jnp.zeros_like(piece))
        qm[2 * p + 1] = jnp.where(lane >= HEAD_DIM, piece, jnp.zeros_like(piece))
    acc[...] = jnp.zeros_like(acc)
    lay_local = pltpu.make_async_copy(lay.at[r], lay_out.at[own_rows], load.at[8 + 4 * n])
    lay_local.start()
    d_ctx[own_rows, :] = dctx[r]
    send(dctx.at[1 - r], d_ctx.at[other_rows], single, 0, place.to_x()).wait_recv()
    send(lay.at[1 - r], lay_out.at[own_rows], single, 1, place.to_x()).start()
    send(dres_low.at[1 - r], dres_far, single, 2, place.to_x()).start()
    upper = lax.broadcasted_iota(jnp.int32, (128, rows), 0) < HEAD_DIM
    for p in range(PAIRS):
        turned = d_ctx[:, p * 128 : (p + 1) * 128].astype(F32).T
        product = turned * ctxt[p]
        delta[2 * p] = jnp.sum(product[:HEAD_DIM], axis=0, keepdims=True)
        delta[2 * p + 1] = jnp.sum(product[HEAD_DIM:], axis=0, keepdims=True)
        dtot[2 * p] = jnp.where(upper, turned, 0.0)
        dtot[2 * p + 1] = jnp.where(upper, 0.0, turned)

    def core_send(pair):
        return send(big.at[2 * pair], cb.at[pair], ks, pair, place.to_core())

    def core_add(pair):
        core_send(pair).wait_recv()
        for piece in range(2 * PAIRS):
            total = big[2 * pair + 1, piece].astype(F32) + cb[pair, piece].astype(F32)
            big[2 * pair + 1, piece] = total.astype(BF16)

    keys, values = pl.ds(0, PAIRS), pl.ds(PAIRS, PAIRS)

    def hop(number):
        pair, part_of, along_z = (
            (0, keys, False),
            (0, values, True),
            (1, keys, True),
            (1, values, True),
            (2, values, False),
            (2, keys, False),
        )[number]
        peer = place.to_z_near() if along_z else place.to_y()
        return send(big.at[2 * pair + 1, part_of], rb.at[number], ks, 4 + number, peer)

    def hop_add(number, pair, start):
        hop(number).wait_recv()
        for piece in range(PAIRS):
            total = big[2 * pair + 1, start + piece].astype(F32) + rb[number, piece].astype(F32)
            big[2 * pair + 1, start + piece] = total.astype(BF16)

    def fold(target, source, at):
        total = target[at].astype(F32) + source.astype(F32)
        target[at] = total.astype(BF16)

    def g_core_add(index):
        c_move(index).wait_recv()
        g_load(index).wait()
        fold(st, b1[index], index)

    def g_x_send(index):
        return send(st.at[index], b2.at[index], gs, at_x + index, place.to_x())

    def g_x_add(index):
        g_x_send(index).wait_recv()
        fold(st, b2[index], 2 * n + index)

    def g_y_send(k):
        return send(st.at[2 * n + k], b3.at[k], gs, at_y + k, place.to_y())

    def g_y_add(k):
        g_y_send(k).wait_recv()
        fold(st, b3[k], 3 * n + k)

    def g_z_send(k):
        return send(st.at[3 * n + k], b4.at[k - 1], gs, at_z + k - 1, place.to_z(k))

    events = {}

    def add(step, what, *inputs):
        events.setdefault(step, []).append(functools.partial(what, *inputs))

    def start(what, number):
        what(number).start()

    for at in range(n):
        add(at, lambda at: loop(2, lambda i: g_core_add(2 * at + i)), at)
        add(at + 1, lambda at: loop(2, lambda i: g_x_send(2 * at + i).start()), at)
    for at in range(n):
        add(n + 1 + at, lambda at: loop(2, lambda i: g_core_add(2 * n + 2 * at + i)), at)
    for pair in range(4):
        add(6 * pair + 3, start, core_send, pair)
        if pair < 3:
            add(6 * pair + 6, core_add, pair)
    add(7, start, hop, 0)
    add(7, start, hop, 1)
    add(13, start, hop, 3)
    add(17, hop_add, 0, 1, 0)
    add(18, start, hop, 2)
    add(19, start, hop, 5)
    add(20, hop_add, 1, 2, PAIRS)
    add(21, start, hop, 4)

    steps = SPAN * PAIRS

    def back(t, carry):
        i, p = lax.div(t, PAIRS), lax.rem(t, PAIRS)
        for step, calls in sorted(events.items()):

            @pl.when(t == step)
            def _(calls=calls):
                for call in calls:
                    call()

        slot = lax.rem(t, 2)

        @pl.when(t + 1 < steps)
        def _():
            p_load(t + 1, 1 - slot).start()

        @pl.when(p == 0)
        def _():
            kv_load(i).wait()

        p_load(t, slot).wait()
        where = b_block(i)
        key = kv[i, p]
        value = kv[i, PAIRS + p]
        key_t = key.T
        d_key = d_value = None
        for h in range(2):
            g = 2 * p + h
            factor = jnp.exp(m_in[where, g] - lse_in[g])
            d_rows = (dtot[g] * factor).astype(BF16)
            weights = pbuf[slot, h]
            d_probs = dot(value, d_rows, NN)
            d_scores = (weights.astype(F32) * (d_probs - delta[g] * factor)).astype(BF16)
            value_term = dot(weights, d_rows, NT)
            key_term = dot(d_scores, qm[g], NN)
            acc[g] += dot(key_t[h * HEAD_DIM : (h + 1) * HEAD_DIM], d_scores, NN)
            d_key = key_term if d_key is None else d_key + key_term
            d_value = value_term if d_value is None else d_value + value_term
        big[i, p] = d_key.astype(BF16)
        big[i, PAIRS + p] = d_value.astype(BF16)
        return carry

    lax.fori_loop(0, steps, back, jnp.int32(0))

    for p in range(PAIRS):
        both = jnp.concatenate([acc[2 * p], acc[2 * p + 1]], axis=0)
        d_all[:, p * 128 : (p + 1) * 128] = (both.T * 0.125).astype(BF16)
    core_send(3).wait_recv()
    for number in (2, 3, 4, 5):
        hop(number).wait_recv()
    for piece in range(PAIRS):
        at = HALF + piece * 128
        total = big[7, piece].astype(F32) + cb[3, piece].astype(F32)
        total += rb[2, piece].astype(F32) + rb[5, piece].astype(F32)
        d_all[:, at : at + 128] = total.astype(BF16)
        at = 2 * HALF + piece * 128
        total = big[7, PAIRS + piece].astype(F32) + cb[3, PAIRS + piece].astype(F32)
        total += rb[3, piece].astype(F32) + rb[4, piece].astype(F32)
        d_all[:, at : at + 128] = total.astype(BF16)

    half = size // 2
    blk = wq_all.shape[1]

    def input_term(which):
        weight = wq_all[pl.ds(which * half, half)].reshape(HALF, QKV)
        return dot(d_all[...], weight, NT)

    near[0] = input_term(1 - r).astype(BF16)
    for which in range(2):
        term = dot(hid_all[which], d_all[...], TN).astype(BF16)
        gq[which * half : (which + 1) * half] = term.reshape(half, blk, QKV)
    to_near = send(near.at[0], near.at[1], single, 3, place.to_x())
    to_near.start()
    qz = (q_send, q_recv)

    def q_block(index, core):
        m, k = lax.div(index, n), lax.rem(index, n)
        return place.col_block(place.plane(k), lax.rem(y + 1 + m, 2), core)

    def q_core(index):
        return send(gq.at[q_block(index, 1 - j)], q1.at[index], qz, index, place.to_core())

    def q_side(k):
        return send(gq.at[q_block(k, j)], q2.at[k], qz, 2 * n + k, place.to_y())

    def q_plane(k):
        return send(gq.at[q_block(n + k, j)], q3.at[k - 1], qz, 3 * n + k - 1, place.to_z(k))

    loop(2 * n, lambda index: q_core(index).start())
    bias_own[0, 0:1] = jnp.sum(d_all[:, :HALF].astype(F32), axis=0, keepdims=True)
    bias_own[0, 1:2] = jnp.sum(d_all[:, 2 * HALF :].astype(F32), axis=0, keepdims=True)
    bias_own[0, 2:8] = jnp.zeros((6, HALF), F32)
    sz = (s_send, s_recv)

    def small(number):
        level = min(number, 2)
        peer = (place.to_core(), place.to_y(), place.to_z(max(number - 1, 1)))[level]
        return send(bias_own.at[level], bias_got.at[number], sz, number, peer)

    grad_out[...] = input_term(r)
    small(0).start()

    def q_core_add(index):
        q_core(index).wait_recv()
        fold(gq, q1[index], q_block(index, j))

    loop(n, q_core_add)
    small(0).wait_recv()
    bias_own[1] = bias_own[0] + bias_got[0]
    loop(n, lambda k: q_side(k).start())
    loop(n, lambda k: q_core_add(n + k))
    small(1).start()
    grad_out[own_rows, :] = grad_out[own_rows, :] + dres_own[...]
    send(dres_low.at[1 - r], dres_far, single, 2, place.to_x()).wait_recv()
    grad_out[other_rows, :] = grad_out[other_rows, :] + dres_far[...].astype(F32)
    small(1).wait_recv()
    bias_own[2] = bias_own[1] + bias_got[1]

    def q_side_add(k):
        q_side(k).wait_recv()
        fold(gq, q2[k], q_block(n + k, j))

    loop(n, q_side_add)
    loop(n - 1, lambda k: q_plane(k + 1).start())
    for step in range(1, n):
        small(1 + step).start()

    loop(n, g_x_add)
    loop(n, lambda k: g_y_send(k).start())
    loop(n, lambda k: g_x_add(n + k))
    loop(n, g_y_add)
    for k in range(1, n):
        g_z_send(k).start()
    to_near.wait_recv()
    grad_out[...] = grad_out[...] + near[1].astype(F32)
    total = bias_own[2]
    for step in range(1, n):
        small(1 + step).wait_recv()
        total = total + bias_got[1 + step]
    bias_out[...] = total
    total = gq[q_block(n, j)].astype(F32)
    for k in range(1, n):
        q_plane(k).wait_recv()
        total = total + q3[k - 1].astype(F32)
    qkv_out[...] = total
    total = st[3 * n].astype(F32)
    for k in range(1, n):
        g_z_send(k).wait_recv()
        total = total + b4[k - 1].astype(F32)
    rest_out[...] = total

    loop(4 * n, lambda index: c_move(index).wait_send())
    loop(2 * n, lambda index: g_x_send(index).wait_send())
    loop(n, lambda k: g_y_send(k).wait_send())
    for k in range(1, n):
        g_z_send(k).wait_send()
        q_plane(k).wait_send()
        small(1 + k).wait_send()
    small(0).wait_send()
    small(1).wait_send()
    loop(2 * n, lambda index: q_core(index).wait_send())
    loop(n, lambda k: q_side(k).wait_send())
    for pair in range(4):
        core_send(pair).wait_send()
    for number in range(6):
        hop(number).wait_send()
    to_near.wait_send()
    send(dctx.at[1 - r], d_ctx.at[own_rows], single, 0, place.to_x()).wait_send()
    to_lay = send(lay.at[1 - r], lay_out.at[other_rows], single, 1, place.to_x())
    to_lay.wait_recv()
    to_lay.wait_send()
    send(dres_low.at[1 - r], dres_far, single, 2, place.to_x()).wait_send()
    lay_local.wait()


def backward_attention(
    size, dctx, qs, m_in, lse_in, ctxt, hid_all, wq_all, lay, dres_low, dres_own, kv_in, p_in, g_in
):
    rows = qs.shape[1]
    part = rows // 2
    blk = wq_all.shape[1]
    n = size // 4
    any_space = pl.BlockSpec(memory_space=pl.ANY)
    vmem = pl.BlockSpec(memory_space=pltpu.VMEM)
    shape = jax.ShapeDtypeStruct
    dma = pltpu.SemaphoreType.DMA
    scratch = pltpu.VMEM
    g_count, q_count = 4 * n + 2 * n + n + n - 1, 2 * n + n + n - 1
    return pl.pallas_call(
        functools.partial(kernel_c, size),
        out_shape=(
            shape((blk, WIDE), F32),
            shape((blk, QKV), F32),
            shape((8, HALF), F32),
            shape((rows, HALF), F32),
            shape((rows, HALF), BF16),
        ),
        in_specs=[vmem] * 10 + [any_space] * 3,
        out_specs=[vmem] * 4 + [any_space],
        scratch_shapes=[
            scratch((rows, HALF), BF16),
            scratch((2 * PAIRS, 128, rows), F32),
            scratch((2 * PAIRS, 1, rows), F32),
            scratch((2 * PAIRS, rows, 128), BF16),
            scratch((2 * PAIRS, HEAD_DIM, rows), F32),
            scratch((SPAN, 2 * PAIRS, rows, 128), BF16),
            scratch((2, 2, rows, rows), BF16),
            scratch((SPAN, 2 * PAIRS, rows, 128), BF16),
            scratch((4, 2 * PAIRS, rows, 128), BF16),
            scratch((6, PAIRS, rows, 128), BF16),
            scratch((4 * n, blk, WIDE), BF16),
            scratch((4 * n, blk, WIDE), BF16),
            scratch((2 * n, blk, WIDE), BF16),
            scratch((n, blk, WIDE), BF16),
            scratch((n - 1, blk, WIDE), BF16),
            scratch((rows, QKV), BF16),
            scratch((size, blk, QKV), BF16),
            scratch((2 * n, blk, QKV), BF16),
            scratch((n, blk, QKV), BF16),
            scratch((n - 1, blk, QKV), BF16),
            scratch((2, rows, HALF), BF16),
            scratch((part, HALF), BF16),
            scratch((3, 8, HALF), F32),
            scratch((n + 1, 8, HALF), F32),
            dma((4,)),
            dma((4,)),
            dma((10,)),
            dma((10,)),
            dma((g_count,)),
            dma((g_count,)),
            dma((q_count,)),
            dma((q_count,)),
            dma((n + 1,)),
            dma((n + 1,)),
            dma((9 + 4 * n,)),
            dma((2,)),
        ],
        compiler_params=pltpu.CompilerParams(
            collective_id=1, has_side_effects=True, vmem_limit_bytes=63 * 2**20
        ),
        name="backward_attention",
    )(dctx, qs, m_in, lse_in, ctxt, hid_all, wq_all, lay, dres_low, dres_own, kv_in, p_in, g_in)


def gelu(argument):
    return 0.5 * argument * (1.0 + lax.erf(argument * 0.7071067811865476))


def gelu_slope(argument):
    bell = jnp.exp(argument * argument * -0.5) * 0.3989422804014327
    return 0.5 * (1.0 + lax.erf(argument * 0.7071067811865476)) + argument * bell


def norm_forward(resid, gain, shift):
    center = resid - jnp.mean(resid, axis=1, keepdims=True)
    scale = lax.rsqrt(jnp.mean(center * center, axis=1, keepdims=True) + EPSILON)
    normal = center * scale
    return normal * gain + shift, normal, scale


def norm_backward(incoming, normal, scale, gain):
    scaled = incoming * gain
    first = jnp.mean(scaled, axis=1, keepdims=True)
    second = jnp.mean(scaled * normal, axis=1, keepdims=True)
    result = scale * (scaled - first - normal * second)
    return result, jnp.sum(incoming * normal, axis=0), jnp.sum(incoming, axis=0)


def middle(size, keep, ctx, hidden, cotangent, wr_all):
    tall = wr_all.reshape(2, D, WIDE)
    w_out = [tall[h, :, :HALF] for h in range(2)]
    w_in = [tall[h, :, HALF : HALF + FF_HALF] for h in range(2)]
    w_outer = [tall[h, :, HALF + FF_HALF : REST] for h in range(2)]
    per = D // (2 * size)
    vectors = tall[:, :, REST : REST + 5].reshape(2 * size, 10 * per).astype(F32)
    b_output, b_outer, gain_one, shift_one, gain_two, shift_two = [
        vectors[:, at * per : (at + 1) * per].reshape(1, D) for at in range(6)
    ]
    b_inner = vectors[:, 6 * per :].reshape(2, 2 * D)

    attn = dot(ctx[0], w_out[0], NT) + dot(ctx[1], w_out[1], NT) + b_output
    normed, normal_one, scale_one = norm_forward(hidden.astype(F32) + attn, gain_one, shift_one)
    normed_low = normed.astype(BF16)
    inner = [dot(normed_low, w_in[h], NN) + b_inner[h] for h in range(2)]
    act = [gelu(inner[h]).astype(BF16) for h in range(2)]
    outer = dot(act[0], w_outer[0], NT) + dot(act[1], w_outer[1], NT) + b_outer
    result, normal_two, scale_two = norm_forward(normed + outer, gain_two, shift_two)
    seed = cotangent.astype(F32) * keep
    d_res_two, g_gain_two, g_shift_two = norm_backward(seed, normal_two, scale_two, gain_two)
    d_outer = d_res_two.astype(BF16)
    d_inner = [
        (dot(d_outer, w_outer[h], NN) * gelu_slope(inner[h])).astype(BF16) for h in range(2)
    ]
    d_normed = d_res_two + dot(d_inner[0], w_in[0], NT) + dot(d_inner[1], w_in[1], NT)
    d_res_one, g_gain_one, g_shift_one = norm_backward(d_normed, normal_one, scale_one, gain_one)
    d_attn = d_res_one.astype(BF16)
    d_context = [(dot(d_attn, w_out[h], NN) * keep).astype(BF16) for h in range(2)]

    sums = [
        jnp.sum(d_attn.astype(F32), axis=0),
        jnp.sum(d_outer.astype(F32), axis=0),
        g_gain_one,
        g_shift_one,
        g_gain_two,
        g_shift_two,
    ]
    g_b_inner = jnp.stack([jnp.sum(d_inner[h].astype(F32), axis=0) for h in range(2)])
    small = jnp.concatenate(
        [v.reshape(2 * size, per) for v in sums] + [g_b_inner.reshape(2 * size, 4 * per)], axis=1
    )
    small = jnp.pad(small.reshape(2, D, 5), ((0, 0), (0, 0), (0, 123))).astype(BF16)
    parts = []
    for h in range(2):
        parts += [
            jnp.concatenate(
                [
                    dot(d_attn, ctx[h], TN).astype(BF16),
                    dot(normed_low, d_inner[h], TN).astype(BF16),
                    dot(d_outer, act[h], TN).astype(BF16),
                    small[h],
                ],
                axis=1,
            )
        ]
    g_parts = jnp.stack(parts).reshape(wr_all.shape)
    return result.astype(BF16), d_res_one, d_attn, jnp.stack(d_context), g_parts


def halves(array):
    return jnp.stack([array[:, :HALF], array[:, HALF:]])


def per_device(
    group,
    hidden_in,
    cotangent,
    lengths,
    w_query,
    w_key,
    w_value,
    w_output,
    w_inner,
    w_outer,
    b_query,
    b_value,
    b_output,
    b_inner,
    b_outer,
    gain_one,
    shift_one,
    gain_two,
    shift_two,
):
    cols = lax.axis_size("col")
    size = group
    ways = cols // size
    col = lax.axis_index("col")
    row = lax.axis_index("row")
    inside = col % size
    rows = hidden_in.shape[0]
    part = rows // 2

    def regroup(block):
        if ways == 1:
            return block
        whole = lax.all_gather(block, "col", axis=0, tiled=True)
        count = block.shape[0] * ways
        return lax.dynamic_slice_in_dim(whole, inside * count, count, axis=0)

    wq_block = regroup(jnp.concatenate([w_query, w_key, w_value], axis=1))
    bq, bv = regroup(b_query), regroup(b_value)
    vectors = [
        regroup(v) for v in (b_output, b_outer, gain_one, shift_one, gain_two, shift_two, b_inner)
    ]
    blk = wq_block.shape[0]
    per = blk // 2
    column = jnp.concatenate(vectors).reshape(blk, 5)
    wr_block = jnp.concatenate(
        [
            regroup(w_output.T),
            regroup(w_inner),
            regroup(w_outer.T),
            jnp.pad(column, ((0, 0), (0, 123))),
        ],
        axis=1,
    )
    placed = jnp.stack([bq, bv]).reshape(2, 1, per)
    slots = lax.broadcasted_iota(jnp.int32, (1, size, 1), 1)
    placed = jnp.where(slots == inside, placed, jnp.zeros((), BF16)).reshape(2, HALF)
    placed = jnp.pad(placed, ((0, 14), (0, 0)))

    (hid_all, wq_all, qs, kv, probs, m_all, lse, ctxt, ctx_dp, cot_dp, wr_all) = forward_attention(
        size, lengths, hidden_in, wq_block, placed, wr_block, cotangent
    )

    spot = (col % SPAN) * rows + row * part + lax.broadcasted_iota(jnp.int32, (part, 1), 0)
    keep = (spot < lengths[col // SPAN]).astype(F32)
    hid_dp = lax.dynamic_slice_in_dim(hid_all, row * part, part, axis=1)
    hid_dp = jnp.concatenate([hid_dp[0], hid_dp[1]], axis=1)
    cot_own = jnp.concatenate([cot_dp[0], cot_dp[1]], axis=1)
    result, d_res_one, d_attn, d_context, g_parts = middle(
        size, keep, ctx_dp, hid_dp, cot_own, wr_all
    )
    d_res_own = lax.dynamic_slice_in_dim(d_res_one, row * HALF, HALF, axis=1)
    g_rest, g_qkv, g_bias, grad_in, layer_out = backward_attention(
        size,
        d_context,
        qs,
        m_all,
        lse,
        ctxt,
        hid_all,
        wq_all,
        halves(result),
        halves(d_attn),
        d_res_own,
        kv,
        probs,
        g_parts,
    )

    def spread(block):
        if ways == 1:
            return block
        count = block.shape[0]
        whole = jnp.zeros((count * size,) + block.shape[1:], block.dtype)
        whole = lax.dynamic_update_slice_in_dim(whole, block, inside * count, axis=0)
        return lax.psum_scatter(whole, "col", scatter_dimension=0, tiled=True)

    flat = g_rest[:, REST : REST + 5].reshape(10 * per)
    pieces = [spread(flat[at * per : (at + 1) * per]) for at in range(6)]
    g_b_output, g_b_outer, g_gain_one, g_shift_one, g_gain_two, g_shift_two = pieces
    g_b_inner = spread(flat[6 * per :])
    g_b_query = spread(lax.dynamic_slice_in_dim(g_bias[0], inside * per, per))
    g_b_value = spread(lax.dynamic_slice_in_dim(g_bias[1], inside * per, per))
    return (
        layer_out,
        grad_in,
        spread(g_qkv[:, :HALF]),
        spread(g_qkv[:, HALF : 2 * HALF]),
        spread(g_qkv[:, 2 * HALF :]),
        spread(g_rest[:, :HALF]).T,
        spread(g_rest[:, HALF : HALF + FF_HALF]),
        spread(g_rest[:, HALF + FF_HALF : REST]).T,
        g_b_query,
        g_b_value,
        g_b_output,
        g_b_inner,
        g_b_outer,
        g_gain_one,
        g_shift_one,
        g_gain_two,
        g_shift_two,
    )


def solution(mesh):
    cols = mesh.shape["col"]
    group = max(s for s in range(SPAN, cols + 1, 4) if cols % s == 0 and D // s % 16 == 0)
    token, weight, turned = P("col", "row"), P("col", "row"), P("row", "col")
    vector = P(("row", "col"))
    return jax.shard_map(
        functools.partial(per_device, group),
        mesh=mesh,
        in_specs=(token, token, P()) + (weight,) * 3 + (turned, weight, turned) + (vector,) * 9,
        out_specs=(token, token) + (weight,) * 3 + (turned, weight, turned) + (vector,) * 9,
        check_vma=False,
    )
```

```python
import functools

import jax
import jax.numpy as jnp
from jax import lax
from jax.experimental import pallas as pl
from jax.experimental.pallas import tpu as pltpu
from jax.sharding import PartitionSpec as P

D = 768
HALF = 384
HEAD_DIM = 64
FF_HALF = 1536
PAIRS = 3
SPAN = 8
EPSILON = 1e-12
MASKED = -1e30
MESH = pl.DeviceIdType.MESH
F32 = jnp.float32
BF16 = jnp.bfloat16
FIRST = HALF + FF_HALF
REST = HALF + 2 * FF_HALF
QKV = 3 * HALF


def dot(left, right, contract):
    return lax.dot_general(left, right, (contract, ((), ())), preferred_element_type=F32)


NN = ((1,), (0,))
NT = ((1,), (1,))
TN = ((0,), (0,))


class Place:
    def __init__(self, size):
        self.size = size
        self.planes = size // 4
        self.r = lax.axis_index("row")
        col = lax.axis_index("col")
        self.base = lax.div(col, size) * size
        inner = lax.rem(col, size)
        self.slot = lax.div(col, SPAN)
        self.block = lax.rem(col, SPAN)
        self.z = lax.div(inner, 4)
        self.y = lax.rem(lax.div(inner, 2), 2)
        self.j = lax.rem(inner, 2)
        self.zl = lax.rem(self.z, 2)

    def plane(self, step):
        return lax.rem(self.z + step + self.planes, self.planes)

    def device(self, r, z, y, j):
        return (r, self.base + z * 4 + y * 2 + j)

    def to_z(self, step):
        return self.device(self.r, self.plane(step), self.y, self.j)

    def to_z_near(self):
        return self.device(self.r, self.z - self.zl + (1 - self.zl), self.y, self.j)

    def to_y(self):
        return self.device(self.r, self.z, 1 - self.y, self.j)

    def to_x(self):
        return self.device(1 - self.r, self.z, self.y, self.j)

    def to_core(self):
        return self.device(self.r, self.z, self.y, 1 - self.j)

    def col_block(self, z, y, j):
        return z * 4 + y * 2 + j

    def any_block(self, r, z, y, j):
        return r * self.size + z * 4 + y * 2 + j

    def near_block(self, dz, dy, j):
        return lax.rem(self.zl + dz, 2) * 4 + lax.rem(self.y + dy, 2) * 2 + j


def meet(place):
    barrier = pltpu.get_barrier_semaphore()
    peers = [place.to_z(step) for step in range(1, place.planes)]
    peers += [place.to_y(), place.to_x(), place.to_core()]
    for peer in peers:
        pl.semaphore_signal(barrier, inc=1, device_id=peer, device_id_type=MESH)
    pl.semaphore_wait(barrier, len(peers))


def send(src, dst, sems, index, peer):
    return pltpu.make_async_remote_copy(
        src_ref=src,
        dst_ref=dst,
        send_sem=sems[0].at[index],
        recv_sem=sems[1].at[index],
        device_id=peer,
        device_id_type=MESH,
    )


class Gather:
    def __init__(self, place, own, full, sems, with_rows):
        self.place, self.own, self.full, self.sems = place, own, full, sems
        self.rows = 2 if with_rows else 1
        self.with_rows = with_rows
        n = place.planes
        self.at_y = n - 1
        self.at_x = self.at_y + n
        self.at_c = self.at_x + (2 * n if with_rows else 0)
        self.total = self.at_c + 2 * n * self.rows

    def index(self, n, k, m, j):
        p = self.place
        z, y = p.plane(-k), lax.rem(p.y + m, 2)
        if self.with_rows:
            return p.any_block(lax.rem(p.r + n, 2), z, y, j)
        return p.col_block(z, y, j)

    def move(self, number, peer, n, k, m, j, local):
        where = self.index(n, k, m, j)
        src = self.own if local else self.full.at[where]
        return send(src, self.full.at[where], self.sems, number, peer)

    def z_sends(self):
        p = self.place
        for step in range(1, p.planes):
            self.move(step - 1, p.to_z(step), 0, 0, 0, p.j, True).start()

    def z_done(self, k):
        p = self.place
        self.move(k - 1, p.to_z(k), 0, k, 0, p.j, False).wait_recv()

    def y_send(self, k):
        p = self.place
        self.move(self.at_y + k, p.to_y(), 0, k, 0, p.j, k == 0).start()

    def y_done(self, k):
        p = self.place
        self.move(self.at_y + k, p.to_y(), 0, k, 1, p.j, False).wait_recv()

    def x_send(self, k, m):
        p = self.place
        self.move(self.at_x + 2 * k + m, p.to_x(), 0, k, m, p.j, k + m == 0).start()

    def x_done(self, k, m):
        p = self.place
        self.move(self.at_x + 2 * k + m, p.to_x(), 1, k, m, p.j, False).wait_recv()

    def c_number(self, n, k, m):
        return self.at_c + (2 * k + m) * self.rows + n

    def c_send(self, n, k, m):
        p = self.place
        number = self.c_number(n, k, m)
        self.move(number, p.to_core(), n, k, m, p.j, n + k + m == 0).start()

    def c_done(self, n, k, m):
        p = self.place
        self.move(self.c_number(n, k, m), p.to_core(), n, k, m, 1 - p.j, False).wait_recv()

    def all_sent(self):
        for number in range(self.total):
            send(self.own, self.own, self.sems, number, self.place.to_core()).wait_send()


def spread_rows(tiles, picks, per, width):
    blocks = tiles.shape[0]
    flat = tiles.reshape(blocks * 16, 128)
    total = len(picks) * blocks
    line = lax.broadcasted_iota(jnp.int32, (total, blocks * 16), 0)
    at = lax.broadcasted_iota(jnp.int32, (total, blocks * 16), 1)
    wanted = jnp.zeros((total, blocks * 16), F32)
    for spot, pick in enumerate(picks):
        hit = at == (line - spot * blocks) * 16 + pick
        inside = (line >= spot * blocks) & (line < (spot + 1) * blocks)
        wanted = jnp.where(hit & inside, 1.0, wanted)
    taken = dot(wanted.astype(BF16), flat, NN).astype(BF16)
    lane = lax.broadcasted_iota(jnp.int32, (128, width), 1).astype(F32)
    group = jnp.floor((lane + 0.5) * (1.0 / per))
    place = lax.broadcasted_iota(jnp.int32, (128, width), 0).astype(F32)
    copies = jnp.where(lane - group * per == place, 1.0, 0.0).astype(BF16)
    wide = dot(taken, copies, NN)
    first = lax.broadcasted_iota(jnp.int32, (blocks, width), 0) * per
    column = lax.broadcasted_iota(jnp.int32, (blocks, width), 1)
    mask = (column >= first) & (column < first + per)
    rows = []
    for spot in range(len(picks)):
        part = jnp.where(mask, wide[spot * blocks : (spot + 1) * blocks], 0.0)
        rows.append(jnp.sum(part, axis=0, keepdims=True))
    return rows


def gelu_both(argument):
    spread = 1.0 + lax.erf(argument * 0.7071067811865476)
    bell = jnp.exp(argument * argument * -0.5) * 0.3989422804014327
    return 0.5 * argument * spread, 0.5 * spread + argument * bell


def norm_forward(resid, gain, shift):
    center = resid - jnp.mean(resid, axis=1, keepdims=True)
    scale = lax.rsqrt(jnp.mean(center * center, axis=1, keepdims=True) + EPSILON)
    normal = center * scale
    return normal * gain + shift, normal, scale


def norm_backward(incoming, normal, scale, gain):
    scaled = incoming * gain
    first = jnp.mean(scaled, axis=1, keepdims=True)
    second = jnp.mean(scaled * normal, axis=1, keepdims=True)
    result = scale * (scaled - first - normal * second)
    sums = jnp.sum(incoming * normal, axis=0, keepdims=True)
    return result, sums, jnp.sum(incoming, axis=0, keepdims=True)


def kernel_a(
    size,
    lengths,
    hid,
    w_query,
    w_key,
    w_value,
    w_output,
    w_inner,
    w_outer,
    vec_in,
    cot,
    hid_out,
    wq_out,
    q_out,
    kv_out,
    p_out,
    m_out,
    lse_out,
    ctxt_out,
    g_out,
    final_out,
    low_out,
    own_out,
    d_out,
    small_out,
    hid_all,
    wq_own,
    wq_all,
    vec_all,
    one_own,
    one_all,
    two_all,
    kv,
    qs,
    qm,
    acc,
    high,
    low,
    pbuf,
    ctx_tp,
    ctx_in,
    cot_in,
    lay_out,
    lay_far,
    normed_ref,
    normal_ref,
    low_ref,
    slope_ref,
    act_ref,
    d_ref,
    one_send,
    one_recv,
    two_send,
    two_recv,
    wq_send,
    wq_recv,
    vec_send,
    vec_recv,
    kv_send,
    kv_recv,
    lone_send,
    lone_recv,
    local,
    p_sem,
):
    place = Place(size)
    rows = hid.shape[0]
    part = rows // 2
    n = place.planes
    r, y, j = place.r, place.y, place.j
    blk = w_query.shape[0]
    for at, source in enumerate((w_query, w_key, w_value)):
        wq_own[:, at * HALF : (at + 1) * HALF] = source[...]
    one_own[:, :HALF] = w_output[...]
    one_own[:, HALF:] = w_inner[...]
    with jax.named_scope("meet"):
        meet(place)

    single = (lone_send, lone_recv)
    own_rows = pl.ds(pl.multiple_of(r * part, part), part)
    other_rows = pl.ds(pl.multiple_of((1 - r) * part, part), part)
    to_hid = send(hid, hid_all.at[r], single, 0, place.to_x())
    to_hid.start()
    vec = Gather(place, vec_in, vec_all, (vec_send, vec_recv), True)
    wq = Gather(place, wq_own, wq_all, (wq_send, wq_recv), False)
    one = Gather(place, one_own, one_all, (one_send, one_recv), True)
    two = Gather(place, w_outer, two_all, (two_send, two_recv), True)
    for gather in (vec, wq):
        gather.z_sends()
        gather.y_send(0)
        gather.c_send(0, 0, 0)
    vec.x_send(0, 0)
    one.x_send(0, 0)
    one.y_send(0)
    two.x_send(0, 0)
    to_cot = send(cot.at[other_rows], cot_in.at[r], single, 1, place.to_x())
    to_cot.start()
    one.c_send(0, 0, 0)
    two.c_send(0, 0, 0)
    hid_all[r] = hid[...]
    mine = place.any_block(r, place.z, y, j)
    wq_all[place.col_block(place.z, y, j)] = wq_own[...]
    vec_all[mine] = vec_in[...]
    one_all[mine] = one_own[...]
    two_all[mine] = w_outer[...]
    cot_in[r] = cot[own_rows, :]
    for k in range(1, n):
        with jax.named_scope(f"qkv_plane_{k}"):
            for gather in (vec, wq):
                gather.z_done(k)
                gather.y_send(k)
                gather.c_send(0, k, 0)
            vec.x_send(k, 0)
    one.z_sends()
    two.y_send(0)
    for k in range(n):
        with jax.named_scope(f"qkv_side_{k}"):
            for gather in (vec, wq):
                gather.y_done(k)
                gather.c_send(0, k, 1)
            vec.x_send(k, 1)
    with jax.named_scope("qkv_core"):
        for k in range(n):
            for m in range(2):
                for gather in (vec, wq):
                    gather.c_done(0, k, m)
    with jax.named_scope("hidden"):
        send(hid, hid_all.at[1 - r], single, 0, place.to_x()).wait_recv()

    def rest_y(gather, k):
        gather.z_done(k)
        gather.y_send(k)
        gather.x_send(k, 0)
        gather.c_send(0, k, 0)

    def rest_x(gather, k):
        gather.y_done(k)
        gather.x_send(k, 1)
        gather.c_send(0, k, 1)

    def rest_c(gather, k, m):
        gather.x_done(k, m)
        gather.c_send(1, k, m)

    def rest_all(gather):
        for n_at in range(2):
            for k in range(n):
                for m in range(2):
                    if gather is not vec or n_at:
                        gather.c_done(n_at, k, m)

    hid_local = pltpu.make_async_copy(hid_all, hid_out, local.at[2])
    hid_local.start()
    wq_local = pltpu.make_async_copy(wq_all, wq_out, local.at[3])
    wq_local.start()

    own_tiles = vec_all[pl.ds(r * size, size)]
    b_query, b_value = spread_rows(own_tiles, (0, 1), HALF // size, HALF)
    own = place.near_block(0, 0, j)
    half = size // 2
    for which in (1, 2, 0):
        columns = slice(which * HALF, (which + 1) * HALF)
        total = dot(hid_all[0], wq_all[:half, :, columns].reshape(HALF, HALF), NN)
        total += dot(hid_all[1], wq_all[half:, :, columns].reshape(HALF, HALF), NN)
        if which == 0:
            total += b_query
        if which == 2:
            total += b_value
        total = total.astype(BF16)
        for p in range(PAIRS):
            piece = total[:, p * 128 : (p + 1) * 128]
            if which == 0:
                lane = lax.broadcasted_iota(jnp.int32, (rows, 128), 1)
                piece = piece * jnp.asarray(0.125, BF16)
                qs[p] = piece
                qm[2 * p] = jnp.where(lane < HEAD_DIM, piece, jnp.zeros_like(piece))
                qm[2 * p + 1] = jnp.where(lane >= HEAD_DIM, piece, jnp.zeros_like(piece))
            else:
                kv[own, (which - 1) * PAIRS + p] = piece
        if which == 1:
            with jax.named_scope("after_key"):
                rest_x(one, 0)
        if which == 2:
            with jax.named_scope("after_value"):
                rest_y(one, 1)
    acc[...] = jnp.zeros_like(acc)
    high[...] = jnp.full_like(high, MASKED)
    low[...] = jnp.zeros_like(low)

    n_one = place.device(r, place.z - place.zl + lax.rem(place.zl + 1 - j, 2), lax.rem(y + j, 2), j)
    n_two = place.device(r, place.z - place.zl + lax.rem(place.zl + j, 2), lax.rem(y + 1 - j, 2), j)
    kvs = (kv_send, kv_recv)

    def kv_block(i):
        pair, core = lax.div(i, 2), lax.rem(j + lax.rem(i, 2), 2)
        b0, b1 = lax.rem(pair, 2), lax.div(pair, 2)
        return place.near_block(b0 * (1 - core) + b1 * core, b0 * core + b1 * (1 - core), core)

    def kv_move(number, what, peer):
        where = kv_block(what)
        return send(kv.at[where], kv.at[where], kvs, number, peer)

    kv_move(1, 0, place.to_core()).start()
    kv_move(2, 0, n_one).start()
    q_local = pltpu.make_async_copy(qs, q_out, local.at[4])
    q_local.start()

    def arrived(number):
        kv_move(number, number, n_one).wait_recv()

    def second():
        kv_move(4, 0, n_two).start()

    def first_here():
        arrived(2)
        kv_move(3, 2, place.to_core()).start()

    def third():
        kv_move(6, 2, n_two).start()

    def second_here():
        arrived(4)
        kv_move(5, 4, place.to_core()).start()

    def third_here():
        arrived(6)
        kv_move(7, 6, place.to_core()).start()

    def vec_rows():
        for k in range(n):
            for m in range(2):
                rest_c(vec, k, m)

    def two_start():
        two.z_sends()

    events = {}

    def add(step, what, *inputs):
        events.setdefault(step, []).append(functools.partial(what, *inputs))

    add(1, vec_rows)
    add(2, rest_x, one, 1)
    add(2, two_start)
    add(3, arrived, 1)
    add(4, rest_y, one, 2)
    add(5, rest_y, one, 3)
    add(5, second)
    add(6, rest_x, two, 0)
    add(6, first_here)
    add(7, rest_x, one, 2)
    add(8, rest_x, one, 3)
    add(8, rest_c, one, 0, 0)
    add(8, third)
    add(9, rest_c, one, 1, 0)
    add(9, arrived, 3)
    add(10, rest_y, two, 1)
    add(12, second_here)
    add(13, rest_c, one, 0, 1)
    add(13, rest_c, one, 1, 1)
    add(13, rest_y, two, 2)
    add(14, rest_x, two, 1)
    add(15, arrived, 5)
    add(15, rest_y, two, 3)
    add(16, rest_c, one, 2, 0)
    add(17, rest_c, one, 3, 0)
    add(17, rest_x, two, 2)
    add(18, third_here)
    add(19, rest_c, one, 2, 1)
    add(20, rest_x, two, 3)
    add(21, arrived, 7)
    add(21, rest_c, one, 3, 1)
    add(22, rest_c, two, 0, 0)
    add(23, rest_c, two, 0, 1)

    length = lengths[place.slot]

    def p_copy(t, slot):
        i, p = lax.div(t, PAIRS), lax.rem(t, PAIRS)
        return pltpu.make_async_copy(
            pbuf.at[slot], p_out.at[kv_block(i), pl.ds(2 * p, 2)], p_sem.at[slot]
        )

    def kv_copy(i):
        where = kv_block(i)
        return pltpu.make_async_copy(kv.at[where], kv_out.at[where], local.at[8 + i])

    steps = SPAN * PAIRS

    def attend(t, carry):
        i, p = lax.div(t, PAIRS), lax.rem(t, PAIRS)
        for step, calls in sorted(events.items()):

            @pl.when(t == step)
            def _(calls=calls):
                for call in calls:
                    with jax.named_scope(f"at_{step}"):
                        call()

        @pl.when(p == 0)
        def _():
            kv_copy(i).start()

        slot = lax.rem(t, 2)

        @pl.when(t >= 2)
        def _():
            p_copy(t - 2, slot).wait()

        where = kv_block(i)
        place_of = lax.broadcasted_iota(jnp.int32, (rows, 128), 0) + where * rows
        bias = jnp.where(place_of < length, 0.0, MASKED)
        bias = jnp.concatenate([bias] * (rows // 128), axis=1)
        key = kv[where, p]
        value_t = kv[where, PAIRS + p].T
        for h in range(2):
            g = 2 * p + h
            scores = dot(key, qm[g], NT) + bias
            top = jnp.max(scores, axis=0, keepdims=True)
            weights = jnp.exp(scores - top)
            below = jnp.sum(weights, axis=0, keepdims=True)
            rounded = weights.astype(BF16)
            pbuf[slot, h] = rounded
            term = dot(value_t[h * HEAD_DIM : (h + 1) * HEAD_DIM], rounded, NN)
            old = high[g]
            new = jnp.maximum(old, top)
            keep_old, keep_new = jnp.exp(old - new), jnp.exp(top - new)
            high[g] = new
            low[g] = low[g] * keep_old + below * keep_new
            acc[g] = acc[g] * keep_old + term * keep_new
            m_out[where, g] = top
        p_copy(t, slot).start()
        return carry

    lax.fori_loop(0, steps, attend, jnp.int32(0))

    column = lax.broadcasted_iota(jnp.int32, (1, rows), 1) + place.block * rows
    keep = jnp.where(column < length, 1.0, 0.0)
    for p in range(PAIRS):
        parts = []
        for h in range(2):
            g = 2 * p + h
            lse_out[g] = high[g] + jnp.log(low[g])
            parts.append(acc[g] / low[g])
        both = jnp.concatenate(parts, axis=0)
        ctxt_out[p] = both
        ctx_tp[:, p * 128 : (p + 1) * 128] = (both * keep).T.astype(BF16)
    for t in (steps - 2, steps - 1):
        p_copy(jnp.int32(t), t % 2).wait()
    to_ctx = send(ctx_tp.at[other_rows], ctx_in.at[r], single, 2, place.to_x())
    to_ctx.start()
    ctx_in[r] = ctx_tp[own_rows, :]
    with jax.named_scope("one_all"):
        rest_all(vec)
        rest_all(one)
    six = spread_rows(vec_all[...], (2, 3, 4, 5, 6, 7), HALF // size, D)
    b_output, b_outer, gain_one, shift_one, gain_two, shift_two = six
    (b_inner,) = spread_rows(vec_all[...], (8,), FF_HALF // size, 2 * FF_HALF)
    hidden = jnp.concatenate([hid_all[0, own_rows, :], hid_all[1, own_rows, :]], axis=1)
    with jax.named_scope("context"):
        send(ctx_tp.at[other_rows], ctx_in.at[1 - r], single, 2, place.to_x()).wait_recv()

    def weight(ref, h, columns):
        block = ref[h * size : (h + 1) * size, :, columns]
        return block.reshape(D, block.shape[2])

    out_cols, in_cols, all_cols = slice(0, HALF), slice(HALF, FIRST), slice(0, FF_HALF)
    with jax.named_scope("middle_one"):
        attn = dot(ctx_in[0], weight(one_all, 0, out_cols), NT)
        attn += dot(ctx_in[1], weight(one_all, 1, out_cols), NT) + b_output
        normed, normal, scale_one = norm_forward(hidden.astype(F32) + attn, gain_one, shift_one)
        normed_ref[...] = normed
        normal_ref[...] = normal
        low_ref[...] = normed.astype(BF16)
    with jax.named_scope("two_late"):
        rest_c(two, 1, 0)
        rest_c(two, 1, 1)
    for h in range(2):
        with jax.named_scope(f"inner_{h}"):
            span = slice(h * FF_HALF, (h + 1) * FF_HALF)
            inner = dot(low_ref[...], weight(one_all, h, in_cols), NN) + b_inner[:, span]
            value, slope = gelu_both(inner)
            act_ref[:, span] = value.astype(BF16)
            slope_ref[:, span] = slope
    with jax.named_scope("two_all"):
        for k in range(2, n):
            for m in range(2):
                rest_c(two, k, m)
        rest_all(two)
    with jax.named_scope("outer"):
        outer = dot(act_ref[:, :FF_HALF], weight(two_all, 0, all_cols), NT)
        outer += dot(act_ref[:, FF_HALF:], weight(two_all, 1, all_cols), NT) + b_outer
        result, normal_two, scale_two = norm_forward(normed_ref[...] + outer, gain_two, shift_two)
        lay_out[0] = result[:, :HALF].astype(BF16)
        lay_out[1] = result[:, HALF:].astype(BF16)
    to_lay = send(lay_out.at[1 - r], lay_far.at[r], single, 3, place.to_x())
    to_lay.start()
    spot = lax.broadcasted_iota(jnp.int32, (part, 1), 0) + place.block * rows + r * part
    keep = jnp.where(spot < length, 1.0, 0.0)
    with jax.named_scope("cotangent"):
        send(cot.at[other_rows], cot_in.at[1 - r], single, 1, place.to_x()).wait_recv()
    with jax.named_scope("norm_two"):
        seed = jnp.concatenate([cot_in[0], cot_in[1]], axis=1).astype(F32) * keep
        d_two, g_gain_two, g_shift_two = norm_backward(seed, normal_two, scale_two, gain_two)
        d_outer = d_two.astype(BF16)
        small_out[4:5] = g_gain_two
        small_out[5:6] = g_shift_two
        small_out[1:2] = jnp.sum(d_outer.astype(F32), axis=0, keepdims=True)
    d_normed = d_two
    d_outer_t = d_outer.T
    for h in range(2):
        with jax.named_scope(f"d_inner_{h}"):
            span = slice(h * FF_HALF, (h + 1) * FF_HALF)
            d_inner = dot(d_outer, weight(two_all, h, all_cols), NN) * slope_ref[:, span]
            d_inner = d_inner.astype(BF16)
            d_ref[:, span] = d_inner
            sums = jnp.sum(d_inner.astype(F32), axis=0, keepdims=True)
            small_out[6 + 2 * h : 7 + 2 * h] = sums[:, :D]
            small_out[7 + 2 * h : 8 + 2 * h] = sums[:, D:]
            d_normed += dot(d_inner, weight(one_all, h, in_cols), NT)
    with jax.named_scope("all_sent"):
        for gather in (vec, wq, one, two):
            gather.all_sent()
    own_col = pl.ds(pl.multiple_of(r * HALF, HALF), HALF)

    def give(number, ref, h, columns, target):
        return pltpu.make_async_copy(
            ref.at[pl.ds(h * size, size), :, columns],
            g_out.at[pl.ds(h * size, size), :, target],
            local.at[16 + number],
        )

    gives = []
    for h in range(2):
        with jax.named_scope(f"g_outer_{h}"):
            span = slice(h * FF_HALF, (h + 1) * FF_HALF)
            term = dot(d_outer_t, act_ref[:, span], NN).astype(BF16)
            two_all[h * size : (h + 1) * size] = term.reshape(size, blk, FF_HALF)
            copy = give(h, two_all, h, pl.ds(0, FF_HALF), pl.ds(FIRST, FF_HALF))
            copy.start()
            gives.append(copy)
    with jax.named_scope("norm_one"):
        d_one, g_gain_one, g_shift_one = norm_backward(d_normed, normal_ref[...], scale_one, gain_one)
        d_attn = d_one.astype(BF16)
        small_out[2:3] = g_gain_one
        small_out[3:4] = g_shift_one
        small_out[0:1] = jnp.sum(d_attn.astype(F32), axis=0, keepdims=True)
        small_out[10:16] = jnp.zeros((6, D), F32)
        for h in range(2):
            low_out[h] = d_attn[:, h * HALF : (h + 1) * HALF]
        normed_ref[...] = d_one
        own_out[...] = normed_ref[:, own_col]
    with jax.named_scope("d_context"):
        for h in range(2):
            d_context = dot(d_attn, weight(one_all, h, out_cols), NN) * keep
            d_out[h] = d_context.astype(BF16)
    low_t = low_ref[...].T
    d_attn_t = d_attn.T
    for h in range(2):
        with jax.named_scope(f"g_inner_{h}"):
            span = slice(h * FF_HALF, (h + 1) * FF_HALF)
            term = dot(low_t, d_ref[:, span], NN).astype(BF16)
            one_all[h * size : (h + 1) * size, :, HALF:] = term.reshape(size, blk, FF_HALF)
            term = dot(d_attn_t, ctx_in[h], NN).astype(BF16)
            one_all[h * size : (h + 1) * size, :, :HALF] = term.reshape(size, blk, HALF)
            copy = give(2 + h, one_all, h, pl.ds(0, FIRST), pl.ds(0, FIRST))
            copy.start()
            gives.append(copy)
    for number in range(1, 8):
        kv_move(number, 0, n_one).wait_send()
    to_lay.wait_send()
    send(lay_far.at[r], lay_far.at[1 - r], single, 3, place.to_x()).wait_recv()
    final_out[own_rows, :] = lay_out[r]
    final_out[other_rows, :] = lay_far[1 - r]
    for number in range(3):
        block = hid if number == 0 else ctx_in.at[0]
        send(block, block, single, number, place.to_x()).wait_send()
    for copy in [hid_local, wq_local, q_local] + gives:
        copy.wait()
    for i in range(SPAN):
        kv_copy(jnp.int32(i)).wait()


def forward_attention(size, lengths, hid, qkv_weights, rest_weights, vec, cot):
    rows = hid.shape[0]
    part = rows // 2
    blk = qkv_weights[0].shape[0]
    n = size // 4
    any_space = pl.BlockSpec(memory_space=pl.ANY)
    vmem = pl.BlockSpec(memory_space=pltpu.VMEM)
    shape = jax.ShapeDtypeStruct
    n_col, n_all = (n - 1) + n + 2 * n, (n - 1) + n + 2 * n + 4 * n
    dma = pltpu.SemaphoreType.DMA
    scratch = pltpu.VMEM
    return pl.pallas_call(
        functools.partial(kernel_a, size),
        out_shape=(
            shape((2, rows, HALF), BF16),
            shape((size, blk, QKV), BF16),
            shape((PAIRS, rows, 128), BF16),
            shape((SPAN, 2 * PAIRS, rows, 128), BF16),
            shape((SPAN, 2 * PAIRS, rows, rows), BF16),
            shape((SPAN, 2 * PAIRS, 1, rows), F32),
            shape((2 * PAIRS, 1, rows), F32),
            shape((PAIRS, 128, rows), F32),
            shape((2 * size, blk, REST), BF16),
            shape((rows, HALF), BF16),
            shape((2, part, HALF), BF16),
            shape((part, HALF), F32),
            shape((2, part, HALF), BF16),
            shape((16, D), F32),
        ),
        in_specs=[pl.BlockSpec(memory_space=pltpu.SMEM)] + [vmem] * 9,
        out_specs=[any_space] * 5 + [vmem] * 3 + [any_space] + [vmem] * 5,
        scratch_shapes=[
            scratch((2, rows, HALF), BF16),
            scratch((blk, QKV), BF16),
            scratch((size, blk, QKV), BF16),
            scratch((2 * size, 16, 128), BF16),
            scratch((blk, FIRST), BF16),
            scratch((2 * size, blk, FIRST), BF16),
            scratch((2 * size, blk, FF_HALF), BF16),
            scratch((SPAN, 2 * PAIRS, rows, 128), BF16),
            scratch((PAIRS, rows, 128), BF16),
            scratch((2 * PAIRS, rows, 128), BF16),
            scratch((2 * PAIRS, HEAD_DIM, rows), F32),
            scratch((2 * PAIRS, 1, rows), F32),
            scratch((2 * PAIRS, 1, rows), F32),
            scratch((2, 2, rows, rows), BF16),
            scratch((rows, HALF), BF16),
            scratch((2, part, HALF), BF16),
            scratch((2, part, HALF), BF16),
            scratch((2, part, HALF), BF16),
            scratch((2, part, HALF), BF16),
            scratch((part, D), F32),
            scratch((part, D), F32),
            scratch((part, D), BF16),
            scratch((part, 2 * FF_HALF), F32),
            scratch((part, 2 * FF_HALF), BF16),
            scratch((part, 2 * FF_HALF), BF16),
            dma((n_all,)),
            dma((n_all,)),
            dma((n_all,)),
            dma((n_all,)),
            dma((n_col,)),
            dma((n_col,)),
            dma((n_all,)),
            dma((n_all,)),
            dma((8,)),
            dma((8,)),
            dma((4,)),
            dma((4,)),
            dma((20,)),
            dma((2,)),
        ],
        compiler_params=pltpu.CompilerParams(
            collective_id=0, has_side_effects=True, vmem_limit_bytes=62 * 2**20
        ),
        name="forward_attention",
    )(lengths, hid, *qkv_weights, *rest_weights, vec, cot)


def kernel_c(
    size,
    dctx,
    qs,
    m_in,
    lse_in,
    ctxt,
    hid_all,
    wq_all,
    dres_low,
    dres_own,
    small_in,
    kv_in,
    p_in,
    g_in,
    query_out,
    key_out,
    value_out,
    wo_out,
    wi_out,
    wu_out,
    small_out,
    bias_out,
    grad_out,
    d_ctx,
    dtot,
    delta,
    qm,
    acc,
    kv,
    pbuf,
    big,
    cb,
    rb,
    st,
    b1,
    b2,
    b3,
    b4,
    d_all,
    gq,
    q1,
    q2,
    q3,
    near,
    bias_own,
    bias_got,
    vec_sum,
    vec_got,
    one_send,
    one_recv,
    kv_send,
    kv_recv,
    g_send,
    g_recv,
    q_send,
    q_recv,
    s_send,
    s_recv,
    v_send,
    v_recv,
    load,
    p_sem,
):
    place = Place(size)
    rows = qs.shape[1]
    part = rows // 2
    n = place.planes
    r, y, j = place.r, place.y, place.j
    with jax.named_scope("meet"):
        meet(place)
    single = (one_send, one_recv)
    gs = (g_send, g_recv)
    ks = (kv_send, kv_recv)
    at_x, at_y, at_z = 4 * n, 6 * n, 7 * n

    own_rows = pl.ds(pl.multiple_of(r * part, part), part)
    other_rows = pl.ds(pl.multiple_of((1 - r) * part, part), part)
    send(dctx.at[1 - r], d_ctx.at[own_rows], single, 0, place.to_x()).start()
    send(small_in, vec_got.at[0], (v_send, v_recv), 0, place.to_x()).start()

    def g_block(index, core):
        n_at, m = lax.div(index, 2 * n), lax.rem(index, 2)
        k = lax.rem(lax.div(lax.rem(index, 2 * n), 2) + 1, n)
        return place.any_block(
            lax.rem(r + 1 + n_at, 2), place.plane(k), lax.rem(y + 1 + m, 2), core
        )

    def c_move(index):
        return send(g_in.at[g_block(index, 1 - j)], b1.at[index], gs, index, place.to_core())

    def g_load(index):
        return pltpu.make_async_copy(g_in.at[g_block(index, j)], st.at[index], load.at[8 + index])

    def loop(count, body):
        def step(index, carry):
            body(index)
            return carry

        lax.fori_loop(0, count, step, jnp.int32(0))

    loop(4 * n, lambda index: c_move(index).start())
    loop(4 * n, lambda index: g_load(index).start())

    def b_block(i):
        pair, core = lax.div(i, 2), lax.rem(j + 1 + lax.rem(i, 2), 2)
        return place.near_block(1 - lax.div(pair, 2), 1 - lax.rem(pair, 2), core)

    def kv_load(i):
        return pltpu.make_async_copy(kv_in.at[b_block(i)], kv.at[i], load.at[i])

    def p_load(t, slot):
        i, p = lax.div(t, PAIRS), lax.rem(t, PAIRS)
        return pltpu.make_async_copy(
            p_in.at[b_block(i), pl.ds(2 * p, 2)], pbuf.at[slot], p_sem.at[slot]
        )

    p_load(jnp.int32(0), 0).start()
    loop(SPAN, lambda i: kv_load(i).start())

    lane = lax.broadcasted_iota(jnp.int32, (rows, 128), 1)
    for p in range(PAIRS):
        piece = qs[p]
        qm[2 * p] = jnp.where(lane < HEAD_DIM, piece, jnp.zeros_like(piece))
        qm[2 * p + 1] = jnp.where(lane >= HEAD_DIM, piece, jnp.zeros_like(piece))
    acc[...] = jnp.zeros_like(acc)
    d_ctx[own_rows, :] = dctx[r]
    def core_send(pair):
        return send(big.at[2 * pair], cb.at[pair], ks, pair, place.to_core())

    def core_add(pair):
        core_send(pair).wait_recv()
        for piece in range(2 * PAIRS):
            total = big[2 * pair + 1, piece].astype(F32) + cb[pair, piece].astype(F32)
            big[2 * pair + 1, piece] = total.astype(BF16)

    keys, values = pl.ds(0, PAIRS), pl.ds(PAIRS, PAIRS)

    def hop(number):
        pair, part_of, along_z = (
            (0, keys, False),
            (0, values, True),
            (1, keys, True),
            (1, values, True),
            (2, values, False),
            (2, keys, False),
        )[number]
        peer = place.to_z_near() if along_z else place.to_y()
        return send(big.at[2 * pair + 1, part_of], rb.at[number], ks, 4 + number, peer)

    def hop_add(number, pair, start):
        hop(number).wait_recv()
        for piece in range(PAIRS):
            total = big[2 * pair + 1, start + piece].astype(F32) + rb[number, piece].astype(F32)
            big[2 * pair + 1, start + piece] = total.astype(BF16)

    def fold(target, source, at):
        total = target[at].astype(F32) + source.astype(F32)
        target[at] = total.astype(BF16)

    def g_core_add(index):
        c_move(index).wait_recv()
        g_load(index).wait()
        fold(st, b1[index], index)

    def g_x_send(index):
        return send(st.at[index], b2.at[index], gs, at_x + index, place.to_x())

    def g_x_add(index):
        g_x_send(index).wait_recv()
        fold(st, b2[index], 2 * n + index)

    def kept(m, k):
        return 2 * n + 2 * ((k + n - 1) % n) + m

    def g_y_send(k):
        return send(st.at[kept(0, k)], b3.at[k], gs, at_y + k, place.to_y())

    def g_y_add(k):
        g_y_send(k).wait_recv()
        fold(st, b3[k], kept(1, k))

    def g_z_send(k):
        return send(st.at[kept(1, k)], b4.at[k - 1], gs, at_z + k - 1, place.to_z(k))

    with jax.named_scope("first_adds"):
        for at in range(2):
            g_core_add(at)
            g_x_send(at).start()
    with jax.named_scope("context_row"):
        send(dctx.at[1 - r], d_ctx.at[other_rows], single, 0, place.to_x()).wait_recv()
    upper = lax.broadcasted_iota(jnp.int32, (128, rows), 0) < HEAD_DIM
    for p in range(PAIRS):
        turned = d_ctx[:, p * 128 : (p + 1) * 128].astype(F32).T
        product = turned * ctxt[p]
        delta[2 * p] = jnp.sum(product[:HEAD_DIM], axis=0, keepdims=True)
        delta[2 * p + 1] = jnp.sum(product[HEAD_DIM:], axis=0, keepdims=True)
        dtot[2 * p] = jnp.where(upper, turned, 0.0)
        dtot[2 * p + 1] = jnp.where(upper, 0.0, turned)

    vz = (v_send, v_recv)

    def vector(number):
        level = min(number, 3)
        step = max(number - 2, 1)
        peer = (place.to_x(), place.to_core(), place.to_y(), place.to_z(step))[level]
        source = small_in if level == 0 else vec_sum.at[level - 1]
        return send(source, vec_got.at[number], vz, number, peer)

    def vector_add(level):
        vector(level).wait_recv()
        before = small_in[...] if level == 0 else vec_sum[level - 1]
        vec_sum[level] = before + vec_got[level]

    events = {}

    def add(step, what, *inputs):
        events.setdefault(step, []).append(functools.partial(what, *inputs))

    def start(what, number):
        what(number).start()

    for at in range(2 * n):
        if at > 1:
            add(at - 2, g_core_add, at)
            add(at - 1, start, g_x_send, at)
        add(6 + at, g_core_add, 2 * n + at)
    arrive = [8, 13, 18, 23]
    for at, step in enumerate(arrive):
        add(step, g_x_add, at)
    for pair in range(4):
        add(6 * pair + 3, start, core_send, pair)
        if pair < 3:
            add(6 * pair + 6, core_add, pair)
    for level in range(3):
        add(2 * level, vector_add, level)
        add(2 * level + 1, start, vector, level + 1)
    for step in range(2, n):
        add(5, start, vector, 2 + step)
    add(7, start, hop, 0)
    add(7, start, hop, 1)
    add(13, start, hop, 3)
    add(17, hop_add, 0, 1, 0)
    add(18, start, hop, 2)
    add(19, start, hop, 5)
    add(20, hop_add, 1, 2, PAIRS)
    add(21, start, hop, 4)
    add(9, start, g_y_send, 1)
    add(18, g_y_add, 1)
    add(19, start, g_z_send, 1)
    add(22, start, g_y_send, 2)

    steps = SPAN * PAIRS

    def back(t, carry):
        i, p = lax.div(t, PAIRS), lax.rem(t, PAIRS)
        for step, calls in sorted(events.items()):

            @pl.when(t == step)
            def _(calls=calls):
                with jax.named_scope(f"step_{step}"):
                    for call in calls:
                        call()

        slot = lax.rem(t, 2)

        @pl.when(t + 1 < steps)
        def _():
            p_load(t + 1, 1 - slot).start()

        @pl.when(p == 0)
        def _():
            kv_load(i).wait()

        p_load(t, slot).wait()
        where = b_block(i)
        key = kv[i, p]
        value = kv[i, PAIRS + p]
        key_t = key.T
        d_key = d_value = None
        for h in range(2):
            g = 2 * p + h
            factor = jnp.exp(m_in[where, g] - lse_in[g])
            d_rows = (dtot[g] * factor).astype(BF16)
            weights = pbuf[slot, h]
            d_probs = dot(value, d_rows, NN)
            d_scores = (weights.astype(F32) * (d_probs - delta[g] * factor)).astype(BF16)
            value_term = dot(weights, d_rows, NT)
            key_term = dot(d_scores, qm[g], NN)
            acc[g] += dot(key_t[h * HEAD_DIM : (h + 1) * HEAD_DIM], d_scores, NN)
            d_key = key_term if d_key is None else d_key + key_term
            d_value = value_term if d_value is None else d_value + value_term
        big[i, p] = d_key.astype(BF16)
        big[i, PAIRS + p] = d_value.astype(BF16)
        return carry

    lax.fori_loop(0, steps, back, jnp.int32(0))

    for p in range(PAIRS):
        both = jnp.concatenate([acc[2 * p], acc[2 * p + 1]], axis=0)
        d_all[:, p * 128 : (p + 1) * 128] = (both.T * 0.125).astype(BF16)
    with jax.named_scope("g_x_4"):
        g_x_add(4)
        g_x_add(5)
    g_y_send(3).start()
    with jax.named_scope("last_hops"):
        core_send(3).wait_recv()
        for number in (2, 3, 5, 4):
            hop(number).wait_recv()
    for piece in range(PAIRS):
        at = HALF + piece * 128
        total = big[7, piece].astype(F32) + cb[3, piece].astype(F32)
        total += rb[2, piece].astype(F32) + rb[5, piece].astype(F32)
        d_all[:, at : at + 128] = total.astype(BF16)
        at = 2 * HALF + piece * 128
        total = big[7, PAIRS + piece].astype(F32) + cb[3, PAIRS + piece].astype(F32)
        total += rb[3, piece].astype(F32) + rb[4, piece].astype(F32)
        d_all[:, at : at + 128] = total.astype(BF16)

    half = size // 2
    blk = wq_all.shape[1]

    def input_term(which):
        weight = wq_all[pl.ds(which * half, half)].reshape(HALF, QKV)
        return dot(d_all[...], weight, NT)

    with jax.named_scope("input_term"):
        grad_out[...] = input_term(1 - r)
        grad_out[own_rows, :] = grad_out[own_rows, :] + dres_low[1 - r].astype(F32)
        near[0] = grad_out[...].astype(BF16)
    with jax.named_scope("g_x_6"):
        g_x_add(6)
    with jax.named_scope("g_y_2"):
        g_y_add(2)
    to_near = send(near.at[0], near.at[1], single, 3, place.to_x())
    to_near.start()
    g_z_send(2).start()
    with jax.named_scope("qkv_grad"):
        for which in range(2):
            term = dot(hid_all[which], d_all[...], TN).astype(BF16)
            gq[which * half : (which + 1) * half] = term.reshape(half, blk, QKV)
    g_y_send(0).start()
    qz = (q_send, q_recv)

    def q_block(index, core):
        m, k = lax.div(index, n), lax.rem(index, n)
        return place.col_block(place.plane(k), lax.rem(y + 1 + m, 2), core)

    def q_core(index):
        return send(gq.at[q_block(index, 1 - j)], q1.at[index], qz, index, place.to_core())

    def q_side(k):
        return send(gq.at[q_block(k, j)], q2.at[k], qz, 2 * n + k, place.to_y())

    def q_plane(k):
        return send(gq.at[q_block(n + k, j)], q3.at[k - 1], qz, 3 * n + k - 1, place.to_z(k))

    bias_own[0, 0:1] = jnp.sum(d_all[:, :HALF].astype(F32), axis=0, keepdims=True)
    bias_own[0, 1:2] = jnp.sum(d_all[:, 2 * HALF :].astype(F32), axis=0, keepdims=True)
    bias_own[0, 2:8] = jnp.zeros((6, HALF), F32)
    sz = (s_send, s_recv)

    def small(number):
        level = min(number, 2)
        peer = (place.to_core(), place.to_y(), place.to_z(max(number - 1, 1)))[level]
        return send(bias_own.at[level], bias_got.at[number], sz, number, peer)

    loop(2 * n, lambda index: q_core(index).start())
    with jax.named_scope("input_own"):
        grad_out[...] = input_term(r)
        grad_out[own_rows, :] = grad_out[own_rows, :] + dres_own[...]
    small(0).start()

    def q_core_add(index):
        q_core(index).wait_recv()
        fold(gq, q1[index], q_block(index, j))

    with jax.named_scope("q_core_a"):
        loop(n, q_core_add)
        small(0).wait_recv()
    bias_own[1] = bias_own[0] + bias_got[0]
    loop(n, lambda k: q_side(k).start())
    with jax.named_scope("q_core_b"):
        loop(n, lambda k: q_core_add(n + k))
    small(1).start()
    with jax.named_scope("g_x_7"):
        g_x_add(7)
    with jax.named_scope("g_y_3"):
        g_y_add(3)
        g_z_send(3).start()
    with jax.named_scope("g_y_0"):
        g_y_add(0)
    with jax.named_scope("q_side"):
        for k in range(n):
            q_side(k).wait_recv()
            fold(gq, q2[k], q_block(n + k, j))
            if k:
                q_plane(k).start()
        small(1).wait_recv()
    bias_own[2] = bias_own[1] + bias_got[1]
    with jax.named_scope("near_wait"):
        to_near.wait_recv()
    grad_out[...] = grad_out[...] + near[1].astype(F32)
    for step in range(1, n):
        small(1 + step).start()
    total = vec_sum[2]
    for step in range(1, n):
        vector(2 + step).wait_recv()
        total = total + vec_got[2 + step]
    small_out[...] = total
    total = st[kept(1, 0)].astype(F32)
    with jax.named_scope("g_plane"):
        for k in range(1, n):
            g_z_send(k).wait_recv()
            total = total + b4[k - 1].astype(F32)
        wo_out[...] = total[:, :HALF]
        wi_out[...] = total[:, HALF:FIRST]
        wu_out[...] = total[:, FIRST:]
    total = gq[q_block(n, j)].astype(F32)
    with jax.named_scope("q_plane"):
        for k in range(1, n):
            q_plane(k).wait_recv()
            total = total + q3[k - 1].astype(F32)
        query_out[...] = total[:, :HALF]
        key_out[...] = total[:, HALF : 2 * HALF]
        value_out[...] = total[:, 2 * HALF :]
        total = bias_own[2]
        for step in range(1, n):
            small(1 + step).wait_recv()
            total = total + bias_got[1 + step]
        bias_out[...] = total

    loop(4 * n, lambda index: c_move(index).wait_send())
    loop(2 * n, lambda index: g_x_send(index).wait_send())
    for k in range(n):
        g_y_send(k).wait_send()
    for k in range(1, n):
        g_z_send(k).wait_send()
        q_plane(k).wait_send()
        small(1 + k).wait_send()
    small(0).wait_send()
    for number in range(n + 2):
        vector(number).wait_send()
    small(1).wait_send()
    loop(2 * n, lambda index: q_core(index).wait_send())
    loop(n, lambda k: q_side(k).wait_send())
    for pair in range(4):
        core_send(pair).wait_send()
    for number in range(6):
        hop(number).wait_send()
    to_near.wait_send()
    send(dctx.at[1 - r], d_ctx.at[own_rows], single, 0, place.to_x()).wait_send()


def backward_attention(
    size, dctx, qs, m_in, lse_in, ctxt, hid_all, wq_all, dres_low, dres_own, small_in, kv_in, p_in, g_in
):
    rows = qs.shape[1]
    part = rows // 2
    blk = wq_all.shape[1]
    n = size // 4
    any_space = pl.BlockSpec(memory_space=pl.ANY)
    vmem = pl.BlockSpec(memory_space=pltpu.VMEM)
    shape = jax.ShapeDtypeStruct
    dma = pltpu.SemaphoreType.DMA
    scratch = pltpu.VMEM
    g_count, q_count = 4 * n + 2 * n + n + n - 1, 2 * n + n + n - 1
    return pl.pallas_call(
        functools.partial(kernel_c, size),
        out_shape=(
            shape((blk, HALF), F32),
            shape((blk, HALF), F32),
            shape((blk, HALF), F32),
            shape((blk, HALF), F32),
            shape((blk, FF_HALF), F32),
            shape((blk, FF_HALF), F32),
            shape((16, D), F32),
            shape((8, HALF), F32),
            shape((rows, HALF), F32),
        ),
        in_specs=[vmem] * 10 + [any_space] * 3,
        out_specs=[vmem] * 9,
        scratch_shapes=[
            scratch((rows, HALF), BF16),
            scratch((2 * PAIRS, 128, rows), F32),
            scratch((2 * PAIRS, 1, rows), F32),
            scratch((2 * PAIRS, rows, 128), BF16),
            scratch((2 * PAIRS, HEAD_DIM, rows), F32),
            scratch((SPAN, 2 * PAIRS, rows, 128), BF16),
            scratch((2, 2, rows, rows), BF16),
            scratch((SPAN, 2 * PAIRS, rows, 128), BF16),
            scratch((4, 2 * PAIRS, rows, 128), BF16),
            scratch((6, PAIRS, rows, 128), BF16),
            scratch((4 * n, blk, REST), BF16),
            scratch((4 * n, blk, REST), BF16),
            scratch((2 * n, blk, REST), BF16),
            scratch((n, blk, REST), BF16),
            scratch((n - 1, blk, REST), BF16),
            scratch((rows, QKV), BF16),
            scratch((size, blk, QKV), BF16),
            scratch((2 * n, blk, QKV), BF16),
            scratch((n, blk, QKV), BF16),
            scratch((n - 1, blk, QKV), BF16),
            scratch((2, rows, HALF), BF16),
            scratch((3, 8, HALF), F32),
            scratch((n + 1, 8, HALF), F32),
            scratch((3, 16, D), F32),
            scratch((n + 2, 16, D), F32),
            dma((4,)),
            dma((4,)),
            dma((10,)),
            dma((10,)),
            dma((g_count,)),
            dma((g_count,)),
            dma((q_count,)),
            dma((q_count,)),
            dma((n + 1,)),
            dma((n + 1,)),
            dma((n + 2,)),
            dma((n + 2,)),
            dma((9 + 4 * n,)),
            dma((2,)),
        ],
        compiler_params=pltpu.CompilerParams(
            collective_id=1, has_side_effects=True, vmem_limit_bytes=63 * 2**20
        ),
        name="backward_attention",
    )(dctx, qs, m_in, lse_in, ctxt, hid_all, wq_all, dres_low, dres_own, small_in, kv_in, p_in, g_in)


def kernel_d(size, per, big, small, bias, *refs):
    sources, targets, tile = refs[: big + 2], refs[big + 2 : -1], refs[-1]
    for source, target in zip(sources, targets):
        target[...] = source[...]
    row = lax.axis_index("row")
    inside = lax.rem(lax.axis_index("col"), size)
    start = row * HALF + inside * per
    lines = small[...]
    tile[0:6] = pltpu.roll(lines, D - start, 1)[0:6, :128]
    spot = inside * 4 * per
    hidden = pltpu.roll(lines, D - lax.rem(spot, D), 1)[:, :128]
    wanted = 6 + 2 * row + lax.div(spot, D)
    line = lax.broadcasted_iota(jnp.int32, hidden.shape, 0)
    tile[6:7] = jnp.sum(jnp.where(line == wanted, hidden, 0.0), axis=0, keepdims=True)
    tile[7:9] = pltpu.roll(bias[...], HALF - inside * per, 1)[0:2, :128]
    tile[9:16] = jnp.zeros((7, 128), F32)


def finish(size, small, bias, arrays):
    vmem = pl.BlockSpec(memory_space=pltpu.VMEM)
    shapes = [jax.ShapeDtypeStruct(a.shape, a.dtype) for a in arrays]
    return pl.pallas_call(
        functools.partial(kernel_d, size, HALF // size, len(arrays) - 2),
        out_shape=shapes + [jax.ShapeDtypeStruct((16, 128), F32)],
        in_specs=[vmem] * (len(arrays) + 2),
        out_specs=[vmem] * (len(arrays) + 1),
        compiler_params=pltpu.CompilerParams(vmem_limit_bytes=32 * 2**20),
        name="finish",
    )(small, bias, *arrays)


def per_device(group, hidden_in, cotangent, lengths, *params):
    w_query, w_key, w_value, w_output, w_inner, w_outer = params[:6]
    b_query, b_value, b_output, b_inner, b_outer = params[6:11]
    gain_one, shift_one, gain_two, shift_two = params[11:]
    cols = lax.axis_size("col")
    size = group
    ways = cols // size
    inside = lax.axis_index("col") % size
    row = lax.axis_index("row")

    def regroup(block):
        if ways == 1:
            return block
        whole = lax.all_gather(block, "col", axis=0, tiled=True)
        count = block.shape[0] * ways
        return lax.dynamic_slice_in_dim(whole, inside * count, count, axis=0)

    vec = jnp.zeros((16, 128), BF16)
    vectors = (b_query, b_value, b_output, b_outer, gain_one, shift_one, gain_two, shift_two)
    for at, vector in enumerate(vectors + (b_inner,)):
        line = regroup(vector)
        vec += jnp.pad(line[None, :], ((at, 15 - at), (0, 128 - line.shape[0])))
    qkv_weights = [regroup(w) for w in (w_query, w_key, w_value)]
    rest_weights = [regroup(w) for w in (w_output.T, w_inner, w_outer.T)]
    (hid_all, wq_all, qs, kv, probs, m_all, lse, ctxt, g_parts, layer_out, low, own, d_context, small) = (
        forward_attention(size, lengths, hidden_in, qkv_weights, rest_weights, vec, cotangent)
    )
    (g_query, g_key, g_value, g_output, g_inner, g_outer, g_small, g_bias, grad_in) = (
        backward_attention(
            size,
            d_context,
            qs,
            m_all,
            lse,
            ctxt,
            hid_all,
            wq_all,
            low,
            own,
            small,
            kv,
            probs,
            g_parts,
        )
    )

    def spread(block):
        if ways == 1:
            return block
        count = block.shape[0]
        whole = jnp.zeros((count * size,) + block.shape[1:], block.dtype)
        whole = lax.dynamic_update_slice_in_dim(whole, block, inside * count, axis=0)
        return lax.psum_scatter(whole, "col", scatter_dimension=0, tiled=True)

    arrays = [g_query, g_key, g_value, g_output, g_inner, g_outer, grad_in, layer_out]
    *arrays, tile = finish(size, g_small, g_bias, arrays)
    g_query, g_key, g_value, g_output, g_inner, g_outer, grad_in, layer_out = arrays
    per = HALF // size
    pieces = [spread(tile[at, : 4 * per if at == 6 else per]) for at in range(9)]
    g_b_output, g_b_outer, g_gain_one, g_shift_one, g_gain_two, g_shift_two = pieces[:6]
    g_b_inner, g_b_query, g_b_value = pieces[6:]
    return (
        layer_out,
        grad_in,
        spread(g_query),
        spread(g_key),
        spread(g_value),
        spread(g_output).T,
        spread(g_inner),
        spread(g_outer).T,
        g_b_query,
        g_b_value,
        g_b_output,
        g_b_inner,
        g_b_outer,
        g_gain_one,
        g_shift_one,
        g_gain_two,
        g_shift_two,
    )


def solution(mesh):
    cols = mesh.shape["col"]
    group = max(s for s in range(SPAN, cols + 1, 4) if cols % s == 0 and D // s % 16 == 0)
    token, weight, turned = P("col", "row"), P("col", "row"), P("row", "col")
    vector = P(("row", "col"))
    return jax.shard_map(
        functools.partial(per_device, group),
        mesh=mesh,
        in_specs=(token, token, P()) + (weight,) * 3 + (turned, weight, turned) + (vector,) * 9,
        out_specs=(token, token) + (weight,) * 3 + (turned, weight, turned) + (vector,) * 9,
        check_vma=False,
    )
```

```python
import functools

import jax
import jax.numpy as jnp
from jax import lax
from jax.experimental import pallas as pl
from jax.experimental.pallas import tpu as pltpu
from jax.sharding import PartitionSpec as P

D = 768
HALF = 384
HEAD_DIM = 64
FF_HALF = 1536
PAIRS = 3
SPAN = 8
EPSILON = 1e-12
MASKED = -1e30
MESH = pl.DeviceIdType.MESH
F32 = jnp.float32
BF16 = jnp.bfloat16
FIRST = HALF + FF_HALF
REST = HALF + 2 * FF_HALF
QKV = 3 * HALF


def dot(left, right, contract):
    return lax.dot_general(left, right, (contract, ((), ())), preferred_element_type=F32)


NN = ((1,), (0,))
NT = ((1,), (1,))
TN = ((0,), (0,))


class Place:
    def __init__(self, size):
        self.size = size
        self.planes = size // 4
        self.r = lax.axis_index("row")
        col = lax.axis_index("col")
        self.base = lax.div(col, size) * size
        inner = lax.rem(col, size)
        self.slot = lax.div(col, SPAN)
        self.block = lax.rem(col, SPAN)
        self.z = lax.div(inner, 4)
        self.y = lax.rem(lax.div(inner, 2), 2)
        self.j = lax.rem(inner, 2)
        self.zl = lax.rem(self.z, 2)

    def plane(self, step):
        return lax.rem(self.z + step + self.planes, self.planes)

    def device(self, r, z, y, j):
        return (r, self.base + z * 4 + y * 2 + j)

    def to_z(self, step):
        return self.device(self.r, self.plane(step), self.y, self.j)

    def to_z_near(self):
        return self.device(self.r, self.z - self.zl + (1 - self.zl), self.y, self.j)

    def to_y(self):
        return self.device(self.r, self.z, 1 - self.y, self.j)

    def to_x(self):
        return self.device(1 - self.r, self.z, self.y, self.j)

    def to_core(self):
        return self.device(self.r, self.z, self.y, 1 - self.j)

    def col_block(self, z, y, j):
        return z * 4 + y * 2 + j

    def any_block(self, r, z, y, j):
        return r * self.size + z * 4 + y * 2 + j

    def near_block(self, dz, dy, j):
        return lax.rem(self.zl + dz, 2) * 4 + lax.rem(self.y + dy, 2) * 2 + j


def meet(place):
    barrier = pltpu.get_barrier_semaphore()
    peers = [place.to_z(step) for step in range(1, place.planes)]
    peers += [place.to_y(), place.to_x(), place.to_core()]
    for peer in peers:
        pl.semaphore_signal(barrier, inc=1, device_id=peer, device_id_type=MESH)
    pl.semaphore_wait(barrier, len(peers))


def send(src, dst, sems, index, peer):
    return pltpu.make_async_remote_copy(
        src_ref=src,
        dst_ref=dst,
        send_sem=sems[0].at[index],
        recv_sem=sems[1].at[index],
        device_id=peer,
        device_id_type=MESH,
    )


class Gather:
    def __init__(self, place, own, full, sems, with_rows):
        self.place, self.own, self.full, self.sems = place, own, full, sems
        self.rows = 2 if with_rows else 1
        self.with_rows = with_rows
        n = place.planes
        self.at_y = n - 1
        self.at_x = self.at_y + n
        self.at_c = self.at_x + (2 * n if with_rows else 0)
        self.total = self.at_c + 2 * n * self.rows

    def index(self, n, k, m, j):
        p = self.place
        z, y = p.plane(-k), lax.rem(p.y + m, 2)
        if self.with_rows:
            return p.any_block(lax.rem(p.r + n, 2), z, y, j)
        return p.col_block(z, y, j)

    def move(self, number, peer, n, k, m, j, local):
        where = self.index(n, k, m, j)
        src = self.own if local else self.full.at[where]
        return send(src, self.full.at[where], self.sems, number, peer)

    def z_sends(self):
        p = self.place
        for step in range(1, p.planes):
            self.move(step - 1, p.to_z(step), 0, 0, 0, p.j, True).start()

    def z_done(self, k):
        p = self.place
        self.move(k - 1, p.to_z(k), 0, k, 0, p.j, False).wait_recv()

    def y_send(self, k):
        p = self.place
        self.move(self.at_y + k, p.to_y(), 0, k, 0, p.j, k == 0).start()

    def y_done(self, k):
        p = self.place
        self.move(self.at_y + k, p.to_y(), 0, k, 1, p.j, False).wait_recv()

    def x_send(self, k, m):
        p = self.place
        self.move(self.at_x + 2 * k + m, p.to_x(), 0, k, m, p.j, k + m == 0).start()

    def x_done(self, k, m):
        p = self.place
        self.move(self.at_x + 2 * k + m, p.to_x(), 1, k, m, p.j, False).wait_recv()

    def c_number(self, n, k, m):
        return self.at_c + (2 * k + m) * self.rows + n

    def c_send(self, n, k, m):
        p = self.place
        number = self.c_number(n, k, m)
        self.move(number, p.to_core(), n, k, m, p.j, n + k + m == 0).start()

    def c_done(self, n, k, m):
        p = self.place
        self.move(self.c_number(n, k, m), p.to_core(), n, k, m, 1 - p.j, False).wait_recv()

    def all_sent(self):
        for number in range(self.total):
            send(self.own, self.own, self.sems, number, self.place.to_core()).wait_send()


def spread_rows(tiles, picks, per, width):
    blocks = tiles.shape[0]
    flat = tiles.reshape(blocks * 16, 128)
    total = len(picks) * blocks
    line = lax.broadcasted_iota(jnp.int32, (total, blocks * 16), 0)
    at = lax.broadcasted_iota(jnp.int32, (total, blocks * 16), 1)
    wanted = jnp.zeros((total, blocks * 16), F32)
    for spot, pick in enumerate(picks):
        hit = at == (line - spot * blocks) * 16 + pick
        inside = (line >= spot * blocks) & (line < (spot + 1) * blocks)
        wanted = jnp.where(hit & inside, 1.0, wanted)
    taken = dot(wanted.astype(BF16), flat, NN).astype(BF16)
    lane = lax.broadcasted_iota(jnp.int32, (128, width), 1).astype(F32)
    group = jnp.floor((lane + 0.5) * (1.0 / per))
    place = lax.broadcasted_iota(jnp.int32, (128, width), 0).astype(F32)
    copies = jnp.where(lane - group * per == place, 1.0, 0.0).astype(BF16)
    wide = dot(taken, copies, NN)
    first = lax.broadcasted_iota(jnp.int32, (blocks, width), 0) * per
    column = lax.broadcasted_iota(jnp.int32, (blocks, width), 1)
    mask = (column >= first) & (column < first + per)
    rows = []
    for spot in range(len(picks)):
        part = jnp.where(mask, wide[spot * blocks : (spot + 1) * blocks], 0.0)
        rows.append(jnp.sum(part, axis=0, keepdims=True))
    return rows


def gelu_both(argument):
    spread = 1.0 + lax.erf(argument * 0.7071067811865476)
    bell = jnp.exp(argument * argument * -0.5) * 0.3989422804014327
    return 0.5 * argument * spread, 0.5 * spread + argument * bell


def norm_forward(resid, gain, shift):
    center = resid - jnp.mean(resid, axis=1, keepdims=True)
    scale = lax.rsqrt(jnp.mean(center * center, axis=1, keepdims=True) + EPSILON)
    normal = center * scale
    return normal * gain + shift, normal, scale


def norm_backward(incoming, normal, scale, gain):
    scaled = incoming * gain
    first = jnp.mean(scaled, axis=1, keepdims=True)
    second = jnp.mean(scaled * normal, axis=1, keepdims=True)
    result = scale * (scaled - first - normal * second)
    sums = jnp.sum(incoming * normal, axis=0, keepdims=True)
    return result, sums, jnp.sum(incoming, axis=0, keepdims=True)


def kernel_a(
    size,
    lengths,
    hid,
    w_query,
    w_key,
    w_value,
    w_output,
    w_inner,
    w_outer,
    vec_in,
    cot,
    hid_out,
    wq_out,
    q_out,
    kv_out,
    p_out,
    m_out,
    lse_out,
    ctxt_out,
    g_out,
    final_out,
    low_out,
    own_out,
    d_out,
    small_out,
    hid_all,
    wq_own,
    wq_all,
    vec_all,
    one_own,
    one_all,
    two_all,
    kv,
    qs,
    qm,
    acc,
    high,
    low,
    pbuf,
    ctx_tp,
    ctx_in,
    cot_in,
    lay_out,
    lay_far,
    normed_ref,
    normal_ref,
    low_ref,
    slope_ref,
    act_ref,
    d_ref,
    one_send,
    one_recv,
    two_send,
    two_recv,
    wq_send,
    wq_recv,
    vec_send,
    vec_recv,
    kv_send,
    kv_recv,
    lone_send,
    lone_recv,
    local,
    p_sem,
):
    place = Place(size)
    rows = hid.shape[0]
    part = rows // 2
    n = place.planes
    r, y, j = place.r, place.y, place.j
    blk = w_query.shape[0]
    for at, source in enumerate((w_query, w_key, w_value)):
        wq_own[:, at * HALF : (at + 1) * HALF] = source[...]
    one_own[:, :HALF] = w_output[...]
    one_own[:, HALF:] = w_inner[...]
    with jax.named_scope("meet"):
        meet(place)

    single = (lone_send, lone_recv)
    own_rows = pl.ds(pl.multiple_of(r * part, part), part)
    other_rows = pl.ds(pl.multiple_of((1 - r) * part, part), part)
    to_hid = send(hid, hid_all.at[r], single, 0, place.to_x())
    to_hid.start()
    vec = Gather(place, vec_in, vec_all, (vec_send, vec_recv), True)
    wq = Gather(place, wq_own, wq_all, (wq_send, wq_recv), False)
    one = Gather(place, one_own, one_all, (one_send, one_recv), True)
    two = Gather(place, w_outer, two_all, (two_send, two_recv), True)
    for gather in (vec, wq):
        gather.z_sends()
        gather.y_send(0)
        gather.c_send(0, 0, 0)
    vec.x_send(0, 0)
    one.x_send(0, 0)
    one.y_send(0)
    two.x_send(0, 0)
    to_cot = send(cot.at[other_rows], cot_in.at[r], single, 1, place.to_x())
    to_cot.start()
    one.c_send(0, 0, 0)
    two.c_send(0, 0, 0)
    hid_all[r] = hid[...]
    mine = place.any_block(r, place.z, y, j)
    wq_all[place.col_block(place.z, y, j)] = wq_own[...]
    vec_all[mine] = vec_in[...]
    one_all[mine] = one_own[...]
    two_all[mine] = w_outer[...]
    cot_in[r] = cot[own_rows, :]
    for k in range(1, n):
        with jax.named_scope(f"qkv_plane_{k}"):
            for gather in (vec, wq):
                gather.z_done(k)
                gather.y_send(k)
                gather.c_send(0, k, 0)
            vec.x_send(k, 0)
    one.z_sends()
    two.y_send(0)
    for k in range(n):
        with jax.named_scope(f"qkv_side_{k}"):
            for gather in (vec, wq):
                gather.y_done(k)
                gather.c_send(0, k, 1)
            vec.x_send(k, 1)
    with jax.named_scope("qkv_core"):
        for k in range(n):
            for m in range(2):
                for gather in (vec, wq):
                    gather.c_done(0, k, m)
    with jax.named_scope("hidden"):
        send(hid, hid_all.at[1 - r], single, 0, place.to_x()).wait_recv()

    def rest_y(gather, k):
        gather.z_done(k)
        gather.y_send(k)
        gather.x_send(k, 0)
        gather.c_send(0, k, 0)

    def rest_x(gather, k):
        gather.y_done(k)
        gather.x_send(k, 1)
        gather.c_send(0, k, 1)

    def rest_c(gather, k, m):
        gather.x_done(k, m)
        gather.c_send(1, k, m)

    def rest_all(gather):
        for n_at in range(2):
            for k in range(n):
                for m in range(2):
                    if gather is not vec or n_at:
                        gather.c_done(n_at, k, m)

    hid_local = pltpu.make_async_copy(hid_all, hid_out, local.at[2])
    hid_local.start()
    wq_local = pltpu.make_async_copy(wq_all, wq_out, local.at[3])
    wq_local.start()

    own_tiles = vec_all[pl.ds(r * size, size)]
    b_query, b_value = spread_rows(own_tiles, (0, 1), HALF // size, HALF)
    own = place.near_block(0, 0, j)
    half = size // 2
    for which in (1, 2, 0):
        columns = slice(which * HALF, (which + 1) * HALF)
        total = dot(hid_all[0], wq_all[:half, :, columns].reshape(HALF, HALF), NN)
        total += dot(hid_all[1], wq_all[half:, :, columns].reshape(HALF, HALF), NN)
        if which == 0:
            total += b_query
        if which == 2:
            total += b_value
        total = total.astype(BF16)
        for p in range(PAIRS):
            piece = total[:, p * 128 : (p + 1) * 128]
            if which == 0:
                lane = lax.broadcasted_iota(jnp.int32, (rows, 128), 1)
                piece = piece * jnp.asarray(0.125, BF16)
                qs[p] = piece
                qm[2 * p] = jnp.where(lane < HEAD_DIM, piece, jnp.zeros_like(piece))
                qm[2 * p + 1] = jnp.where(lane >= HEAD_DIM, piece, jnp.zeros_like(piece))
            else:
                kv[own, (which - 1) * PAIRS + p] = piece
        if which == 1:
            with jax.named_scope("after_key"):
                rest_x(one, 0)
        if which == 2:
            with jax.named_scope("after_value"):
                rest_y(one, 1)
    acc[...] = jnp.zeros_like(acc)
    high[...] = jnp.full_like(high, MASKED)
    low[...] = jnp.zeros_like(low)

    n_one = place.device(r, place.z - place.zl + lax.rem(place.zl + 1 - j, 2), lax.rem(y + j, 2), j)
    n_two = place.device(r, place.z - place.zl + lax.rem(place.zl + j, 2), lax.rem(y + 1 - j, 2), j)
    kvs = (kv_send, kv_recv)

    def kv_block(i):
        pair, core = lax.div(i, 2), lax.rem(j + lax.rem(i, 2), 2)
        b0, b1 = lax.rem(pair, 2), lax.div(pair, 2)
        return place.near_block(b0 * (1 - core) + b1 * core, b0 * core + b1 * (1 - core), core)

    def kv_move(number, what, peer):
        where = kv_block(what)
        return send(kv.at[where], kv.at[where], kvs, number, peer)

    kv_move(1, 0, place.to_core()).start()
    kv_move(2, 0, n_one).start()
    q_local = pltpu.make_async_copy(qs, q_out, local.at[4])
    q_local.start()

    def arrived(number):
        kv_move(number, number, n_one).wait_recv()

    def second():
        kv_move(4, 0, n_two).start()

    def first_here():
        arrived(2)
        kv_move(3, 2, place.to_core()).start()

    def third():
        kv_move(6, 2, n_two).start()

    def second_here():
        arrived(4)
        kv_move(5, 4, place.to_core()).start()

    def third_here():
        arrived(6)
        kv_move(7, 6, place.to_core()).start()

    def vec_rows():
        for k in range(n):
            for m in range(2):
                rest_c(vec, k, m)

    def two_start():
        two.z_sends()

    events = {}

    def add(step, what, *inputs):
        events.setdefault(step, []).append(functools.partial(what, *inputs))

    add(1, vec_rows)
    add(2, rest_x, one, 1)
    add(2, two_start)
    add(3, arrived, 1)
    add(4, rest_y, one, 2)
    add(5, rest_y, one, 3)
    add(5, second)
    add(6, rest_x, two, 0)
    add(6, first_here)
    add(7, rest_x, one, 2)
    add(8, rest_x, one, 3)
    add(8, rest_c, one, 0, 0)
    add(8, third)
    add(9, rest_c, one, 1, 0)
    add(9, arrived, 3)
    add(10, rest_y, two, 1)
    add(12, second_here)
    add(13, rest_c, one, 0, 1)
    add(13, rest_c, one, 1, 1)
    add(13, rest_y, two, 2)
    add(14, rest_x, two, 1)
    add(15, arrived, 5)
    add(15, rest_y, two, 3)
    add(16, rest_c, one, 2, 0)
    add(17, rest_c, one, 3, 0)
    add(17, rest_x, two, 2)
    add(18, third_here)
    add(19, rest_c, one, 2, 1)
    add(20, rest_x, two, 3)
    add(21, arrived, 7)
    add(21, rest_c, one, 3, 1)
    add(22, rest_c, two, 0, 0)
    add(23, rest_c, two, 0, 1)

    length = lengths[place.slot]

    def p_copy(t, slot):
        i, p = lax.div(t, PAIRS), lax.rem(t, PAIRS)
        return pltpu.make_async_copy(
            pbuf.at[slot], p_out.at[kv_block(i), pl.ds(2 * p, 2)], p_sem.at[slot]
        )

    def kv_copy(i):
        where = kv_block(i)
        return pltpu.make_async_copy(kv.at[where], kv_out.at[where], local.at[8 + i])

    steps = SPAN * PAIRS

    def attend(t, carry):
        i, p = lax.div(t, PAIRS), lax.rem(t, PAIRS)
        for step, calls in sorted(events.items()):

            @pl.when(t == step)
            def _(calls=calls):
                for call in calls:
                    with jax.named_scope(f"at_{step}"):
                        call()

        @pl.when(p == 0)
        def _():
            kv_copy(i).start()

        slot = lax.rem(t, 2)

        @pl.when(t >= 2)
        def _():
            p_copy(t - 2, slot).wait()

        where = kv_block(i)
        place_of = lax.broadcasted_iota(jnp.int32, (rows, 128), 0) + where * rows
        bias = jnp.where(place_of < length, 0.0, MASKED)
        bias = jnp.concatenate([bias] * (rows // 128), axis=1)
        key = kv[where, p]
        value_t = kv[where, PAIRS + p].T
        for h in range(2):
            g = 2 * p + h
            scores = dot(key, qm[g], NT) + bias
            top = jnp.max(scores, axis=0, keepdims=True)
            weights = jnp.exp(scores - top)
            below = jnp.sum(weights, axis=0, keepdims=True)
            rounded = weights.astype(BF16)
            pbuf[slot, h] = rounded
            term = dot(value_t[h * HEAD_DIM : (h + 1) * HEAD_DIM], rounded, NN)
            old = high[g]
            new = jnp.maximum(old, top)
            keep_old, keep_new = jnp.exp(old - new), jnp.exp(top - new)
            high[g] = new
            low[g] = low[g] * keep_old + below * keep_new
            acc[g] = acc[g] * keep_old + term * keep_new
            m_out[where, g] = top
        p_copy(t, slot).start()
        return carry

    lax.fori_loop(0, steps, attend, jnp.int32(0))

    column = lax.broadcasted_iota(jnp.int32, (1, rows), 1) + place.block * rows
    keep = jnp.where(column < length, 1.0, 0.0)
    for p in range(PAIRS):
        parts = []
        for h in range(2):
            g = 2 * p + h
            lse_out[g] = high[g] + jnp.log(low[g])
            parts.append(acc[g] / low[g])
        both = jnp.concatenate(parts, axis=0)
        ctxt_out[p] = both
        ctx_tp[:, p * 128 : (p + 1) * 128] = (both * keep).T.astype(BF16)
    for t in (steps - 2, steps - 1):
        p_copy(jnp.int32(t), t % 2).wait()
    to_ctx = send(ctx_tp.at[other_rows], ctx_in.at[r], single, 2, place.to_x())
    to_ctx.start()
    ctx_in[r] = ctx_tp[own_rows, :]
    with jax.named_scope("one_all"):
        rest_all(vec)
        rest_all(one)
    six = spread_rows(vec_all[...], (2, 3, 4, 5, 6, 7), HALF // size, D)
    b_output, b_outer, gain_one, shift_one, gain_two, shift_two = six
    (b_inner,) = spread_rows(vec_all[...], (8,), FF_HALF // size, 2 * FF_HALF)
    hidden = jnp.concatenate([hid_all[0, own_rows, :], hid_all[1, own_rows, :]], axis=1)
    with jax.named_scope("context"):
        send(ctx_tp.at[other_rows], ctx_in.at[1 - r], single, 2, place.to_x()).wait_recv()

    def weight(ref, h, columns):
        block = ref[h * size : (h + 1) * size, :, columns]
        return block.reshape(D, block.shape[2])

    out_cols, in_cols, all_cols = slice(0, HALF), slice(HALF, FIRST), slice(0, FF_HALF)
    with jax.named_scope("middle_one"):
        attn = dot(ctx_in[0], weight(one_all, 0, out_cols), NT)
        attn += dot(ctx_in[1], weight(one_all, 1, out_cols), NT) + b_output
        normed, normal, scale_one = norm_forward(hidden.astype(F32) + attn, gain_one, shift_one)
        normed_ref[...] = normed
        normal_ref[...] = normal
        low_ref[...] = normed.astype(BF16)
    with jax.named_scope("two_late"):
        rest_c(two, 1, 0)
        rest_c(two, 1, 1)
    for h in range(2):
        with jax.named_scope(f"inner_{h}"):
            span = slice(h * FF_HALF, (h + 1) * FF_HALF)
            inner = dot(low_ref[...], weight(one_all, h, in_cols), NN) + b_inner[:, span]
            value, slope = gelu_both(inner)
            act_ref[:, span] = value.astype(BF16)
            slope_ref[:, span] = slope
    with jax.named_scope("two_all"):
        for k in range(2, n):
            for m in range(2):
                rest_c(two, k, m)
        rest_all(two)
    with jax.named_scope("outer"):
        outer = dot(act_ref[:, :FF_HALF], weight(two_all, 0, all_cols), NT)
        outer += dot(act_ref[:, FF_HALF:], weight(two_all, 1, all_cols), NT) + b_outer
        result, normal_two, scale_two = norm_forward(normed_ref[...] + outer, gain_two, shift_two)
        lay_out[0] = result[:, :HALF].astype(BF16)
        lay_out[1] = result[:, HALF:].astype(BF16)
    to_lay = send(lay_out.at[1 - r], lay_far.at[r], single, 3, place.to_x())
    to_lay.start()
    spot = lax.broadcasted_iota(jnp.int32, (part, 1), 0) + place.block * rows + r * part
    keep = jnp.where(spot < length, 1.0, 0.0)
    with jax.named_scope("cotangent"):
        send(cot.at[other_rows], cot_in.at[1 - r], single, 1, place.to_x()).wait_recv()
    with jax.named_scope("norm_two"):
        seed = jnp.concatenate([cot_in[0], cot_in[1]], axis=1).astype(F32) * keep
        d_two, g_gain_two, g_shift_two = norm_backward(seed, normal_two, scale_two, gain_two)
        d_outer = d_two.astype(BF16)
        small_out[4:5] = g_gain_two
        small_out[5:6] = g_shift_two
        small_out[1:2] = jnp.sum(d_outer.astype(F32), axis=0, keepdims=True)
    d_normed = d_two
    d_outer_t = d_outer.T
    for h in range(2):
        with jax.named_scope(f"d_inner_{h}"):
            span = slice(h * FF_HALF, (h + 1) * FF_HALF)
            d_inner = dot(d_outer, weight(two_all, h, all_cols), NN) * slope_ref[:, span]
            d_inner = d_inner.astype(BF16)
            d_ref[:, span] = d_inner
            sums = jnp.sum(d_inner.astype(F32), axis=0, keepdims=True)
            small_out[6 + 2 * h : 7 + 2 * h] = sums[:, :D]
            small_out[7 + 2 * h : 8 + 2 * h] = sums[:, D:]
            d_normed += dot(d_inner, weight(one_all, h, in_cols), NT)
    with jax.named_scope("all_sent"):
        for gather in (vec, wq, one, two):
            gather.all_sent()
    own_col = pl.ds(pl.multiple_of(r * HALF, HALF), HALF)

    def give(number, ref, h, columns, target):
        return pltpu.make_async_copy(
            ref.at[pl.ds(h * size, size), :, columns],
            g_out.at[pl.ds(h * size, size), :, target],
            local.at[16 + number],
        )

    gives = []
    for h in range(2):
        with jax.named_scope(f"g_outer_{h}"):
            span = slice(h * FF_HALF, (h + 1) * FF_HALF)
            term = dot(d_outer_t, act_ref[:, span], NN).astype(BF16)
            two_all[h * size : (h + 1) * size] = term.reshape(size, blk, FF_HALF)
            copy = give(h, two_all, h, pl.ds(0, FF_HALF), pl.ds(FIRST, FF_HALF))
            copy.start()
            gives.append(copy)
    with jax.named_scope("norm_one"):
        d_one, g_gain_one, g_shift_one = norm_backward(d_normed, normal_ref[...], scale_one, gain_one)
        d_attn = d_one.astype(BF16)
        small_out[2:3] = g_gain_one
        small_out[3:4] = g_shift_one
        small_out[0:1] = jnp.sum(d_attn.astype(F32), axis=0, keepdims=True)
        small_out[10:16] = jnp.zeros((6, D), F32)
        for h in range(2):
            low_out[h] = d_attn[:, h * HALF : (h + 1) * HALF]
        normed_ref[...] = d_one
        own_out[...] = normed_ref[:, own_col]
    with jax.named_scope("d_context"):
        for h in range(2):
            d_context = dot(d_attn, weight(one_all, h, out_cols), NN) * keep
            d_out[h] = d_context.astype(BF16)
    low_t = low_ref[...].T
    d_attn_t = d_attn.T
    for h in range(2):
        with jax.named_scope(f"g_inner_{h}"):
            span = slice(h * FF_HALF, (h + 1) * FF_HALF)
            term = dot(low_t, d_ref[:, span], NN).astype(BF16)
            one_all[h * size : (h + 1) * size, :, HALF:] = term.reshape(size, blk, FF_HALF)
            term = dot(d_attn_t, ctx_in[h], NN).astype(BF16)
            one_all[h * size : (h + 1) * size, :, :HALF] = term.reshape(size, blk, HALF)
            copy = give(2 + h, one_all, h, pl.ds(0, FIRST), pl.ds(0, FIRST))
            copy.start()
            gives.append(copy)
    for number in range(1, 8):
        kv_move(number, 0, n_one).wait_send()
    to_lay.wait_send()
    send(lay_far.at[r], lay_far.at[1 - r], single, 3, place.to_x()).wait_recv()
    final_out[own_rows, :] = lay_out[r]
    final_out[other_rows, :] = lay_far[1 - r]
    for number in range(3):
        block = hid if number == 0 else ctx_in.at[0]
        send(block, block, single, number, place.to_x()).wait_send()
    for copy in [hid_local, wq_local, q_local] + gives:
        copy.wait()
    for i in range(SPAN):
        kv_copy(jnp.int32(i)).wait()


def forward_attention(size, lengths, hid, qkv_weights, rest_weights, vec, cot):
    rows = hid.shape[0]
    part = rows // 2
    blk = qkv_weights[0].shape[0]
    n = size // 4
    any_space = pl.BlockSpec(memory_space=pl.ANY)
    vmem = pl.BlockSpec(memory_space=pltpu.VMEM)
    shape = jax.ShapeDtypeStruct
    n_col, n_all = (n - 1) + n + 2 * n, (n - 1) + n + 2 * n + 4 * n
    dma = pltpu.SemaphoreType.DMA
    scratch = pltpu.VMEM
    return pl.pallas_call(
        functools.partial(kernel_a, size),
        out_shape=(
            shape((2, rows, HALF), BF16),
            shape((size, blk, QKV), BF16),
            shape((PAIRS, rows, 128), BF16),
            shape((SPAN, 2 * PAIRS, rows, 128), BF16),
            shape((SPAN, 2 * PAIRS, rows, rows), BF16),
            shape((SPAN, 2 * PAIRS, 1, rows), F32),
            shape((2 * PAIRS, 1, rows), F32),
            shape((PAIRS, 128, rows), F32),
            shape((2 * size, blk, REST), BF16),
            shape((rows, HALF), BF16),
            shape((2, part, HALF), BF16),
            shape((part, HALF), F32),
            shape((2, part, HALF), BF16),
            shape((16, D), F32),
        ),
        in_specs=[pl.BlockSpec(memory_space=pltpu.SMEM)] + [vmem] * 9,
        out_specs=[any_space] * 5 + [vmem] * 3 + [any_space] + [vmem] * 5,
        scratch_shapes=[
            scratch((2, rows, HALF), BF16),
            scratch((blk, QKV), BF16),
            scratch((size, blk, QKV), BF16),
            scratch((2 * size, 16, 128), BF16),
            scratch((blk, FIRST), BF16),
            scratch((2 * size, blk, FIRST), BF16),
            scratch((2 * size, blk, FF_HALF), BF16),
            scratch((SPAN, 2 * PAIRS, rows, 128), BF16),
            scratch((PAIRS, rows, 128), BF16),
            scratch((2 * PAIRS, rows, 128), BF16),
            scratch((2 * PAIRS, HEAD_DIM, rows), F32),
            scratch((2 * PAIRS, 1, rows), F32),
            scratch((2 * PAIRS, 1, rows), F32),
            scratch((2, 2, rows, rows), BF16),
            scratch((rows, HALF), BF16),
            scratch((2, part, HALF), BF16),
            scratch((2, part, HALF), BF16),
            scratch((2, part, HALF), BF16),
            scratch((2, part, HALF), BF16),
            scratch((part, D), F32),
            scratch((part, D), F32),
            scratch((part, D), BF16),
            scratch((part, 2 * FF_HALF), F32),
            scratch((part, 2 * FF_HALF), BF16),
            scratch((part, 2 * FF_HALF), BF16),
            dma((n_all,)),
            dma((n_all,)),
            dma((n_all,)),
            dma((n_all,)),
            dma((n_col,)),
            dma((n_col,)),
            dma((n_all,)),
            dma((n_all,)),
            dma((8,)),
            dma((8,)),
            dma((4,)),
            dma((4,)),
            dma((20,)),
            dma((2,)),
        ],
        compiler_params=pltpu.CompilerParams(
            collective_id=0, has_side_effects=True, vmem_limit_bytes=62 * 2**20
        ),
        name="forward_attention",
    )(lengths, hid, *qkv_weights, *rest_weights, vec, cot)


def kernel_c(
    size,
    dctx,
    qs,
    m_in,
    lse_in,
    ctxt,
    hid_all,
    wq_all,
    dres_low,
    dres_own,
    small_in,
    kv_in,
    p_in,
    g_in,
    query_out,
    key_out,
    value_out,
    wo_out,
    wi_out,
    wu_out,
    small_out,
    bias_out,
    grad_out,
    d_ctx,
    dtot,
    delta,
    qm,
    acc,
    kv,
    pbuf,
    big,
    cb,
    rb,
    st,
    b1,
    b2,
    b3,
    b4,
    d_all,
    hid_t,
    far,
    gq,
    q1,
    q2,
    q3,
    near,
    bias_own,
    bias_got,
    vec_sum,
    vec_got,
    one_send,
    one_recv,
    kv_send,
    kv_recv,
    g_send,
    g_recv,
    q_send,
    q_recv,
    s_send,
    s_recv,
    v_send,
    v_recv,
    load,
    p_sem,
):
    place = Place(size)
    rows = qs.shape[1]
    part = rows // 2
    n = place.planes
    r, y, j = place.r, place.y, place.j
    half = size // 2
    blk = wq_all.shape[1]
    own_rows = pl.ds(pl.multiple_of(r * part, part), part)
    other_rows = pl.ds(pl.multiple_of((1 - r) * part, part), part)

    def b_block(i):
        pair, core = lax.div(i, 2), lax.rem(j + 1 + lax.rem(i, 2), 2)
        return place.near_block(1 - lax.div(pair, 2), 1 - lax.rem(pair, 2), core)

    def kv_load(i):
        return pltpu.make_async_copy(kv_in.at[b_block(i)], kv.at[i], load.at[i])

    def p_load(t, slot):
        p, i = lax.div(t, SPAN), lax.rem(t, SPAN)
        return pltpu.make_async_copy(
            p_in.at[b_block(i), pl.ds(2 * p, 2)], pbuf.at[slot], p_sem.at[slot]
        )

    def index(other, k, m):
        return 2 * n * other + 2 * ((k + n - 1) % n) + m

    def g_block(at, core):
        n_at, m = at // (2 * n), at % 2
        k = ((at % (2 * n)) // 2 + 1) % n
        return place.any_block(
            lax.rem(r + 1 + n_at, 2), place.plane(k), lax.rem(y + 1 + m, 2), core
        )

    def g_load(at):
        return pltpu.make_async_copy(g_in.at[g_block(at, j)], st.at[at], load.at[8 + at])

    def loop(count, body):
        def step(at, carry):
            body(at)
            return carry

        lax.fori_loop(0, count, step, jnp.int32(0))

    needed = [(0, 1, 0), (0, 2, 0), (1, 2, 0), (0, 1, 1), (0, 3, 0), (0, 3, 1), (0, 2, 1), (1, 2, 1)]
    needed += [(1, 1, 0), (1, 1, 1), (0, 0, 0), (0, 0, 1), (1, 3, 0), (1, 3, 1), (1, 0, 0), (1, 0, 1)]
    needed = [index(*at) for at in needed]
    p_load(jnp.int32(0), 0).start()
    for at in needed[:4]:
        g_load(at).start()
    loop(SPAN, lambda i: kv_load(i).start())
    for at in needed[4:]:
        g_load(at).start()
    lane = lax.broadcasted_iota(jnp.int32, (rows, 128), 1)
    for p in range(PAIRS):
        piece = qs[p]
        qm[2 * p] = jnp.where(lane < HEAD_DIM, piece, jnp.zeros_like(piece))
        qm[2 * p + 1] = jnp.where(lane >= HEAD_DIM, piece, jnp.zeros_like(piece))
    acc[...] = jnp.zeros_like(acc)
    for which in range(2):
        hid_t[which] = hid_all[which].T
    d_ctx[own_rows, :] = dctx[r]
    far[...] = jnp.zeros_like(far)
    far[own_rows, :] = dres_low[1 - r].astype(F32)
    grad_out[...] = jnp.zeros_like(grad_out)
    grad_out[own_rows, :] = dres_own[...]
    with jax.named_scope("meet"):
        meet(place)
    single = (one_send, one_recv)
    gs = (g_send, g_recv)
    ks = (kv_send, kv_recv)
    at_x, at_y, at_z = 4 * n, 6 * n, 8 * n

    send(dctx.at[1 - r], d_ctx.at[own_rows], single, 0, place.to_x()).start()
    send(small_in, vec_got.at[0], (v_send, v_recv), 0, place.to_x()).start()

    def c_move(at):
        return send(g_in.at[g_block(at, 1 - j)], b1.at[at], gs, at, place.to_core())

    for at in needed:
        c_move(at).start()

    def fold(target, source, at):
        total = target[at].astype(F32) + source.astype(F32)
        target[at] = total.astype(BF16)

    def pieces(p):
        return pl.ds(2 * p, 2)

    def core_send(p, pair):
        return send(
            big.at[2 * pair, pieces(p)], cb.at[pair, pieces(p)], ks, 4 * p + pair, place.to_core()
        )

    def core_add(p, pair):
        core_send(p, pair).wait_recv()
        for piece in (2 * p, 2 * p + 1):
            fold(big, cb[pair, piece], (2 * pair + 1, piece))

    def hop(p, pair):
        peer = place.to_y() if pair == 2 else place.to_z_near()
        number = 4 * PAIRS + 3 * p + pair
        return send(big.at[2 * pair + 1, pieces(p)], rb.at[pair, pieces(p)], ks, number, peer)

    def hop_add(p):
        hop(p, 0).wait_recv()
        for piece in (2 * p, 2 * p + 1):
            fold(big, rb[0, piece], (5, piece))

    def g_core_add(other, k, m):
        at = index(other, k, m)
        c_move(at).wait_recv()
        g_load(at).wait()
        fold(st, b1[at], at)

    def gx(k, m):
        at = index(0, k, m)
        return send(st.at[at], b2.at[at], gs, at_x + at, place.to_x())

    def gx_add(k, m):
        gx(k, m).wait_recv()
        fold(st, b2[index(0, k, m)], index(1, k, m))

    def gy(k, other):
        slot = 2 * k + other
        return send(st.at[index(other, k, 0)], b3.at[slot], gs, at_y + slot, place.to_y())

    def gy_add(k, other):
        gy(k, other).wait_recv()
        fold(st, b3[2 * k + other], index(other, k, 1))

    def gz(k):
        return send(st.at[index(1, k, 1)], b4.at[k - 1], gs, at_z + k - 1, place.to_z(k))

    vz = (v_send, v_recv)

    def vector(number):
        level = min(number, 3)
        step = max(number - 2, 1)
        peer = (place.to_x(), place.to_core(), place.to_y(), place.to_z(step))[level]
        source = small_in if level == 0 else vec_sum.at[level - 1]
        return send(source, vec_got.at[number], vz, number, peer)

    def vector_add(level):
        vector(level).wait_recv()
        before = small_in[...] if level == 0 else vec_sum[level - 1]
        vec_sum[level] = before + vec_got[level]

    with jax.named_scope("first_adds"):
        g_core_add(0, 1, 0)
        gx(1, 0).start()
        g_core_add(0, 2, 0)
        gy(2, 0).start()
    with jax.named_scope("context_row"):
        send(dctx.at[1 - r], d_ctx.at[other_rows], single, 0, place.to_x()).wait_recv()
    upper = lax.broadcasted_iota(jnp.int32, (128, rows), 0) < HEAD_DIM
    for p in range(PAIRS):
        turned = d_ctx[:, p * 128 : (p + 1) * 128].astype(F32).T
        product = turned * ctxt[p]
        delta[2 * p] = jnp.sum(product[:HEAD_DIM], axis=0, keepdims=True)
        delta[2 * p + 1] = jnp.sum(product[HEAD_DIM:], axis=0, keepdims=True)
        dtot[2 * p] = jnp.where(upper, turned, 0.0)
        dtot[2 * p + 1] = jnp.where(upper, 0.0, turned)
    with jax.named_scope("vector_row"):
        vector_add(0)
        vector(1).start()

    qz = (q_send, q_recv)

    def q_core(p):
        return send(gq.at[p, 1 - j], q1.at[p], qz, (n + 1) * p, place.to_core())

    def q_side(p):
        return send(gq.at[p, j, 1 - y], q2.at[p], qz, (n + 1) * p + 1, place.to_y())

    def q_plane(p, k):
        return send(
            gq.at[p, j, y, place.plane(k)], q3.at[p, k - 1], qz, (n + 1) * p + 1 + k, place.to_z(k)
        )

    def q_core_add(p):
        q_core(p).wait_recv()
        for side in range(2):
            fold(gq, q1[p, side], (p, j, side))

    def q_side_add(p):
        q_side(p).wait_recv()
        fold(gq, q2[p], (p, j, y))

    def q_planes(p):
        for k in range(1, n):
            q_plane(p, k).start()

    def settle(p):
        core_send(p, 3).wait_recv()
        hop(p, 1).wait_recv()
        hop(p, 2).wait_recv()
        both = jnp.concatenate([acc[2 * p], acc[2 * p + 1]], axis=0)
        d_query = (both.T * 0.125).astype(BF16)
        d_all[p, :, 0:128] = d_query
        lanes = slice(p * 128, (p + 1) * 128)
        bias_own[0, 0:1, lanes] = jnp.sum(d_query.astype(F32), axis=0, keepdims=True)
        for at in range(2):
            piece = 2 * p + at
            total = big[7, piece].astype(F32) + cb[3, piece].astype(F32)
            total += rb[1, piece].astype(F32) + rb[2, piece].astype(F32)
            low = total.astype(BF16)
            d_all[p, :, (at + 1) * 128 : (at + 2) * 128] = low
        bias_own[0, 1:2, lanes] = jnp.sum(low.astype(F32), axis=0, keepdims=True)

    def input_term(p, which):
        parts = []
        for at in range(3):
            columns = slice(at * HALF + p * 128, at * HALF + (p + 1) * 128)
            parts.append(wq_all[pl.ds(which * half, half), :, columns].reshape(HALF, 128))
        return dot(d_all[p], jnp.concatenate(parts, axis=1), NT)

    def far_term(p):
        far[...] = far[...] + input_term(p, 1 - r)

    def own_term(p):
        grad_out[...] = grad_out[...] + input_term(p, r)

    def grads(p):
        for which in range(2):
            term = dot(hid_t[which], d_all[p], NN).astype(BF16)
            for b in range(half):
                c = which * half + b
                gq[p, c % 2, (c // 2) % 2, c // 4] = term[b * blk : (b + 1) * blk]

    events = {}

    def add(step, what, *inputs):
        events.setdefault(step, []).append(functools.partial(what, *inputs))

    def start(step, what, *inputs):
        add(step, lambda: what(*inputs).start())

    bias_own[0, 2:8] = jnp.zeros((6, HALF), F32)
    add(0, g_core_add, 0, 1, 1)
    add(0, g_core_add, 1, 2, 0)
    start(1, gx, 1, 1)
    start(1, gy, 2, 1)
    add(1, g_core_add, 0, 3, 0)
    add(2, g_core_add, 0, 3, 1)
    late = [(1, 1, 0), (1, 1, 1), (0, 2, 1), (1, 2, 1), (0, 0, 0), (0, 0, 1), (1, 3, 0), (1, 3, 1)]
    for at, what in enumerate(late + [(1, 0, 0), (1, 0, 1)]):
        add(3 + at, g_core_add, *what)
    start(2, gx, 3, 0)
    add(5, vector_add, 1)
    start(5, vector, 2)
    add(7, gy_add, 2, 0)
    add(7, gx_add, 1, 0)
    add(7, gx_add, 1, 1)
    start(8, gy, 1, 1)
    add(8, gy_add, 2, 1)
    start(9, gx, 2, 1)
    start(9, gx, 3, 1)
    start(9, gx, 0, 0)
    start(10, gx, 0, 1)
    add(10, vector_add, 2)
    for step in range(1, n):
        start(10, vector, 2 + step)
    add(15, gy_add, 1, 1)
    start(15, gz, 1)
    add(17, gx_add, 2, 1)
    add(18, gx_add, 3, 0)
    add(18, gx_add, 3, 1)
    start(18, gy, 3, 1)
    start(22, gz, 2)
    for p in range(PAIRS):
        base = SPAN * p
        late = 7 if p == PAIRS - 1 else 8
        start(base + 2, core_send, p, 0)
        add(base + 3, core_add, p, 0)
        start(base + 3, hop, p, 0)
        start(base + 4, core_send, p, 1)
        add(base + 5, core_add, p, 1)
        start(base + 5, hop, p, 1)
        start(base + 6, core_send, p, 2)
        add(base + 7, core_add, p, 2)
        add(base + late, hop_add, p)
        start(base + late, hop, p, 2)
        start(base + 8, core_send, p, 3)
        if p < PAIRS - 1:
            add(base + 14, settle, p)
            add(base + 14, grads, p)
            start(base + 14, q_core, p)
            add(base + 15, far_term, p)
            add(base + 15, own_term, p)
            add(base + 15, q_core_add, p)
    add(23, gy_add, 3, 1)
    start(23, gz, 3)

    steps = SPAN * PAIRS

    def back(t, carry):
        p, i = lax.div(t, SPAN), lax.rem(t, SPAN)
        for step, calls in sorted(events.items()):
            if step < steps:

                @pl.when(t == step)
                def _(calls=calls):
                    with jax.named_scope(f"step_{step}"):
                        for call in calls:
                            call()

        slot = lax.rem(t, 2)

        @pl.when(t + 1 < steps)
        def _():
            p_load(t + 1, 1 - slot).start()

        @pl.when(p == 0)
        def _():
            kv_load(i).wait()

        p_load(t, slot).wait()
        where = b_block(i)
        key = kv[i, p]
        value = kv[i, PAIRS + p]
        key_t = key.T
        d_key = d_value = None
        for h in range(2):
            g = 2 * p + h
            factor = jnp.exp(m_in[where, g] - lse_in[g])
            d_rows = (dtot[g] * factor).astype(BF16)
            weights = pbuf[slot, h]
            d_probs = dot(value, d_rows, NN)
            d_scores = (weights.astype(F32) * (d_probs - delta[g] * factor)).astype(BF16)
            value_term = dot(weights, d_rows, NT)
            key_term = dot(d_scores, qm[g], NN)
            acc[g] += dot(key_t[h * HEAD_DIM : (h + 1) * HEAD_DIM], d_scores, NN)
            d_key = key_term if d_key is None else d_key + key_term
            d_value = value_term if d_value is None else d_value + value_term
        big[i, 2 * p] = d_key.astype(BF16)
        big[i, 2 * p + 1] = d_value.astype(BF16)
        return carry

    lax.fori_loop(0, steps, back, jnp.int32(0))

    last = PAIRS - 1
    for call in events[steps]:
        call()
    q_side(0).start()
    q_side(1).start()
    with jax.named_scope("settle"):
        settle(last)
    with jax.named_scope("far"):
        far_term(last)
        near[0] = far[...].astype(BF16)
    to_near = send(near.at[0], near.at[1], single, 3, place.to_x())
    with jax.named_scope("grads"):
        grads(last)
    to_near.start()
    q_core(last).start()
    sz = (s_send, s_recv)

    def small(number):
        level = min(number, 2)
        peer = (place.to_core(), place.to_y(), place.to_z(max(number - 1, 1)))[level]
        return send(bias_own.at[level], bias_got.at[number], sz, number, peer)

    small(0).start()
    with jax.named_scope("own"):
        own_term(last)
    with jax.named_scope("q_core"):
        q_core_add(last)
        small(0).wait_recv()
        bias_own[1] = bias_own[0] + bias_got[0]
    q_side(last).start()
    small(1).start()
    with jax.named_scope("g_x_0"):
        gx_add(0, 0)
        gx_add(0, 1)
    gy(0, 1).start()
    with jax.named_scope("q_side_0"):
        q_side_add(0)
        q_planes(0)
    with jax.named_scope("q_side_1"):
        q_side_add(1)
        q_planes(1)
    with jax.named_scope("q_side_2"):
        q_side_add(last)
        q_planes(last)
        small(1).wait_recv()
        bias_own[2] = bias_own[1] + bias_got[1]
    for step in range(1, n):
        small(1 + step).start()
    with jax.named_scope("vectors"):
        total = vec_sum[2]
        for step in range(1, n):
            vector(2 + step).wait_recv()
            total = total + vec_got[2 + step]
        small_out[...] = total

    def q_out(p):
        total = gq[p, j, y, place.z].astype(F32)
        for k in range(1, n):
            q_plane(p, k).wait_recv()
            total = total + q3[p, k - 1].astype(F32)
        lanes = slice(p * 128, (p + 1) * 128)
        query_out[:, lanes] = total[:, :128]
        key_out[:, lanes] = total[:, 128:256]
        value_out[:, lanes] = total[:, 256:]

    with jax.named_scope("q_out_0"):
        q_out(0)
    with jax.named_scope("near_wait"):
        to_near.wait_recv()
        grad_out[...] = grad_out[...] + near[1].astype(F32)
    with jax.named_scope("g_z"):
        total = None
        for k in range(1, n):
            gz(k).wait_recv()
            got = b4[k - 1].astype(F32)
            total = got if total is None else total + got
    with jax.named_scope("g_y_0"):
        gy_add(0, 1)
        total = total + st[index(1, 0, 1)].astype(F32)
        wo_out[...] = total[:, :HALF]
        wi_out[...] = total[:, HALF:FIRST]
        wu_out[...] = total[:, FIRST:]
    with jax.named_scope("q_out"):
        q_out(1)
        q_out(last)
        total = bias_own[2]
        for step in range(1, n):
            small(1 + step).wait_recv()
            total = total + bias_got[1 + step]
        bias_out[...] = total

    for at in range(4 * n):
        c_move(at).wait_send()
    for k in range(n):
        first = (2,) if k == 2 else ()
        for m in range(2):
            if not first or m == 1:
                gx(k, m).wait_send()
            if first or m == 1:
                gy(k, m).wait_send()
    for k in range(1, n):
        gz(k).wait_send()
        small(1 + k).wait_send()
        for p in range(PAIRS):
            q_plane(p, k).wait_send()
    small(0).wait_send()
    small(1).wait_send()
    for number in range(n + 2):
        vector(number).wait_send()
    for p in range(PAIRS):
        q_core(p).wait_send()
        q_side(p).wait_send()
        for pair in range(4):
            core_send(p, pair).wait_send()
        for pair in range(3):
            hop(p, pair).wait_send()
    to_near.wait_send()
    send(dctx.at[1 - r], d_ctx.at[own_rows], single, 0, place.to_x()).wait_send()


def backward_attention(
    size, dctx, qs, m_in, lse_in, ctxt, hid_all, wq_all, dres_low, dres_own, small_in, kv_in, p_in, g_in
):
    rows = qs.shape[1]
    part = rows // 2
    blk = wq_all.shape[1]
    n = size // 4
    any_space = pl.BlockSpec(memory_space=pl.ANY)
    vmem = pl.BlockSpec(memory_space=pltpu.VMEM)
    shape = jax.ShapeDtypeStruct
    dma = pltpu.SemaphoreType.DMA
    scratch = pltpu.VMEM
    g_count, q_count = 4 * n + 2 * n + 2 * n + n - 1, PAIRS * (n + 1)
    return pl.pallas_call(
        functools.partial(kernel_c, size),
        out_shape=(
            shape((blk, HALF), F32),
            shape((blk, HALF), F32),
            shape((blk, HALF), F32),
            shape((blk, HALF), F32),
            shape((blk, FF_HALF), F32),
            shape((blk, FF_HALF), F32),
            shape((16, D), F32),
            shape((8, HALF), F32),
            shape((rows, HALF), F32),
        ),
        in_specs=[vmem] * 10 + [any_space] * 3,
        out_specs=[vmem] * 9,
        scratch_shapes=[
            scratch((rows, HALF), BF16),
            scratch((2 * PAIRS, 128, rows), F32),
            scratch((2 * PAIRS, 1, rows), F32),
            scratch((2 * PAIRS, rows, 128), BF16),
            scratch((2 * PAIRS, HEAD_DIM, rows), F32),
            scratch((SPAN, 2 * PAIRS, rows, 128), BF16),
            scratch((2, 2, rows, rows), BF16),
            scratch((SPAN, 2 * PAIRS, rows, 128), BF16),
            scratch((4, 2 * PAIRS, rows, 128), BF16),
            scratch((3, 2 * PAIRS, rows, 128), BF16),
            scratch((4 * n, blk, REST), BF16),
            scratch((4 * n, blk, REST), BF16),
            scratch((2 * n, blk, REST), BF16),
            scratch((2 * n, blk, REST), BF16),
            scratch((n - 1, blk, REST), BF16),
            scratch((PAIRS, rows, HALF), BF16),
            scratch((2, HALF, rows), BF16),
            scratch((rows, HALF), F32),
            scratch((PAIRS, 2, 2, n, blk, HALF), BF16),
            scratch((PAIRS, 2, n, blk, HALF), BF16),
            scratch((PAIRS, n, blk, HALF), BF16),
            scratch((PAIRS, n - 1, blk, HALF), BF16),
            scratch((2, rows, HALF), BF16),
            scratch((3, 8, HALF), F32),
            scratch((n + 1, 8, HALF), F32),
            scratch((3, 16, D), F32),
            scratch((n + 2, 16, D), F32),
            dma((4,)),
            dma((4,)),
            dma((7 * PAIRS,)),
            dma((7 * PAIRS,)),
            dma((g_count,)),
            dma((g_count,)),
            dma((q_count,)),
            dma((q_count,)),
            dma((n + 1,)),
            dma((n + 1,)),
            dma((n + 2,)),
            dma((n + 2,)),
            dma((9 + 4 * n,)),
            dma((2,)),
        ],
        compiler_params=pltpu.CompilerParams(
            collective_id=1, has_side_effects=True, vmem_limit_bytes=63 * 2**20
        ),
        name="backward_attention",
    )(dctx, qs, m_in, lse_in, ctxt, hid_all, wq_all, dres_low, dres_own, small_in, kv_in, p_in, g_in)


def kernel_d(size, per, count, *refs):
    sources, targets = refs[:count], refs[count : 2 * count - 1]
    held, tile, come, go = refs[2 * count - 1 : 3 * count - 1], refs[-3], refs[-2], refs[-1]
    small, bias = held[0], held[1]
    loads = [pltpu.make_async_copy(s, h, come.at[at]) for at, (s, h) in enumerate(zip(sources, held))]
    done = list(held[2:]) + [tile]
    stores = [pltpu.make_async_copy(h, t, go.at[at]) for at, (h, t) in enumerate(zip(done, targets))]
    for copy in loads:
        copy.start()
    loads[0].wait()
    loads[1].wait()
    row = lax.axis_index("row")
    inside = lax.rem(lax.axis_index("col"), size)
    start = row * HALF + inside * per
    lines = small[...]
    tile[0:6] = pltpu.roll(lines, D - start, 1)[0:6, :128]
    spot = inside * 4 * per
    hidden = pltpu.roll(lines, D - lax.rem(spot, D), 1)[:, :128]
    wanted = 6 + 2 * row + lax.div(spot, D)
    line = lax.broadcasted_iota(jnp.int32, hidden.shape, 0)
    tile[6:7] = jnp.sum(jnp.where(line == wanted, hidden, 0.0), axis=0, keepdims=True)
    tile[7:9] = pltpu.roll(bias[...], HALF - inside * per, 1)[0:2, :128]
    tile[9:16] = jnp.zeros((7, 128), F32)
    stores[-1].start()
    for load, store in zip(loads[2:], stores):
        load.wait()
        store.start()
    for store in stores:
        store.wait()


def finish(size, small, bias, arrays):
    space = pl.BlockSpec(memory_space=pl.ANY)
    shapes = [jax.ShapeDtypeStruct(a.shape, a.dtype) for a in arrays]
    arrays = [small, bias] + arrays
    count = len(arrays)
    return pl.pallas_call(
        functools.partial(kernel_d, size, HALF // size, count),
        out_shape=shapes + [jax.ShapeDtypeStruct((16, 128), F32)],
        in_specs=[space] * count,
        out_specs=[space] * (count - 1),
        scratch_shapes=[pltpu.VMEM(a.shape, a.dtype) for a in arrays]
        + [pltpu.VMEM((16, 128), F32)]
        + [pltpu.SemaphoreType.DMA((count,))] * 2,
        compiler_params=pltpu.CompilerParams(vmem_limit_bytes=63 * 2**20),
        name="finish",
    )(*arrays)


def per_device(group, hidden_in, cotangent, lengths, *params):
    w_query, w_key, w_value, w_output, w_inner, w_outer = params[:6]
    b_query, b_value, b_output, b_inner, b_outer = params[6:11]
    gain_one, shift_one, gain_two, shift_two = params[11:]
    cols = lax.axis_size("col")
    size = group
    ways = cols // size
    inside = lax.axis_index("col") % size
    row = lax.axis_index("row")

    def regroup(block):
        if ways == 1:
            return block
        whole = lax.all_gather(block, "col", axis=0, tiled=True)
        count = block.shape[0] * ways
        return lax.dynamic_slice_in_dim(whole, inside * count, count, axis=0)

    vec = jnp.zeros((16, 128), BF16)
    vectors = (b_query, b_value, b_output, b_outer, gain_one, shift_one, gain_two, shift_two)
    for at, vector in enumerate(vectors + (b_inner,)):
        line = regroup(vector)
        vec += jnp.pad(line[None, :], ((at, 15 - at), (0, 128 - line.shape[0])))
    qkv_weights = [regroup(w) for w in (w_query, w_key, w_value)]
    rest_weights = [regroup(w) for w in (w_output.T, w_inner, w_outer.T)]
    (hid_all, wq_all, qs, kv, probs, m_all, lse, ctxt, g_parts, layer_out, low, own, d_context, small) = (
        forward_attention(size, lengths, hidden_in, qkv_weights, rest_weights, vec, cotangent)
    )
    (g_query, g_key, g_value, g_output, g_inner, g_outer, g_small, g_bias, grad_in) = (
        backward_attention(
            size,
            d_context,
            qs,
            m_all,
            lse,
            ctxt,
            hid_all,
            wq_all,
            low,
            own,
            small,
            kv,
            probs,
            g_parts,
        )
    )

    def spread(block):
        if ways == 1:
            return block
        count = block.shape[0]
        whole = jnp.zeros((count * size,) + block.shape[1:], block.dtype)
        whole = lax.dynamic_update_slice_in_dim(whole, block, inside * count, axis=0)
        return lax.psum_scatter(whole, "col", scatter_dimension=0, tiled=True)

    arrays = [g_query, g_key, g_value, g_output, g_inner, g_outer, grad_in, layer_out]
    *arrays, tile = finish(size, g_small, g_bias, arrays)
    g_query, g_key, g_value, g_output, g_inner, g_outer, grad_in, layer_out = arrays
    per = HALF // size
    pieces = [spread(tile[at, : 4 * per if at == 6 else per]) for at in range(9)]
    g_b_output, g_b_outer, g_gain_one, g_shift_one, g_gain_two, g_shift_two = pieces[:6]
    g_b_inner, g_b_query, g_b_value = pieces[6:]
    return (
        layer_out,
        grad_in,
        spread(g_query),
        spread(g_key),
        spread(g_value),
        spread(g_output).T,
        spread(g_inner),
        spread(g_outer).T,
        g_b_query,
        g_b_value,
        g_b_output,
        g_b_inner,
        g_b_outer,
        g_gain_one,
        g_shift_one,
        g_gain_two,
        g_shift_two,
    )


def solution(mesh):
    cols = mesh.shape["col"]
    group = max(s for s in range(SPAN, cols + 1, 4) if cols % s == 0 and D // s % 16 == 0)
    token, weight, turned = P("col", "row"), P("col", "row"), P("row", "col")
    vector = P(("row", "col"))
    return jax.shard_map(
        functools.partial(per_device, group),
        mesh=mesh,
        in_specs=(token, token, P()) + (weight,) * 3 + (turned, weight, turned) + (vector,) * 9,
        out_specs=(token, token) + (weight,) * 3 + (turned, weight, turned) + (vector,) * 9,
        check_vma=False,
    )
```

```python
import functools

import jax
import jax.numpy as jnp
from jax import lax
from jax.experimental import pallas as pl
from jax.experimental.pallas import tpu as pltpu
from jax.sharding import PartitionSpec as P

D = 768
HALF = 384
HEAD_DIM = 64
FF_HALF = 1536
PAIRS = 3
SPAN = 8
EPSILON = 1e-12
MASKED = -1e30
MESH = pl.DeviceIdType.MESH
F32 = jnp.float32
BF16 = jnp.bfloat16
FIRST = HALF + FF_HALF
REST = HALF + 2 * FF_HALF
QKV = 3 * HALF


def dot(left, right, contract):
    return lax.dot_general(left, right, (contract, ((), ())), preferred_element_type=F32)


NN = ((1,), (0,))
NT = ((1,), (1,))
TN = ((0,), (0,))


class Place:
    def __init__(self, size):
        self.size = size
        self.planes = size // 4
        self.r = lax.axis_index("row")
        col = lax.axis_index("col")
        self.base = lax.div(col, size) * size
        inner = lax.rem(col, size)
        self.slot = lax.div(col, SPAN)
        self.block = lax.rem(col, SPAN)
        self.z = lax.div(inner, 4)
        self.y = lax.rem(lax.div(inner, 2), 2)
        self.j = lax.rem(inner, 2)
        self.zl = lax.rem(self.z, 2)

    def plane(self, step):
        return lax.rem(self.z + step + self.planes, self.planes)

    def device(self, r, z, y, j):
        return (r, self.base + z * 4 + y * 2 + j)

    def to_z(self, step):
        return self.device(self.r, self.plane(step), self.y, self.j)

    def to_z_near(self):
        return self.device(self.r, self.z - self.zl + (1 - self.zl), self.y, self.j)

    def to_y(self):
        return self.device(self.r, self.z, 1 - self.y, self.j)

    def to_x(self):
        return self.device(1 - self.r, self.z, self.y, self.j)

    def to_core(self):
        return self.device(self.r, self.z, self.y, 1 - self.j)

    def col_block(self, z, y, j):
        return z * 4 + y * 2 + j

    def any_block(self, r, z, y, j):
        return r * self.size + z * 4 + y * 2 + j

    def near_block(self, dz, dy, j):
        return lax.rem(self.zl + dz, 2) * 4 + lax.rem(self.y + dy, 2) * 2 + j


def meet(place):
    barrier = pltpu.get_barrier_semaphore()
    peers = [place.to_z(step) for step in range(1, place.planes)]
    peers += [place.to_y(), place.to_x(), place.to_core()]
    for peer in peers:
        pl.semaphore_signal(barrier, inc=1, device_id=peer, device_id_type=MESH)
    pl.semaphore_wait(barrier, len(peers))


def send(src, dst, sems, index, peer):
    return pltpu.make_async_remote_copy(
        src_ref=src,
        dst_ref=dst,
        send_sem=sems[0].at[index],
        recv_sem=sems[1].at[index],
        device_id=peer,
        device_id_type=MESH,
    )


class Gather:
    def __init__(self, place, own, full, sems, with_rows):
        self.place, self.own, self.full, self.sems = place, own, full, sems
        self.rows = 2 if with_rows else 1
        self.with_rows = with_rows
        n = place.planes
        self.at_y = n - 1
        self.at_x = self.at_y + n
        self.at_c = self.at_x + (2 * n if with_rows else 0)
        self.total = self.at_c + 2 * n * self.rows

    def index(self, n, k, m, j):
        p = self.place
        z, y = p.plane(-k), lax.rem(p.y + m, 2)
        if self.with_rows:
            return p.any_block(lax.rem(p.r + n, 2), z, y, j)
        return p.col_block(z, y, j)

    def move(self, number, peer, n, k, m, j, local):
        where = self.index(n, k, m, j)
        src = self.own if local else self.full.at[where]
        return send(src, self.full.at[where], self.sems, number, peer)

    def z_sends(self):
        p = self.place
        for step in range(1, p.planes):
            self.move(step - 1, p.to_z(step), 0, 0, 0, p.j, True).start()

    def z_done(self, k):
        p = self.place
        self.move(k - 1, p.to_z(k), 0, k, 0, p.j, False).wait_recv()

    def y_send(self, k):
        p = self.place
        self.move(self.at_y + k, p.to_y(), 0, k, 0, p.j, k == 0).start()

    def y_done(self, k):
        p = self.place
        self.move(self.at_y + k, p.to_y(), 0, k, 1, p.j, False).wait_recv()

    def x_send(self, k, m):
        p = self.place
        self.move(self.at_x + 2 * k + m, p.to_x(), 0, k, m, p.j, k + m == 0).start()

    def x_done(self, k, m):
        p = self.place
        self.move(self.at_x + 2 * k + m, p.to_x(), 1, k, m, p.j, False).wait_recv()

    def c_number(self, n, k, m):
        return self.at_c + (2 * k + m) * self.rows + n

    def c_send(self, n, k, m):
        p = self.place
        number = self.c_number(n, k, m)
        self.move(number, p.to_core(), n, k, m, p.j, n + k + m == 0).start()

    def c_done(self, n, k, m):
        p = self.place
        self.move(self.c_number(n, k, m), p.to_core(), n, k, m, 1 - p.j, False).wait_recv()

    def all_sent(self):
        for number in range(self.total):
            send(self.own, self.own, self.sems, number, self.place.to_core()).wait_send()


def spread_rows(tiles, picks, per, width):
    blocks = tiles.shape[0]
    flat = tiles.reshape(blocks * 16, 128)
    total = len(picks) * blocks
    line = lax.broadcasted_iota(jnp.int32, (total, blocks * 16), 0)
    at = lax.broadcasted_iota(jnp.int32, (total, blocks * 16), 1)
    wanted = jnp.zeros((total, blocks * 16), F32)
    for spot, pick in enumerate(picks):
        hit = at == (line - spot * blocks) * 16 + pick
        inside = (line >= spot * blocks) & (line < (spot + 1) * blocks)
        wanted = jnp.where(hit & inside, 1.0, wanted)
    taken = dot(wanted.astype(BF16), flat, NN).astype(BF16)
    lane = lax.broadcasted_iota(jnp.int32, (128, width), 1).astype(F32)
    group = jnp.floor((lane + 0.5) * (1.0 / per))
    place = lax.broadcasted_iota(jnp.int32, (128, width), 0).astype(F32)
    copies = jnp.where(lane - group * per == place, 1.0, 0.0).astype(BF16)
    wide = dot(taken, copies, NN)
    first = lax.broadcasted_iota(jnp.int32, (blocks, width), 0) * per
    column = lax.broadcasted_iota(jnp.int32, (blocks, width), 1)
    mask = (column >= first) & (column < first + per)
    rows = []
    for spot in range(len(picks)):
        part = jnp.where(mask, wide[spot * blocks : (spot + 1) * blocks], 0.0)
        rows.append(jnp.sum(part, axis=0, keepdims=True))
    return rows


def gelu_both(argument):
    spread = 1.0 + lax.erf(argument * 0.7071067811865476)
    bell = jnp.exp(argument * argument * -0.5) * 0.3989422804014327
    return 0.5 * argument * spread, 0.5 * spread + argument * bell


def norm_forward(resid, gain, shift):
    center = resid - jnp.mean(resid, axis=1, keepdims=True)
    scale = lax.rsqrt(jnp.mean(center * center, axis=1, keepdims=True) + EPSILON)
    normal = center * scale
    return normal * gain + shift, normal, scale


def norm_backward(incoming, normal, scale, gain):
    scaled = incoming * gain
    first = jnp.mean(scaled, axis=1, keepdims=True)
    second = jnp.mean(scaled * normal, axis=1, keepdims=True)
    result = scale * (scaled - first - normal * second)
    sums = jnp.sum(incoming * normal, axis=0, keepdims=True)
    return result, sums, jnp.sum(incoming, axis=0, keepdims=True)


def kernel_a(
    size,
    lengths,
    hid,
    w_query,
    w_key,
    w_value,
    w_output,
    w_inner,
    w_outer,
    vec_in,
    cot,
    hid_out,
    wq_out,
    q_out,
    kv_out,
    p_out,
    m_out,
    lse_out,
    ctxt_out,
    g_out,
    final_out,
    low_out,
    own_out,
    d_out,
    small_out,
    hid_all,
    wq_own,
    wq_all,
    vec_all,
    one_own,
    one_all,
    two_all,
    kv,
    qs,
    qm,
    acc,
    high,
    low,
    pbuf,
    ctx_tp,
    ctx_in,
    cot_in,
    lay_out,
    lay_far,
    normed_ref,
    normal_ref,
    low_ref,
    slope_ref,
    act_ref,
    d_ref,
    one_send,
    one_recv,
    two_send,
    two_recv,
    wq_send,
    wq_recv,
    vec_send,
    vec_recv,
    kv_send,
    kv_recv,
    lone_send,
    lone_recv,
    local,
    p_sem,
):
    place = Place(size)
    rows = hid.shape[0]
    part = rows // 2
    n = place.planes
    r, y, j = place.r, place.y, place.j
    blk = w_query.shape[0]
    for at, source in enumerate((w_query, w_key, w_value)):
        wq_own[:, at * HALF : (at + 1) * HALF] = source[...]
    one_own[:, :HALF] = w_output[...]
    one_own[:, HALF:] = w_inner[...]
    with jax.named_scope("meet"):
        meet(place)

    single = (lone_send, lone_recv)
    own_rows = pl.ds(pl.multiple_of(r * part, part), part)
    other_rows = pl.ds(pl.multiple_of((1 - r) * part, part), part)
    to_hid = send(hid, hid_all.at[r], single, 0, place.to_x())
    to_hid.start()
    vec = Gather(place, vec_in, vec_all, (vec_send, vec_recv), True)
    wq = Gather(place, wq_own, wq_all, (wq_send, wq_recv), False)
    one = Gather(place, one_own, one_all, (one_send, one_recv), True)
    two = Gather(place, w_outer, two_all, (two_send, two_recv), True)
    for gather in (vec, wq):
        gather.z_sends()
        gather.y_send(0)
        gather.c_send(0, 0, 0)
    vec.x_send(0, 0)
    one.x_send(0, 0)
    one.y_send(0)
    two.x_send(0, 0)
    to_cot = send(cot.at[other_rows], cot_in.at[r], single, 1, place.to_x())
    to_cot.start()
    one.c_send(0, 0, 0)
    two.c_send(0, 0, 0)
    hid_all[r] = hid[...]
    mine = place.any_block(r, place.z, y, j)
    wq_all[place.col_block(place.z, y, j)] = wq_own[...]
    vec_all[mine] = vec_in[...]
    one_all[mine] = one_own[...]
    two_all[mine] = w_outer[...]
    cot_in[r] = cot[own_rows, :]
    for k in range(1, n):
        with jax.named_scope(f"qkv_plane_{k}"):
            for gather in (vec, wq):
                gather.z_done(k)
                gather.y_send(k)
                gather.c_send(0, k, 0)
            vec.x_send(k, 0)
    one.z_sends()
    two.y_send(0)
    for k in range(n):
        with jax.named_scope(f"qkv_side_{k}"):
            for gather in (vec, wq):
                gather.y_done(k)
                gather.c_send(0, k, 1)
            vec.x_send(k, 1)
    with jax.named_scope("qkv_core"):
        for k in range(n):
            for m in range(2):
                for gather in (vec, wq):
                    gather.c_done(0, k, m)
    with jax.named_scope("hidden"):
        send(hid, hid_all.at[1 - r], single, 0, place.to_x()).wait_recv()

    def rest_y(gather, k):
        gather.z_done(k)
        gather.y_send(k)
        gather.x_send(k, 0)
        gather.c_send(0, k, 0)

    def rest_x(gather, k):
        gather.y_done(k)
        gather.x_send(k, 1)
        gather.c_send(0, k, 1)

    def rest_c(gather, k, m):
        gather.x_done(k, m)
        gather.c_send(1, k, m)

    def rest_all(gather):
        for n_at in range(2):
            for k in range(n):
                for m in range(2):
                    if gather is not vec or n_at:
                        gather.c_done(n_at, k, m)

    hid_local = pltpu.make_async_copy(hid_all, hid_out, local.at[2])
    hid_local.start()
    wq_local = pltpu.make_async_copy(wq_all, wq_out, local.at[3])
    wq_local.start()

    kvs = (kv_send, kv_recv)

    def kv_block(i):
        pair, core = lax.div(i, 2), lax.rem(j + lax.rem(i, 2), 2)
        return place.near_block(lax.div(pair, 2), lax.rem(pair, 2), core)

    def kv_move(number, p):
        what = (0, 0, 0, 2, 0, 4, 2, 6)[number]
        if number % 2:
            peer = place.to_core()
        else:
            peer = place.to_y() if number == 2 else place.to_z_near()
        where = kv_block(jnp.int32(what))
        block = kv.at[where, pl.ds(2 * p, 2)]
        return send(block, block, kvs, SPAN * p + number, peer)

    def kv_start(number, p):
        kv_move(number, p).start()

    def kv_here(number, p):
        where = kv_block(jnp.int32(number))
        block = kv.at[where, pl.ds(2 * p, 2)]
        send(block, block, kvs, SPAN * p + number, place.to_core()).wait_recv()

    own_tiles = vec_all[pl.ds(r * size, size)]
    b_query, b_value = spread_rows(own_tiles, (0, 1), HALF // size, HALF)
    own = place.near_block(0, 0, j)
    half = size // 2
    for which in (1, 2, 0):
        columns = slice(which * HALF, (which + 1) * HALF)
        total = dot(hid_all[0], wq_all[:half, :, columns].reshape(HALF, HALF), NN)
        total += dot(hid_all[1], wq_all[half:, :, columns].reshape(HALF, HALF), NN)
        if which == 0:
            total += b_query
        if which == 2:
            total += b_value
        total = total.astype(BF16)
        for p in range(PAIRS):
            piece = total[:, p * 128 : (p + 1) * 128]
            if which == 0:
                lane = lax.broadcasted_iota(jnp.int32, (rows, 128), 1)
                piece = piece * jnp.asarray(0.125, BF16)
                qs[p] = piece
                qm[2 * p] = jnp.where(lane < HEAD_DIM, piece, jnp.zeros_like(piece))
                qm[2 * p + 1] = jnp.where(lane >= HEAD_DIM, piece, jnp.zeros_like(piece))
            else:
                kv[own, 2 * p + which - 1] = piece
        if which == 1:
            with jax.named_scope("after_key"):
                rest_x(one, 0)
        if which == 2:
            with jax.named_scope("after_value"):
                for number in (2, 4, 1):
                    kv_start(number, 0)
                rest_y(one, 1)
    acc[...] = jnp.zeros_like(acc)
    high[...] = jnp.full_like(high, MASKED)
    low[...] = jnp.zeros_like(low)

    q_local = pltpu.make_async_copy(qs, q_out, local.at[4])
    q_local.start()

    def vec_rows():
        for k in range(n):
            for m in range(2):
                rest_c(vec, k, m)

    def two_start():
        two.z_sends()

    events = {}

    def add(step, what, *inputs):
        events.setdefault(step, []).append(functools.partial(what, *inputs))

    add(1, kv_here, 1, 0)
    add(1, vec_rows)
    add(2, rest_x, one, 1)
    add(2, kv_here, 2, 0)
    add(2, kv_start, 3, 0)
    add(2, kv_start, 6, 0)
    add(3, kv_here, 3, 0)
    add(3, rest_y, one, 2)
    add(4, kv_here, 4, 0)
    add(4, kv_start, 5, 0)
    add(4, rest_y, one, 3)
    add(5, kv_here, 5, 0)
    add(5, two_start)
    add(5, kv_start, 2, 1)
    add(5, kv_start, 4, 1)
    add(5, kv_start, 1, 1)
    add(6, kv_here, 6, 0)
    add(6, kv_start, 7, 0)
    add(6, rest_x, two, 0)
    add(7, kv_here, 7, 0)
    add(7, rest_x, one, 2)
    add(8, rest_x, one, 3)
    add(8, rest_c, one, 0, 0)
    add(9, kv_here, 1, 1)
    add(9, rest_c, one, 1, 0)
    add(10, kv_here, 2, 1)
    add(10, kv_start, 3, 1)
    add(10, kv_start, 6, 1)
    add(11, kv_here, 3, 1)
    add(11, rest_y, two, 1)
    add(11, kv_start, 2, 2)
    add(11, kv_start, 4, 2)
    add(11, kv_start, 1, 2)
    add(12, kv_here, 4, 1)
    add(12, kv_start, 5, 1)
    add(13, kv_here, 5, 1)
    add(13, rest_c, one, 0, 1)
    add(13, rest_c, one, 1, 1)
    add(13, rest_y, two, 2)
    add(14, kv_here, 6, 1)
    add(14, kv_start, 7, 1)
    add(14, rest_x, two, 1)
    add(15, kv_here, 7, 1)
    add(15, rest_y, two, 3)
    add(16, rest_c, one, 2, 0)
    add(17, kv_here, 1, 2)
    add(17, rest_c, one, 3, 0)
    add(17, rest_x, two, 2)
    add(18, kv_here, 2, 2)
    add(18, kv_start, 3, 2)
    add(18, kv_start, 6, 2)
    add(19, kv_here, 3, 2)
    add(19, rest_c, one, 2, 1)
    add(20, kv_here, 4, 2)
    add(20, kv_start, 5, 2)
    add(20, rest_x, two, 3)
    add(21, kv_here, 5, 2)
    add(21, rest_c, one, 3, 1)
    add(22, kv_here, 6, 2)
    add(22, kv_start, 7, 2)
    add(22, rest_c, two, 0, 0)
    add(23, kv_here, 7, 2)
    add(23, rest_c, two, 0, 1)

    length = lengths[place.slot]

    def p_copy(t, slot):
        p, i = lax.div(t, SPAN), lax.rem(t, SPAN)
        return pltpu.make_async_copy(
            pbuf.at[slot], p_out.at[kv_block(i), pl.ds(2 * p, 2)], p_sem.at[slot]
        )

    def kv_copy(t):
        p, i = lax.div(t, SPAN), lax.rem(t, SPAN)
        where, both = kv_block(i), pl.ds(2 * p, 2)
        return pltpu.make_async_copy(
            kv.at[where, both], kv_out.at[where, both], local.at[8 + t]
        )

    steps = SPAN * PAIRS
    column = lax.broadcasted_iota(jnp.int32, (1, rows), 1) + place.block * rows
    keep_row = jnp.where(column < length, 1.0, 0.0)

    def to_ctx(p):
        lanes = pl.ds(p * 128, 128)
        return send(
            ctx_tp.at[other_rows, lanes], ctx_in.at[r, :, lanes], single, (2, 5, 6)[p], place.to_x()
        )

    def context(p):
        parts = []
        for h in range(2):
            g = 2 * p + h
            lse_out[g] = high[g] + jnp.log(low[g])
            parts.append(acc[g] / low[g])
        both = jnp.concatenate(parts, axis=0)
        ctxt_out[p] = both
        ctx_tp[:, p * 128 : (p + 1) * 128] = (both * keep_row).T.astype(BF16)
        to_ctx(p).start()
        ctx_in[r, :, p * 128 : (p + 1) * 128] = ctx_tp[own_rows, p * 128 : (p + 1) * 128]

    for p in range(PAIRS - 1):
        add(SPAN * (p + 1), context, p)

    def attend(t, carry):
        p, i = lax.div(t, SPAN), lax.rem(t, SPAN)
        for step, calls in sorted(events.items()):

            @pl.when(t == step)
            def _(calls=calls):
                for call in calls:
                    with jax.named_scope(f"at_{step}"):
                        call()

        kv_copy(t).start()

        slot = lax.rem(t, 2)

        @pl.when(t >= 2)
        def _():
            p_copy(t - 2, slot).wait()

        where = kv_block(i)
        place_of = lax.broadcasted_iota(jnp.int32, (rows, 128), 0) + where * rows
        bias = jnp.where(place_of < length, 0.0, MASKED)
        bias = jnp.concatenate([bias] * (rows // 128), axis=1)
        key = kv[where, 2 * p]
        value_t = kv[where, 2 * p + 1].T
        for h in range(2):
            g = 2 * p + h
            scores = dot(key, qm[g], NT) + bias
            top = jnp.max(scores, axis=0, keepdims=True)
            weights = jnp.exp(scores - top)
            below = jnp.sum(weights, axis=0, keepdims=True)
            rounded = weights.astype(BF16)
            pbuf[slot, h] = rounded
            term = dot(value_t[h * HEAD_DIM : (h + 1) * HEAD_DIM], rounded, NN)
            old = high[g]
            new = jnp.maximum(old, top)
            keep_old, keep_new = jnp.exp(old - new), jnp.exp(top - new)
            high[g] = new
            low[g] = low[g] * keep_old + below * keep_new
            acc[g] = acc[g] * keep_old + term * keep_new
            m_out[where, g] = top
        p_copy(t, slot).start()
        return carry

    lax.fori_loop(0, steps, attend, jnp.int32(0))

    context(PAIRS - 1)
    for t in (steps - 2, steps - 1):
        p_copy(jnp.int32(t), t % 2).wait()
    with jax.named_scope("one_all"):
        rest_all(vec)
        rest_all(one)
    six = spread_rows(vec_all[...], (2, 3, 4, 5, 6, 7), HALF // size, D)
    b_output, b_outer, gain_one, shift_one, gain_two, shift_two = six
    (b_inner,) = spread_rows(vec_all[...], (8,), FF_HALF // size, 2 * FF_HALF)
    hidden = jnp.concatenate([hid_all[0, own_rows, :], hid_all[1, own_rows, :]], axis=1)
    with jax.named_scope("context"):
        for p in range(PAIRS):
            lanes = pl.ds(p * 128, 128)
            send(
                ctx_tp.at[other_rows, lanes], ctx_in.at[1 - r, :, lanes], single, (2, 5, 6)[p], place.to_x()
            ).wait_recv()

    def weight(ref, h, columns):
        block = ref[h * size : (h + 1) * size, :, columns]
        return block.reshape(D, block.shape[2])

    out_cols, in_cols, all_cols = slice(0, HALF), slice(HALF, FIRST), slice(0, FF_HALF)
    with jax.named_scope("middle_one"):
        attn = dot(ctx_in[0], weight(one_all, 0, out_cols), NT)
        attn += dot(ctx_in[1], weight(one_all, 1, out_cols), NT) + b_output
        normed, normal, scale_one = norm_forward(hidden.astype(F32) + attn, gain_one, shift_one)
        normed_ref[...] = normed
        normal_ref[...] = normal
        low_ref[...] = normed.astype(BF16)
    with jax.named_scope("two_late"):
        rest_c(two, 1, 0)
        rest_c(two, 1, 1)
    for h in range(2):
        with jax.named_scope(f"inner_{h}"):
            span = slice(h * FF_HALF, (h + 1) * FF_HALF)
            inner = dot(low_ref[...], weight(one_all, h, in_cols), NN) + b_inner[:, span]
            value, slope = gelu_both(inner)
            act_ref[:, span] = value.astype(BF16)
            slope_ref[:, span] = slope
    with jax.named_scope("two_all"):
        for k in range(2, n):
            for m in range(2):
                rest_c(two, k, m)
        rest_all(two)
    with jax.named_scope("outer"):
        outer = dot(act_ref[:, :FF_HALF], weight(two_all, 0, all_cols), NT)
        outer += dot(act_ref[:, FF_HALF:], weight(two_all, 1, all_cols), NT) + b_outer
        result, normal_two, scale_two = norm_forward(normed_ref[...] + outer, gain_two, shift_two)
        lay_out[0] = result[:, :HALF].astype(BF16)
        lay_out[1] = result[:, HALF:].astype(BF16)
    to_lay = send(lay_out.at[1 - r], lay_far.at[r], single, 3, place.to_x())
    to_lay.start()
    spot = lax.broadcasted_iota(jnp.int32, (part, 1), 0) + place.block * rows + r * part
    keep = jnp.where(spot < length, 1.0, 0.0)
    with jax.named_scope("cotangent"):
        send(cot.at[other_rows], cot_in.at[1 - r], single, 1, place.to_x()).wait_recv()
    with jax.named_scope("norm_two"):
        seed = jnp.concatenate([cot_in[0], cot_in[1]], axis=1).astype(F32) * keep
        d_two, g_gain_two, g_shift_two = norm_backward(seed, normal_two, scale_two, gain_two)
        d_outer = d_two.astype(BF16)
        small_out[4:5] = g_gain_two
        small_out[5:6] = g_shift_two
        small_out[1:2] = jnp.sum(d_outer.astype(F32), axis=0, keepdims=True)
    d_normed = d_two
    d_outer_t = d_outer.T
    for h in range(2):
        with jax.named_scope(f"d_inner_{h}"):
            span = slice(h * FF_HALF, (h + 1) * FF_HALF)
            d_inner = dot(d_outer, weight(two_all, h, all_cols), NN) * slope_ref[:, span]
            d_inner = d_inner.astype(BF16)
            d_ref[:, span] = d_inner
            sums = jnp.sum(d_inner.astype(F32), axis=0, keepdims=True)
            small_out[6 + 2 * h : 7 + 2 * h] = sums[:, :D]
            small_out[7 + 2 * h : 8 + 2 * h] = sums[:, D:]
            d_normed += dot(d_inner, weight(one_all, h, in_cols), NT)
    with jax.named_scope("all_sent"):
        for gather in (vec, wq, one, two):
            gather.all_sent()
    own_col = pl.ds(pl.multiple_of(r * HALF, HALF), HALF)

    def give(number, ref, h, columns, target):
        return pltpu.make_async_copy(
            ref.at[pl.ds(h * size, size), :, columns],
            g_out.at[pl.ds(h * size, size), :, target],
            local.at[8 + SPAN * PAIRS + number],
        )

    gives = []
    for h in range(2):
        with jax.named_scope(f"g_outer_{h}"):
            span = slice(h * FF_HALF, (h + 1) * FF_HALF)
            term = dot(d_outer_t, act_ref[:, span], NN).astype(BF16)
            two_all[h * size : (h + 1) * size] = term.reshape(size, blk, FF_HALF)
            copy = give(h, two_all, h, pl.ds(0, FF_HALF), pl.ds(FIRST, FF_HALF))
            copy.start()
            gives.append(copy)
    with jax.named_scope("norm_one"):
        d_one, g_gain_one, g_shift_one = norm_backward(d_normed, normal_ref[...], scale_one, gain_one)
        d_attn = d_one.astype(BF16)
        small_out[2:3] = g_gain_one
        small_out[3:4] = g_shift_one
        small_out[0:1] = jnp.sum(d_attn.astype(F32), axis=0, keepdims=True)
        small_out[10:16] = jnp.zeros((6, D), F32)
        for h in range(2):
            low_out[h] = d_attn[:, h * HALF : (h + 1) * HALF]
        normed_ref[...] = d_one
        own_out[...] = normed_ref[:, own_col]
    with jax.named_scope("d_context"):
        to_lay.wait_send()
        final_out[own_rows, :] = lay_out[r]
        for h in range(2):
            d_context = dot(d_attn, weight(one_all, h, out_cols), NN) * keep
            lay_out[h] = d_context.astype(BF16)
        to_d = send(lay_out.at[1 - r], d_out.at[own_rows], single, 4, place.to_x())
        to_d.start()
        d_out[own_rows, :] = lay_out[r]
    low_t = low_ref[...].T
    d_attn_t = d_attn.T
    for h in range(2):
        with jax.named_scope(f"g_inner_{h}"):
            span = slice(h * FF_HALF, (h + 1) * FF_HALF)
            term = dot(low_t, d_ref[:, span], NN).astype(BF16)
            one_all[h * size : (h + 1) * size, :, HALF:] = term.reshape(size, blk, FF_HALF)
            term = dot(d_attn_t, ctx_in[h], NN).astype(BF16)
            one_all[h * size : (h + 1) * size, :, :HALF] = term.reshape(size, blk, HALF)
            copy = give(2 + h, one_all, h, pl.ds(0, FIRST), pl.ds(0, FIRST))
            copy.start()
            gives.append(copy)
    for number in range(1, SPAN):
        for p in range(PAIRS):
            kv_move(number, p).wait_send()
    send(lay_far.at[r], lay_far.at[1 - r], single, 3, place.to_x()).wait_recv()
    final_out[other_rows, :] = lay_far[1 - r]
    send(hid, hid, single, 0, place.to_x()).wait_send()
    send(ctx_in.at[0], ctx_in.at[0], single, 1, place.to_x()).wait_send()
    for p in range(PAIRS):
        to_ctx(p).wait_send()
    to_d.wait_send()
    send(lay_out.at[1 - r], d_out.at[other_rows], single, 4, place.to_x()).wait_recv()
    for copy in [hid_local, wq_local, q_local] + gives:
        copy.wait()
    for t in range(SPAN * PAIRS):
        kv_copy(jnp.int32(t)).wait()


def forward_attention(size, lengths, hid, qkv_weights, rest_weights, vec, cot):
    rows = hid.shape[0]
    part = rows // 2
    blk = qkv_weights[0].shape[0]
    n = size // 4
    any_space = pl.BlockSpec(memory_space=pl.ANY)
    vmem = pl.BlockSpec(memory_space=pltpu.VMEM)
    shape = jax.ShapeDtypeStruct
    n_col, n_all = (n - 1) + n + 2 * n, (n - 1) + n + 2 * n + 4 * n
    dma = pltpu.SemaphoreType.DMA
    scratch = pltpu.VMEM
    return pl.pallas_call(
        functools.partial(kernel_a, size),
        out_shape=(
            shape((2, rows, HALF), BF16),
            shape((size, blk, QKV), BF16),
            shape((PAIRS, rows, 128), BF16),
            shape((SPAN, 2 * PAIRS, rows, 128), BF16),
            shape((SPAN, 2 * PAIRS, rows, rows), BF16),
            shape((SPAN, 2 * PAIRS, 1, rows), F32),
            shape((2 * PAIRS, 1, rows), F32),
            shape((PAIRS, 128, rows), F32),
            shape((2 * size, blk, REST), BF16),
            shape((rows, HALF), BF16),
            shape((2, part, HALF), BF16),
            shape((part, HALF), F32),
            shape((rows, HALF), BF16),
            shape((16, D), F32),
        ),
        in_specs=[pl.BlockSpec(memory_space=pltpu.SMEM)] + [vmem] * 9,
        out_specs=[any_space] * 5 + [vmem] * 3 + [any_space] + [vmem] * 5,
        scratch_shapes=[
            scratch((2, rows, HALF), BF16),
            scratch((blk, QKV), BF16),
            scratch((size, blk, QKV), BF16),
            scratch((2 * size, 16, 128), BF16),
            scratch((blk, FIRST), BF16),
            scratch((2 * size, blk, FIRST), BF16),
            scratch((2 * size, blk, FF_HALF), BF16),
            scratch((SPAN, 2 * PAIRS, rows, 128), BF16),
            scratch((PAIRS, rows, 128), BF16),
            scratch((2 * PAIRS, rows, 128), BF16),
            scratch((2 * PAIRS, HEAD_DIM, rows), F32),
            scratch((2 * PAIRS, 1, rows), F32),
            scratch((2 * PAIRS, 1, rows), F32),
            scratch((2, 2, rows, rows), BF16),
            scratch((rows, HALF), BF16),
            scratch((2, part, HALF), BF16),
            scratch((2, part, HALF), BF16),
            scratch((2, part, HALF), BF16),
            scratch((2, part, HALF), BF16),
            scratch((part, D), F32),
            scratch((part, D), F32),
            scratch((part, D), BF16),
            scratch((part, 2 * FF_HALF), F32),
            scratch((part, 2 * FF_HALF), BF16),
            scratch((part, 2 * FF_HALF), BF16),
            dma((n_all,)),
            dma((n_all,)),
            dma((n_all,)),
            dma((n_all,)),
            dma((n_col,)),
            dma((n_col,)),
            dma((n_all,)),
            dma((n_all,)),
            dma((SPAN * PAIRS,)),
            dma((SPAN * PAIRS,)),
            dma((7,)),
            dma((7,)),
            dma((12 + SPAN * PAIRS,)),
            dma((2,)),
        ],
        compiler_params=pltpu.CompilerParams(
            collective_id=0, has_side_effects=True, vmem_limit_bytes=62 * 2**20
        ),
        name="forward_attention",
    )(lengths, hid, *qkv_weights, *rest_weights, vec, cot)


def kernel_c(
    size,
    d_ctx,
    qs,
    m_in,
    lse_in,
    ctxt,
    hid_all,
    wq_all,
    dres_low,
    dres_own,
    small_in,
    kv_in,
    p_in,
    g_in,
    query_out,
    key_out,
    value_out,
    wo_out,
    wi_out,
    wu_out,
    small_out,
    bias_out,
    grad_out,
    dtot,
    delta,
    qm,
    acc,
    kv,
    pbuf,
    big,
    cb,
    rb,
    st,
    b1,
    b2,
    b3,
    b4,
    d_all,
    hid_t,
    far,
    gq,
    q1,
    q2,
    q3,
    near,
    bias_own,
    bias_got,
    vec_sum,
    vec_got,
    one_send,
    one_recv,
    kv_send,
    kv_recv,
    g_send,
    g_recv,
    q_send,
    q_recv,
    s_send,
    s_recv,
    v_send,
    v_recv,
    load,
    p_sem,
):
    place = Place(size)
    rows = qs.shape[1]
    part = rows // 2
    n = place.planes
    r, y, j = place.r, place.y, place.j
    half = size // 2
    blk = wq_all.shape[1]
    own_rows = pl.ds(pl.multiple_of(r * part, part), part)

    def b_block(i):
        pair, core = lax.div(i, 2), lax.rem(j + 1 + lax.rem(i, 2), 2)
        return place.near_block(1 - lax.div(pair, 2), 1 - lax.rem(pair, 2), core)

    def kv_load(i):
        return pltpu.make_async_copy(kv_in.at[b_block(i)], kv.at[i], load.at[i])

    def p_load(t, slot):
        p, i = lax.div(t, SPAN), lax.rem(t, SPAN)
        return pltpu.make_async_copy(
            p_in.at[b_block(i), pl.ds(2 * p, 2)], pbuf.at[slot], p_sem.at[slot]
        )

    def index(other, k, m):
        return 2 * n * other + 2 * ((k + n - 1) % n) + m

    def g_block(at, core):
        n_at, m = at // (2 * n), at % 2
        k = ((at % (2 * n)) // 2 + 1) % n
        return place.any_block(
            lax.rem(r + 1 + n_at, 2), place.plane(k), lax.rem(y + 1 + m, 2), core
        )

    def g_load(at):
        return pltpu.make_async_copy(g_in.at[g_block(at, j)], st.at[at], load.at[8 + at])

    def loop(count, body):
        def step(at, carry):
            body(at)
            return carry

        lax.fori_loop(0, count, step, jnp.int32(0))

    needed = [(0, 2, 0), (0, 1, 0), (0, 2, 1), (1, 1, 0), (0, 3, 0), (0, 3, 1), (1, 2, 0), (1, 2, 1)]
    needed += [(0, 1, 1), (1, 1, 1), (0, 0, 0), (0, 0, 1), (1, 3, 0), (1, 3, 1), (1, 0, 0), (1, 0, 1)]
    needed = [index(*at) for at in needed]
    p_load(jnp.int32(0), 0).start()
    for at in needed[:4]:
        g_load(at).start()
    loop(SPAN, lambda i: kv_load(i).start())
    for at in needed[4:]:
        g_load(at).start()
    lane = lax.broadcasted_iota(jnp.int32, (rows, 128), 1)
    for p in range(PAIRS):
        piece = qs[p]
        qm[2 * p] = jnp.where(lane < HEAD_DIM, piece, jnp.zeros_like(piece))
        qm[2 * p + 1] = jnp.where(lane >= HEAD_DIM, piece, jnp.zeros_like(piece))
    acc[...] = jnp.zeros_like(acc)
    for which in range(2):
        hid_t[which] = hid_all[which].T
    far[...] = jnp.zeros_like(far)
    far[own_rows, :] = dres_low[1 - r].astype(F32)
    grad_out[...] = jnp.zeros_like(grad_out)
    grad_out[own_rows, :] = dres_own[...]
    upper = lax.broadcasted_iota(jnp.int32, (128, rows), 0) < HEAD_DIM
    for p in range(PAIRS):
        turned = d_ctx[:, p * 128 : (p + 1) * 128].astype(F32).T
        product = turned * ctxt[p]
        delta[2 * p] = jnp.sum(product[:HEAD_DIM], axis=0, keepdims=True)
        delta[2 * p + 1] = jnp.sum(product[HEAD_DIM:], axis=0, keepdims=True)
        dtot[2 * p] = jnp.where(upper, turned, 0.0)
        dtot[2 * p + 1] = jnp.where(upper, 0.0, turned)
    with jax.named_scope("meet"):
        meet(place)
    single = (one_send, one_recv)
    gs = (g_send, g_recv)
    ks = (kv_send, kv_recv)
    at_x, at_y, at_z = 4 * n, 6 * n, 8 * n

    send(small_in, vec_got.at[0], (v_send, v_recv), 0, place.to_x()).start()

    def c_move(at):
        return send(g_in.at[g_block(at, 1 - j)], b1.at[at], gs, at, place.to_core())

    for at in needed:
        c_move(at).start()

    def fold(target, source, at):
        total = target[at].astype(F32) + source.astype(F32)
        target[at] = total.astype(BF16)

    def pieces(p):
        return pl.ds(2 * p, 2)

    def core_send(p, pair):
        return send(
            big.at[2 * pair, pieces(p)], cb.at[pair, pieces(p)], ks, 4 * p + pair, place.to_core()
        )

    def core_add(p, pair):
        core_send(p, pair).wait_recv()
        for piece in (2 * p, 2 * p + 1):
            fold(big, cb[pair, piece], (2 * pair + 1, piece))

    def hop(p, pair):
        peer = place.to_y() if pair == 2 else place.to_z_near()
        number = 4 * PAIRS + 3 * p + pair
        return send(big.at[2 * pair + 1, pieces(p)], rb.at[pair, pieces(p)], ks, number, peer)

    def hop_add(p):
        hop(p, 0).wait_recv()
        for piece in (2 * p, 2 * p + 1):
            fold(big, rb[0, piece], (5, piece))

    def g_core_add(other, k, m):
        at = index(other, k, m)
        c_move(at).wait_recv()
        g_load(at).wait()
        fold(st, b1[at], at)

    def gx(k, m):
        at = index(0, k, m)
        return send(st.at[at], b2.at[at], gs, at_x + at, place.to_x())

    def gx_add(k, m):
        gx(k, m).wait_recv()
        fold(st, b2[index(0, k, m)], index(1, k, m))

    def gy(k, other):
        slot = 2 * k + other
        return send(st.at[index(other, k, 0)], b3.at[slot], gs, at_y + slot, place.to_y())

    def gy_add(k, other):
        gy(k, other).wait_recv()
        fold(st, b3[2 * k + other], index(other, k, 1))

    def gz(k):
        return send(st.at[index(1, k, 1)], b4.at[k - 1], gs, at_z + k - 1, place.to_z(k))

    vz = (v_send, v_recv)

    def vector(number):
        level = min(number, 3)
        step = max(number - 2, 1)
        peer = (place.to_x(), place.to_core(), place.to_y(), place.to_z(step))[level]
        source = small_in if level == 0 else vec_sum.at[level - 1]
        return send(source, vec_got.at[number], vz, number, peer)

    def vector_add(level):
        vector(level).wait_recv()
        before = small_in[...] if level == 0 else vec_sum[level - 1]
        vec_sum[level] = before + vec_got[level]

    qz = (q_send, q_recv)

    def q_core(p):
        return send(gq.at[p, 1 - j], q1.at[p], qz, (n + 1) * p, place.to_core())

    def q_side(p):
        return send(gq.at[p, j, 1 - y], q2.at[p], qz, (n + 1) * p + 1, place.to_y())

    def q_plane(p, k):
        return send(
            gq.at[p, j, y, place.plane(k)], q3.at[p, k - 1], qz, (n + 1) * p + 1 + k, place.to_z(k)
        )

    def q_core_add(p):
        q_core(p).wait_recv()
        for side in range(2):
            fold(gq, q1[p, side], (p, j, side))

    def q_side_add(p):
        q_side(p).wait_recv()
        fold(gq, q2[p], (p, j, y))

    def q_planes(p):
        for k in range(1, n):
            q_plane(p, k).start()

    def settle(p):
        core_send(p, 3).wait_recv()
        hop(p, 1).wait_recv()
        hop(p, 2).wait_recv()
        both = jnp.concatenate([acc[2 * p], acc[2 * p + 1]], axis=0)
        d_query = (both.T * 0.125).astype(BF16)
        d_all[p, :, 0:128] = d_query
        lanes = slice(p * 128, (p + 1) * 128)
        bias_own[0, 0:1, lanes] = jnp.sum(d_query.astype(F32), axis=0, keepdims=True)
        for at in range(2):
            piece = 2 * p + at
            total = big[7, piece].astype(F32) + cb[3, piece].astype(F32)
            total += rb[1, piece].astype(F32) + rb[2, piece].astype(F32)
            low = total.astype(BF16)
            d_all[p, :, (at + 1) * 128 : (at + 2) * 128] = low
        bias_own[0, 1:2, lanes] = jnp.sum(low.astype(F32), axis=0, keepdims=True)

    def input_term(p, which):
        parts = []
        for at in range(3):
            columns = slice(at * HALF + p * 128, at * HALF + (p + 1) * 128)
            parts.append(wq_all[pl.ds(which * half, half), :, columns].reshape(HALF, 128))
        return dot(d_all[p], jnp.concatenate(parts, axis=1), NT)

    def far_term(p):
        far[...] = far[...] + input_term(p, 1 - r)

    def own_term(p):
        grad_out[...] = grad_out[...] + input_term(p, r)

    def grads(p):
        for which in range(2):
            term = dot(hid_t[which], d_all[p], NN).astype(BF16)
            for b in range(half):
                c = which * half + b
                gq[p, c % 2, (c // 2) % 2, c // 4] = term[b * blk : (b + 1) * blk]

    events = {}

    def add(step, what, *inputs):
        events.setdefault(step, []).append(functools.partial(what, *inputs))

    def start(step, what, *inputs):
        add(step, lambda: what(*inputs).start())

    bias_own[0, 2:8] = jnp.zeros((6, HALF), F32)
    add(0, g_core_add, 0, 2, 0)
    start(0, gx, 2, 0)
    add(0, g_core_add, 0, 1, 0)
    start(0, gy, 1, 0)
    add(1, g_core_add, 0, 2, 1)
    add(1, g_core_add, 1, 1, 0)
    start(2, gx, 2, 1)
    start(2, gy, 1, 1)
    add(2, g_core_add, 0, 3, 0)
    add(3, vector_add, 0)
    start(3, vector, 1)
    start(3, gx, 3, 0)
    add(3, g_core_add, 0, 3, 1)
    late = [(1, 2, 0), (1, 2, 1), (0, 1, 1), (1, 1, 1), (0, 0, 0), (0, 0, 1), (1, 3, 0), (1, 3, 1)]
    for at, what in enumerate(late + [(1, 0, 0), (1, 0, 1)]):
        add(4 + at, g_core_add, *what)
    add(6, vector_add, 1)
    start(6, vector, 2)
    add(8, gx_add, 2, 0)
    add(8, gy_add, 1, 0)
    add(9, gx_add, 2, 1)
    start(9, gy, 2, 1)
    add(9, gy_add, 1, 1)
    start(10, gx, 1, 1)
    start(10, gx, 3, 1)
    start(10, gx, 0, 0)
    start(11, gx, 0, 1)
    add(11, vector_add, 2)
    for step in range(1, n):
        start(11, vector, 2 + step)
    add(15, gy_add, 2, 1)
    start(15, gz, 2)
    add(18, gx_add, 1, 1)
    add(19, gx_add, 3, 0)
    add(19, gx_add, 3, 1)
    start(19, gy, 3, 1)
    for p in range(PAIRS):
        base = SPAN * p
        late = 7 if p == PAIRS - 1 else 8
        start(base + 2, core_send, p, 0)
        add(base + 3, core_add, p, 0)
        start(base + 3, hop, p, 0)
        start(base + 4, core_send, p, 1)
        add(base + 5, core_add, p, 1)
        start(base + 5, hop, p, 1)
        start(base + 6, core_send, p, 2)
        add(base + 7, core_add, p, 2)
        add(base + late, hop_add, p)
        start(base + late, hop, p, 2)
        start(base + 8, core_send, p, 3)
        if p < PAIRS - 1:
            add(base + 14, settle, p)
            add(base + 14, grads, p)
            start(base + 14, q_core, p)
            add(base + 15, far_term, p)
            add(base + 15, own_term, p)
            add(base + 15, q_core_add, p)

    steps = SPAN * PAIRS

    def back(t, carry):
        p, i = lax.div(t, SPAN), lax.rem(t, SPAN)
        for step, calls in sorted(events.items()):
            if step < steps:

                @pl.when(t == step)
                def _(calls=calls):
                    with jax.named_scope(f"step_{step}"):
                        for call in calls:
                            call()

        slot = lax.rem(t, 2)

        @pl.when(t + 1 < steps)
        def _():
            p_load(t + 1, 1 - slot).start()

        @pl.when(p == 0)
        def _():
            kv_load(i).wait()

        p_load(t, slot).wait()
        where = b_block(i)
        key = kv[i, 2 * p]
        value = kv[i, 2 * p + 1]
        key_t = key.T
        d_key = d_value = None
        for h in range(2):
            g = 2 * p + h
            factor = jnp.exp(m_in[where, g] - lse_in[g])
            d_rows = (dtot[g] * factor).astype(BF16)
            weights = pbuf[slot, h]
            d_probs = dot(value, d_rows, NN)
            d_scores = (weights.astype(F32) * (d_probs - delta[g] * factor)).astype(BF16)
            value_term = dot(weights, d_rows, NT)
            key_term = dot(d_scores, qm[g], NN)
            acc[g] += dot(key_t[h * HEAD_DIM : (h + 1) * HEAD_DIM], d_scores, NN)
            d_key = key_term if d_key is None else d_key + key_term
            d_value = value_term if d_value is None else d_value + value_term
        big[i, 2 * p] = d_key.astype(BF16)
        big[i, 2 * p + 1] = d_value.astype(BF16)
        return carry

    lax.fori_loop(0, steps, back, jnp.int32(0))

    last = PAIRS - 1
    for call in events[steps]:
        call()
    gz(1).start()
    q_side(0).start()
    q_side(1).start()
    with jax.named_scope("settle"):
        settle(last)
    with jax.named_scope("far"):
        far_term(last)
        near[0] = far[...].astype(BF16)
    to_near = send(near.at[0], near.at[1], single, 0, place.to_x())
    with jax.named_scope("grads"):
        grads(last)
    to_near.start()
    q_core(last).start()
    sz = (s_send, s_recv)

    def small(number):
        level = min(number, 2)
        peer = (place.to_core(), place.to_y(), place.to_z(max(number - 1, 1)))[level]
        return send(bias_own.at[level], bias_got.at[number], sz, number, peer)

    small(0).start()
    with jax.named_scope("own"):
        own_term(last)
    with jax.named_scope("q_core"):
        q_core_add(last)
        small(0).wait_recv()
        bias_own[1] = bias_own[0] + bias_got[0]
    q_side(last).start()
    small(1).start()
    with jax.named_scope("g_x_0"):
        gx_add(0, 0)
        gx_add(0, 1)
    gy(0, 1).start()
    with jax.named_scope("g_y_3"):
        gy_add(3, 1)
    gz(3).start()
    with jax.named_scope("q_side_0"):
        q_side_add(0)
        q_planes(0)
    with jax.named_scope("q_side_1"):
        q_side_add(1)
        q_planes(1)
    with jax.named_scope("q_side_2"):
        q_side_add(last)
        q_planes(last)
        small(1).wait_recv()
        bias_own[2] = bias_own[1] + bias_got[1]
    for step in range(1, n):
        small(1 + step).start()
    with jax.named_scope("vectors"):
        total = vec_sum[2]
        for step in range(1, n):
            vector(2 + step).wait_recv()
            total = total + vec_got[2 + step]
        small_out[...] = total

    def q_out(p):
        total = gq[p, j, y, place.z].astype(F32)
        for k in range(1, n):
            q_plane(p, k).wait_recv()
            total = total + q3[p, k - 1].astype(F32)
        lanes = slice(p * 128, (p + 1) * 128)
        query_out[:, lanes] = total[:, :128]
        key_out[:, lanes] = total[:, 128:256]
        value_out[:, lanes] = total[:, 256:]

    with jax.named_scope("q_out_0"):
        q_out(0)
    with jax.named_scope("near_wait"):
        to_near.wait_recv()
        grad_out[...] = grad_out[...] + near[1].astype(F32)
    with jax.named_scope("g_z"):
        total = None
        for k in range(1, n):
            gz(k).wait_recv()
            got = b4[k - 1].astype(F32)
            total = got if total is None else total + got
    with jax.named_scope("g_y_0"):
        gy_add(0, 1)
        total = total + st[index(1, 0, 1)].astype(F32)
        wo_out[...] = total[:, :HALF]
        wi_out[...] = total[:, HALF:FIRST]
        wu_out[...] = total[:, FIRST:]
    with jax.named_scope("q_out"):
        q_out(1)
        q_out(last)
        total = bias_own[2]
        for step in range(1, n):
            small(1 + step).wait_recv()
            total = total + bias_got[1 + step]
        bias_out[...] = total

    for at in range(4 * n):
        c_move(at).wait_send()
    for k in range(n):
        first = k == 1
        for m in range(2):
            if not first or m == 1:
                gx(k, m).wait_send()
            if first or m == 1:
                gy(k, m).wait_send()
    for k in range(1, n):
        gz(k).wait_send()
        small(1 + k).wait_send()
        for p in range(PAIRS):
            q_plane(p, k).wait_send()
    small(0).wait_send()
    small(1).wait_send()
    for number in range(n + 2):
        vector(number).wait_send()
    for p in range(PAIRS):
        q_core(p).wait_send()
        q_side(p).wait_send()
        for pair in range(4):
            core_send(p, pair).wait_send()
        for pair in range(3):
            hop(p, pair).wait_send()
    to_near.wait_send()


def backward_attention(
    size, dctx, qs, m_in, lse_in, ctxt, hid_all, wq_all, dres_low, dres_own, small_in, kv_in, p_in, g_in
):
    rows = qs.shape[1]
    part = rows // 2
    blk = wq_all.shape[1]
    n = size // 4
    any_space = pl.BlockSpec(memory_space=pl.ANY)
    vmem = pl.BlockSpec(memory_space=pltpu.VMEM)
    shape = jax.ShapeDtypeStruct
    dma = pltpu.SemaphoreType.DMA
    scratch = pltpu.VMEM
    g_count, q_count = 4 * n + 2 * n + 2 * n + n - 1, PAIRS * (n + 1)
    return pl.pallas_call(
        functools.partial(kernel_c, size),
        out_shape=(
            shape((blk, HALF), F32),
            shape((blk, HALF), F32),
            shape((blk, HALF), F32),
            shape((blk, HALF), F32),
            shape((blk, FF_HALF), F32),
            shape((blk, FF_HALF), F32),
            shape((16, D), F32),
            shape((8, HALF), F32),
            shape((rows, HALF), F32),
        ),
        in_specs=[vmem] * 10 + [any_space] * 3,
        out_specs=[vmem] * 9,
        scratch_shapes=[
            scratch((2 * PAIRS, 128, rows), F32),
            scratch((2 * PAIRS, 1, rows), F32),
            scratch((2 * PAIRS, rows, 128), BF16),
            scratch((2 * PAIRS, HEAD_DIM, rows), F32),
            scratch((SPAN, 2 * PAIRS, rows, 128), BF16),
            scratch((2, 2, rows, rows), BF16),
            scratch((SPAN, 2 * PAIRS, rows, 128), BF16),
            scratch((4, 2 * PAIRS, rows, 128), BF16),
            scratch((3, 2 * PAIRS, rows, 128), BF16),
            scratch((4 * n, blk, REST), BF16),
            scratch((4 * n, blk, REST), BF16),
            scratch((2 * n, blk, REST), BF16),
            scratch((2 * n, blk, REST), BF16),
            scratch((n - 1, blk, REST), BF16),
            scratch((PAIRS, rows, HALF), BF16),
            scratch((2, HALF, rows), BF16),
            scratch((rows, HALF), F32),
            scratch((PAIRS, 2, 2, n, blk, HALF), BF16),
            scratch((PAIRS, 2, n, blk, HALF), BF16),
            scratch((PAIRS, n, blk, HALF), BF16),
            scratch((PAIRS, n - 1, blk, HALF), BF16),
            scratch((2, rows, HALF), BF16),
            scratch((3, 8, HALF), F32),
            scratch((n + 1, 8, HALF), F32),
            scratch((3, 16, D), F32),
            scratch((n + 2, 16, D), F32),
            dma((1,)),
            dma((1,)),
            dma((7 * PAIRS,)),
            dma((7 * PAIRS,)),
            dma((g_count,)),
            dma((g_count,)),
            dma((q_count,)),
            dma((q_count,)),
            dma((n + 1,)),
            dma((n + 1,)),
            dma((n + 2,)),
            dma((n + 2,)),
            dma((9 + 4 * n,)),
            dma((2,)),
        ],
        compiler_params=pltpu.CompilerParams(
            collective_id=1, has_side_effects=True, vmem_limit_bytes=63 * 2**20
        ),
        name="backward_attention",
    )(dctx, qs, m_in, lse_in, ctxt, hid_all, wq_all, dres_low, dres_own, small_in, kv_in, p_in, g_in)


def kernel_d(size, per, count, *refs):
    sources, targets = refs[:count], refs[count : 2 * count - 1]
    held, tile, come, go = refs[2 * count - 1 : 3 * count - 1], refs[-3], refs[-2], refs[-1]
    small, bias = held[0], held[1]
    loads = [pltpu.make_async_copy(s, h, come.at[at]) for at, (s, h) in enumerate(zip(sources, held))]
    done = list(held[2:]) + [tile]
    stores = [pltpu.make_async_copy(h, t, go.at[at]) for at, (h, t) in enumerate(zip(done, targets))]
    for copy in loads:
        copy.start()
    loads[0].wait()
    loads[1].wait()
    row = lax.axis_index("row")
    inside = lax.rem(lax.axis_index("col"), size)
    start = row * HALF + inside * per
    lines = small[...]
    tile[0:6] = pltpu.roll(lines, D - start, 1)[0:6, :128]
    spot = inside * 4 * per
    hidden = pltpu.roll(lines, D - lax.rem(spot, D), 1)[:, :128]
    wanted = 6 + 2 * row + lax.div(spot, D)
    line = lax.broadcasted_iota(jnp.int32, hidden.shape, 0)
    tile[6:7] = jnp.sum(jnp.where(line == wanted, hidden, 0.0), axis=0, keepdims=True)
    tile[7:9] = pltpu.roll(bias[...], HALF - inside * per, 1)[0:2, :128]
    tile[9:16] = jnp.zeros((7, 128), F32)
    stores[-1].start()
    for load, store in zip(loads[2:], stores):
        load.wait()
        store.start()
    for store in stores:
        store.wait()


def finish(size, small, bias, arrays):
    space = pl.BlockSpec(memory_space=pl.ANY)
    shapes = [jax.ShapeDtypeStruct(a.shape, a.dtype) for a in arrays]
    arrays = [small, bias] + arrays
    count = len(arrays)
    return pl.pallas_call(
        functools.partial(kernel_d, size, HALF // size, count),
        out_shape=shapes + [jax.ShapeDtypeStruct((16, 128), F32)],
        in_specs=[space] * count,
        out_specs=[space] * (count - 1),
        scratch_shapes=[pltpu.VMEM(a.shape, a.dtype) for a in arrays]
        + [pltpu.VMEM((16, 128), F32)]
        + [pltpu.SemaphoreType.DMA((count,))] * 2,
        compiler_params=pltpu.CompilerParams(vmem_limit_bytes=63 * 2**20),
        name="finish",
    )(*arrays)


def per_device(group, hidden_in, cotangent, lengths, *params):
    w_query, w_key, w_value, w_output, w_inner, w_outer = params[:6]
    b_query, b_value, b_output, b_inner, b_outer = params[6:11]
    gain_one, shift_one, gain_two, shift_two = params[11:]
    cols = lax.axis_size("col")
    size = group
    ways = cols // size
    inside = lax.axis_index("col") % size
    row = lax.axis_index("row")

    def regroup(block):
        if ways == 1:
            return block
        whole = lax.all_gather(block, "col", axis=0, tiled=True)
        count = block.shape[0] * ways
        return lax.dynamic_slice_in_dim(whole, inside * count, count, axis=0)

    vec = jnp.zeros((16, 128), BF16)
    vectors = (b_query, b_value, b_output, b_outer, gain_one, shift_one, gain_two, shift_two)
    for at, vector in enumerate(vectors + (b_inner,)):
        line = regroup(vector)
        vec += jnp.pad(line[None, :], ((at, 15 - at), (0, 128 - line.shape[0])))
    qkv_weights = [regroup(w) for w in (w_query, w_key, w_value)]
    rest_weights = [regroup(w) for w in (w_output.T, w_inner, w_outer.T)]
    (hid_all, wq_all, qs, kv, probs, m_all, lse, ctxt, g_parts, layer_out, low, own, d_context, small) = (
        forward_attention(size, lengths, hidden_in, qkv_weights, rest_weights, vec, cotangent)
    )
    (g_query, g_key, g_value, g_output, g_inner, g_outer, g_small, g_bias, grad_in) = (
        backward_attention(
            size,
            d_context,
            qs,
            m_all,
            lse,
            ctxt,
            hid_all,
            wq_all,
            low,
            own,
            small,
            kv,
            probs,
            g_parts,
        )
    )

    def spread(block):
        if ways == 1:
            return block
        count = block.shape[0]
        whole = jnp.zeros((count * size,) + block.shape[1:], block.dtype)
        whole = lax.dynamic_update_slice_in_dim(whole, block, inside * count, axis=0)
        return lax.psum_scatter(whole, "col", scatter_dimension=0, tiled=True)

    arrays = [g_query, g_key, g_value, g_output, g_inner, g_outer, grad_in, layer_out]
    *arrays, tile = finish(size, g_small, g_bias, arrays)
    g_query, g_key, g_value, g_output, g_inner, g_outer, grad_in, layer_out = arrays
    per = HALF // size
    pieces = [spread(tile[at, : 4 * per if at == 6 else per]) for at in range(9)]
    g_b_output, g_b_outer, g_gain_one, g_shift_one, g_gain_two, g_shift_two = pieces[:6]
    g_b_inner, g_b_query, g_b_value = pieces[6:]
    return (
        layer_out,
        grad_in,
        spread(g_query),
        spread(g_key),
        spread(g_value),
        spread(g_output).T,
        spread(g_inner),
        spread(g_outer).T,
        g_b_query,
        g_b_value,
        g_b_output,
        g_b_inner,
        g_b_outer,
        g_gain_one,
        g_shift_one,
        g_gain_two,
        g_shift_two,
    )


def solution(mesh):
    cols = mesh.shape["col"]
    group = max(s for s in range(SPAN, cols + 1, 4) if cols % s == 0 and D // s % 16 == 0)
    token, weight, turned = P("col", "row"), P("col", "row"), P("row", "col")
    vector = P(("row", "col"))
    return jax.shard_map(
        functools.partial(per_device, group),
        mesh=mesh,
        in_specs=(token, token, P()) + (weight,) * 3 + (turned, weight, turned) + (vector,) * 9,
        out_specs=(token, token) + (weight,) * 3 + (turned, weight, turned) + (vector,) * 9,
        check_vma=False,
    )
```

```python
import functools

import jax
import jax.numpy as jnp
from jax import lax
from jax.experimental import pallas as pl
from jax.experimental.pallas import tpu as pltpu
from jax.sharding import PartitionSpec as P

D = 768
HALF = 384
HEAD_DIM = 64
FF_HALF = 1536
PAIRS = 3
SPAN = 8
EPSILON = 1e-12
MASKED = -1e30
MESH = pl.DeviceIdType.MESH
F32 = jnp.float32
BF16 = jnp.bfloat16
FIRST = HALF + FF_HALF
REST = HALF + 2 * FF_HALF
QKV = 3 * HALF


def dot(left, right, contract):
    return lax.dot_general(left, right, (contract, ((), ())), preferred_element_type=F32)


NN = ((1,), (0,))
NT = ((1,), (1,))
TN = ((0,), (0,))


class Place:
    def __init__(self, size):
        self.size = size
        self.planes = size // 4
        self.r = lax.axis_index("row")
        col = lax.axis_index("col")
        self.base = lax.div(col, size) * size
        inner = lax.rem(col, size)
        self.slot = lax.div(col, SPAN)
        self.block = lax.rem(col, SPAN)
        self.z = lax.div(inner, 4)
        self.y = lax.rem(lax.div(inner, 2), 2)
        self.j = lax.rem(inner, 2)
        self.zl = lax.rem(self.z, 2)

    def plane(self, step):
        return lax.rem(self.z + step + self.planes, self.planes)

    def device(self, r, z, y, j):
        return (r, self.base + z * 4 + y * 2 + j)

    def to_z(self, step):
        return self.device(self.r, self.plane(step), self.y, self.j)

    def to_z_near(self):
        return self.device(self.r, self.z - self.zl + (1 - self.zl), self.y, self.j)

    def to_y(self):
        return self.device(self.r, self.z, 1 - self.y, self.j)

    def to_x(self):
        return self.device(1 - self.r, self.z, self.y, self.j)

    def to_core(self):
        return self.device(self.r, self.z, self.y, 1 - self.j)

    def col_block(self, z, y, j):
        return z * 4 + y * 2 + j

    def any_block(self, r, z, y, j):
        return r * self.size + z * 4 + y * 2 + j

    def near_block(self, dz, dy, j):
        return lax.rem(self.zl + dz, 2) * 4 + lax.rem(self.y + dy, 2) * 2 + j


def meet(place):
    barrier = pltpu.get_barrier_semaphore()
    peers = [place.to_z(step) for step in range(1, place.planes)]
    peers += [place.to_y(), place.to_x(), place.to_core()]
    for peer in peers:
        pl.semaphore_signal(barrier, inc=1, device_id=peer, device_id_type=MESH)
    pl.semaphore_wait(barrier, len(peers))


def send(src, dst, sems, index, peer):
    return pltpu.make_async_remote_copy(
        src_ref=src,
        dst_ref=dst,
        send_sem=sems[0].at[index],
        recv_sem=sems[1].at[index],
        device_id=peer,
        device_id_type=MESH,
    )


class Gather:
    def __init__(self, place, own, full, sems, with_rows):
        self.place, self.own, self.full, self.sems = place, own, full, sems
        self.rows = 2 if with_rows else 1
        self.with_rows = with_rows
        n = place.planes
        self.at_y = n - 1
        self.at_x = self.at_y + n
        self.at_c = self.at_x + (2 * n if with_rows else 0)
        self.total = self.at_c + 2 * n * self.rows

    def index(self, n, k, m, j):
        p = self.place
        z, y = p.plane(-k), lax.rem(p.y + m, 2)
        if self.with_rows:
            return p.any_block(lax.rem(p.r + n, 2), z, y, j)
        return p.col_block(z, y, j)

    def move(self, number, peer, n, k, m, j, local):
        where = self.index(n, k, m, j)
        src = self.own if local else self.full.at[where]
        return send(src, self.full.at[where], self.sems, number, peer)

    def z_sends(self):
        p = self.place
        for step in range(1, p.planes):
            self.move(step - 1, p.to_z(step), 0, 0, 0, p.j, True).start()

    def z_done(self, k):
        p = self.place
        self.move(k - 1, p.to_z(k), 0, k, 0, p.j, False).wait_recv()

    def y_send(self, k):
        p = self.place
        self.move(self.at_y + k, p.to_y(), 0, k, 0, p.j, k == 0).start()

    def y_done(self, k):
        p = self.place
        self.move(self.at_y + k, p.to_y(), 0, k, 1, p.j, False).wait_recv()

    def x_send(self, k, m):
        p = self.place
        self.move(self.at_x + 2 * k + m, p.to_x(), 0, k, m, p.j, k + m == 0).start()

    def x_done(self, k, m):
        p = self.place
        self.move(self.at_x + 2 * k + m, p.to_x(), 1, k, m, p.j, False).wait_recv()

    def c_number(self, n, k, m):
        return self.at_c + (2 * k + m) * self.rows + n

    def c_send(self, n, k, m):
        p = self.place
        number = self.c_number(n, k, m)
        self.move(number, p.to_core(), n, k, m, p.j, n + k + m == 0).start()

    def c_done(self, n, k, m):
        p = self.place
        self.move(self.c_number(n, k, m), p.to_core(), n, k, m, 1 - p.j, False).wait_recv()

    def all_sent(self):
        for number in range(self.total):
            send(self.own, self.own, self.sems, number, self.place.to_core()).wait_send()


def spread_rows(tiles, picks, per, width):
    blocks = tiles.shape[0]
    flat = tiles.reshape(blocks * 16, 128)
    total = len(picks) * blocks
    line = lax.broadcasted_iota(jnp.int32, (total, blocks * 16), 0)
    at = lax.broadcasted_iota(jnp.int32, (total, blocks * 16), 1)
    wanted = jnp.zeros((total, blocks * 16), F32)
    for spot, pick in enumerate(picks):
        hit = at == (line - spot * blocks) * 16 + pick
        inside = (line >= spot * blocks) & (line < (spot + 1) * blocks)
        wanted = jnp.where(hit & inside, 1.0, wanted)
    taken = dot(wanted.astype(BF16), flat, NN).astype(BF16)
    lane = lax.broadcasted_iota(jnp.int32, (128, width), 1).astype(F32)
    group = jnp.floor((lane + 0.5) * (1.0 / per))
    place = lax.broadcasted_iota(jnp.int32, (128, width), 0).astype(F32)
    copies = jnp.where(lane - group * per == place, 1.0, 0.0).astype(BF16)
    wide = dot(taken, copies, NN)
    first = lax.broadcasted_iota(jnp.int32, (blocks, width), 0) * per
    column = lax.broadcasted_iota(jnp.int32, (blocks, width), 1)
    mask = (column >= first) & (column < first + per)
    rows = []
    for spot in range(len(picks)):
        part = jnp.where(mask, wide[spot * blocks : (spot + 1) * blocks], 0.0)
        rows.append(jnp.sum(part, axis=0, keepdims=True))
    return rows


def gelu_both(argument):
    spread = 1.0 + lax.erf(argument * 0.7071067811865476)
    bell = jnp.exp(argument * argument * -0.5) * 0.3989422804014327
    return 0.5 * argument * spread, 0.5 * spread + argument * bell


def norm_forward(resid, gain, shift):
    center = resid - jnp.mean(resid, axis=1, keepdims=True)
    scale = lax.rsqrt(jnp.mean(center * center, axis=1, keepdims=True) + EPSILON)
    normal = center * scale
    return normal * gain + shift, normal, scale


def norm_backward(incoming, normal, scale, gain):
    scaled = incoming * gain
    first = jnp.mean(scaled, axis=1, keepdims=True)
    second = jnp.mean(scaled * normal, axis=1, keepdims=True)
    result = scale * (scaled - first - normal * second)
    sums = jnp.sum(incoming * normal, axis=0, keepdims=True)
    return result, sums, jnp.sum(incoming, axis=0, keepdims=True)


def staged(kernel, size, inputs, outputs, picks, *refs):
    results, rest = list(refs[inputs : inputs + outputs]), refs[inputs + outputs :]
    held, sems, rest = rest[: len(picks)], rest[len(picks)], rest[len(picks) + 1 :]
    targets = [results[at] for at in picks]
    for at, ref in zip(picks, held):
        results[at] = ref

    def leave(number):
        return pltpu.make_async_copy(held[number], targets[number], sems.at[number])

    kernel(size, leave, *refs[:inputs], *results, *rest)
    for number in range(len(picks)):
        leave(number).wait()


def kernel_a(
    size,
    leave,
    lengths,
    hid,
    w_query,
    w_key,
    w_value,
    w_output,
    w_inner,
    w_outer,
    vec_in,
    cot,
    hid_out,
    wq_out,
    q_out,
    kv_out,
    p_out,
    m_out,
    lse_out,
    ctxt_out,
    g_out,
    final_out,
    low_out,
    own_out,
    d_out,
    small_out,
    hid_all,
    wq_own,
    wq_all,
    vec_all,
    one_own,
    one_all,
    two_all,
    kv,
    qs,
    qm,
    acc,
    high,
    low,
    pbuf,
    ctx_tp,
    ctx_in,
    cot_in,
    lay_out,
    lay_far,
    normed_ref,
    normal_ref,
    low_ref,
    slope_ref,
    act_ref,
    d_ref,
    one_send,
    one_recv,
    two_send,
    two_recv,
    wq_send,
    wq_recv,
    vec_send,
    vec_recv,
    kv_send,
    kv_recv,
    lone_send,
    lone_recv,
    local,
    p_sem,
):
    place = Place(size)
    rows = hid.shape[0]
    part = rows // 2
    n = place.planes
    r, y, j = place.r, place.y, place.j
    blk = w_query.shape[0]
    for at, source in enumerate((w_query, w_key, w_value)):
        wq_own[:, at * HALF : (at + 1) * HALF] = source[...]
    one_own[:, :HALF] = w_output[...]
    one_own[:, HALF:] = w_inner[...]
    with jax.named_scope("meet"):
        meet(place)

    single = (lone_send, lone_recv)
    own_rows = pl.ds(pl.multiple_of(r * part, part), part)
    other_rows = pl.ds(pl.multiple_of((1 - r) * part, part), part)
    to_hid = send(hid, hid_all.at[r], single, 0, place.to_x())
    to_hid.start()
    vec = Gather(place, vec_in, vec_all, (vec_send, vec_recv), True)
    wq = Gather(place, wq_own, wq_all, (wq_send, wq_recv), False)
    one = Gather(place, one_own, one_all, (one_send, one_recv), True)
    two = Gather(place, w_outer, two_all, (two_send, two_recv), True)
    for gather in (vec, wq):
        gather.z_sends()
        gather.y_send(0)
        gather.c_send(0, 0, 0)
    vec.x_send(0, 0)
    one.x_send(0, 0)
    one.y_send(0)
    two.x_send(0, 0)
    to_cot = send(cot.at[other_rows], cot_in.at[r], single, 1, place.to_x())
    to_cot.start()
    one.c_send(0, 0, 0)
    two.c_send(0, 0, 0)
    hid_all[r] = hid[...]
    mine = place.any_block(r, place.z, y, j)
    wq_all[place.col_block(place.z, y, j)] = wq_own[...]
    vec_all[mine] = vec_in[...]
    one_all[mine] = one_own[...]
    two_all[mine] = w_outer[...]
    cot_in[r] = cot[own_rows, :]
    for k in range(1, n):
        with jax.named_scope(f"qkv_plane_{k}"):
            for gather in (vec, wq):
                gather.z_done(k)
                gather.y_send(k)
                gather.c_send(0, k, 0)
            vec.x_send(k, 0)
    one.z_sends()
    two.y_send(0)
    for k in range(n):
        with jax.named_scope(f"qkv_side_{k}"):
            for gather in (vec, wq):
                gather.y_done(k)
                gather.c_send(0, k, 1)
            vec.x_send(k, 1)
    with jax.named_scope("qkv_core"):
        for k in range(n):
            for m in range(2):
                for gather in (vec, wq):
                    gather.c_done(0, k, m)
    with jax.named_scope("hidden"):
        send(hid, hid_all.at[1 - r], single, 0, place.to_x()).wait_recv()

    def rest_y(gather, k):
        gather.z_done(k)
        gather.y_send(k)
        gather.x_send(k, 0)
        gather.c_send(0, k, 0)

    def rest_x(gather, k):
        gather.y_done(k)
        gather.x_send(k, 1)
        gather.c_send(0, k, 1)

    def rest_c(gather, k, m):
        gather.x_done(k, m)
        gather.c_send(1, k, m)

    def rest_all(gather):
        for n_at in range(2):
            for k in range(n):
                for m in range(2):
                    if gather is not vec or n_at:
                        gather.c_done(n_at, k, m)

    hid_local = pltpu.make_async_copy(hid_all, hid_out, local.at[2])
    hid_local.start()
    wq_local = pltpu.make_async_copy(wq_all, wq_out, local.at[3])
    wq_local.start()

    kvs = (kv_send, kv_recv)

    def kv_block(i):
        pair, core = lax.div(i, 2), lax.rem(j + lax.rem(i, 2), 2)
        return place.near_block(lax.div(pair, 2), lax.rem(pair, 2), core)

    def kv_move(number, p):
        what = (0, 0, 0, 2, 0, 4, 2, 6)[number]
        if number % 2:
            peer = place.to_core()
        else:
            peer = place.to_y() if number == 2 else place.to_z_near()
        where = kv_block(jnp.int32(what))
        block = kv.at[where, pl.ds(2 * p, 2)]
        return send(block, block, kvs, SPAN * p + number, peer)

    def kv_start(number, p):
        kv_move(number, p).start()

    def kv_here(number, p):
        where = kv_block(jnp.int32(number))
        block = kv.at[where, pl.ds(2 * p, 2)]
        send(block, block, kvs, SPAN * p + number, place.to_core()).wait_recv()

    own_tiles = vec_all[pl.ds(r * size, size)]
    b_query, b_value = spread_rows(own_tiles, (0, 1), HALF // size, HALF)
    own = place.near_block(0, 0, j)
    half = size // 2
    for which in (1, 2, 0):
        columns = slice(which * HALF, (which + 1) * HALF)
        total = dot(hid_all[0], wq_all[:half, :, columns].reshape(HALF, HALF), NN)
        total += dot(hid_all[1], wq_all[half:, :, columns].reshape(HALF, HALF), NN)
        if which == 0:
            total += b_query
        if which == 2:
            total += b_value
        total = total.astype(BF16)
        for p in range(PAIRS):
            piece = total[:, p * 128 : (p + 1) * 128]
            if which == 0:
                lane = lax.broadcasted_iota(jnp.int32, (rows, 128), 1)
                piece = piece * jnp.asarray(0.125, BF16)
                qs[p] = piece
                qm[2 * p] = jnp.where(lane < HEAD_DIM, piece, jnp.zeros_like(piece))
                qm[2 * p + 1] = jnp.where(lane >= HEAD_DIM, piece, jnp.zeros_like(piece))
            else:
                kv[own, 2 * p + which - 1] = piece
        if which == 1:
            with jax.named_scope("after_key"):
                rest_x(one, 0)
        if which == 2:
            with jax.named_scope("after_value"):
                for number in (2, 4, 1):
                    kv_start(number, 0)
                rest_y(one, 1)
    acc[...] = jnp.zeros_like(acc)
    high[...] = jnp.full_like(high, MASKED)
    low[...] = jnp.zeros_like(low)

    q_local = pltpu.make_async_copy(qs, q_out, local.at[4])
    q_local.start()

    def vec_rows():
        for k in range(n):
            for m in range(2):
                rest_c(vec, k, m)

    def two_start():
        two.z_sends()

    events = {}

    def add(step, what, *inputs):
        events.setdefault(step, []).append(functools.partial(what, *inputs))

    add(1, kv_here, 1, 0)
    add(2, kv_here, 2, 0)
    add(2, kv_start, 3, 0)
    add(2, kv_start, 6, 0)
    add(3, kv_here, 3, 0)
    add(3, rest_x, one, 1)
    add(3, rest_y, one, 2)
    add(3, two_start)
    add(4, kv_here, 4, 0)
    add(4, kv_start, 5, 0)
    add(4, rest_y, one, 3)
    add(5, kv_here, 5, 0)
    add(5, kv_start, 2, 1)
    add(5, kv_start, 4, 1)
    add(5, kv_start, 1, 1)
    add(5, vec_rows)
    add(6, kv_here, 6, 0)
    add(6, kv_start, 7, 0)
    add(6, rest_x, two, 0)
    add(7, kv_here, 7, 0)
    add(7, rest_x, one, 2)
    add(8, rest_x, one, 3)
    add(8, rest_c, one, 0, 0)
    add(9, kv_here, 1, 1)
    add(9, rest_c, one, 1, 0)
    add(10, kv_here, 2, 1)
    add(10, kv_start, 3, 1)
    add(10, kv_start, 6, 1)
    add(11, kv_here, 3, 1)
    add(11, rest_y, two, 1)
    add(11, kv_start, 2, 2)
    add(11, kv_start, 4, 2)
    add(11, kv_start, 1, 2)
    add(12, kv_here, 4, 1)
    add(12, kv_start, 5, 1)
    add(13, kv_here, 5, 1)
    add(13, rest_c, one, 0, 1)
    add(13, rest_c, one, 1, 1)
    add(13, rest_y, two, 2)
    add(14, kv_here, 6, 1)
    add(14, kv_start, 7, 1)
    add(14, rest_x, two, 1)
    add(15, kv_here, 7, 1)
    add(15, rest_y, two, 3)
    add(16, rest_c, one, 2, 0)
    add(17, kv_here, 1, 2)
    add(17, rest_c, one, 3, 0)
    add(17, rest_x, two, 2)
    add(18, kv_here, 2, 2)
    add(18, kv_start, 3, 2)
    add(18, kv_start, 6, 2)
    add(19, kv_here, 3, 2)
    add(19, rest_c, one, 2, 1)
    add(20, kv_here, 4, 2)
    add(20, kv_start, 5, 2)
    add(20, rest_x, two, 3)
    add(21, kv_here, 5, 2)
    add(21, rest_c, one, 3, 1)
    add(22, kv_here, 6, 2)
    add(22, kv_start, 7, 2)
    add(22, rest_c, two, 0, 0)
    add(23, kv_here, 7, 2)
    add(23, rest_c, two, 0, 1)

    length = lengths[place.slot]

    def p_copy(t, slot):
        p, i = lax.div(t, SPAN), lax.rem(t, SPAN)
        return pltpu.make_async_copy(
            pbuf.at[slot], p_out.at[kv_block(i), pl.ds(2 * p, 2)], p_sem.at[slot]
        )

    def kv_copy(t):
        p, i = lax.div(t, SPAN), lax.rem(t, SPAN)
        where, both = kv_block(i), pl.ds(2 * p, 2)
        return pltpu.make_async_copy(
            kv.at[where, both], kv_out.at[where, both], local.at[8 + t]
        )

    steps = SPAN * PAIRS
    column = lax.broadcasted_iota(jnp.int32, (1, rows), 1) + place.block * rows
    keep_row = jnp.where(column < length, 1.0, 0.0)

    def to_ctx(p):
        lanes = pl.ds(p * 128, 128)
        return send(
            ctx_tp.at[other_rows, lanes], ctx_in.at[r, :, lanes], single, (2, 5, 6)[p], place.to_x()
        )

    def context(p):
        parts = []
        for h in range(2):
            g = 2 * p + h
            lse_out[g] = high[g] + jnp.log(low[g])
            parts.append(acc[g] / low[g])
        both = jnp.concatenate(parts, axis=0)
        ctxt_out[p] = both
        ctx_tp[:, p * 128 : (p + 1) * 128] = (both * keep_row).T.astype(BF16)
        to_ctx(p).start()
        ctx_in[r, :, p * 128 : (p + 1) * 128] = ctx_tp[own_rows, p * 128 : (p + 1) * 128]

    for p in range(PAIRS - 1):
        add(SPAN * (p + 1), context, p)

    def attend(t, carry):
        p, i = lax.div(t, SPAN), lax.rem(t, SPAN)
        for step, calls in sorted(events.items()):

            @pl.when(t == step)
            def _(calls=calls):
                for call in calls:
                    with jax.named_scope(f"at_{step}"):
                        call()

        kv_copy(t).start()

        slot = lax.rem(t, 2)

        @pl.when(t >= 2)
        def _():
            p_copy(t - 2, slot).wait()

        where = kv_block(i)
        place_of = lax.broadcasted_iota(jnp.int32, (rows, 128), 0) + where * rows
        bias = jnp.where(place_of < length, 0.0, MASKED)
        bias = jnp.concatenate([bias] * (rows // 128), axis=1)
        key = kv[where, 2 * p]
        value_t = kv[where, 2 * p + 1].T
        for h in range(2):
            g = 2 * p + h
            scores = dot(key, qm[g], NT) + bias
            top = jnp.max(scores, axis=0, keepdims=True)
            weights = jnp.exp(scores - top)
            below = jnp.sum(weights, axis=0, keepdims=True)
            rounded = weights.astype(BF16)
            pbuf[slot, h] = rounded
            term = dot(value_t[h * HEAD_DIM : (h + 1) * HEAD_DIM], rounded, NN)
            old = high[g]
            new = jnp.maximum(old, top)
            keep_old, keep_new = jnp.exp(old - new), jnp.exp(top - new)
            high[g] = new
            low[g] = low[g] * keep_old + below * keep_new
            acc[g] = acc[g] * keep_old + term * keep_new
            m_out[where, g] = top
        p_copy(t, slot).start()
        return carry

    lax.fori_loop(0, steps, attend, jnp.int32(0))

    context(PAIRS - 1)
    for number in range(3):
        leave(number).start()
    for t in (steps - 2, steps - 1):
        p_copy(jnp.int32(t), t % 2).wait()
    with jax.named_scope("one_all"):
        rest_all(vec)
        rest_all(one)
    six = spread_rows(vec_all[...], (2, 3, 4, 5, 6, 7), HALF // size, D)
    b_output, b_outer, gain_one, shift_one, gain_two, shift_two = six
    (b_inner,) = spread_rows(vec_all[...], (8,), FF_HALF // size, 2 * FF_HALF)
    hidden = jnp.concatenate([hid_all[0, own_rows, :], hid_all[1, own_rows, :]], axis=1)
    with jax.named_scope("context"):
        for p in range(PAIRS):
            lanes = pl.ds(p * 128, 128)
            send(
                ctx_tp.at[other_rows, lanes], ctx_in.at[1 - r, :, lanes], single, (2, 5, 6)[p], place.to_x()
            ).wait_recv()

    def weight(ref, h, columns):
        block = ref[h * size : (h + 1) * size, :, columns]
        return block.reshape(D, block.shape[2])

    out_cols, in_cols, all_cols = slice(0, HALF), slice(HALF, FIRST), slice(0, FF_HALF)
    with jax.named_scope("middle_one"):
        attn = dot(ctx_in[0], weight(one_all, 0, out_cols), NT)
        attn += dot(ctx_in[1], weight(one_all, 1, out_cols), NT) + b_output
        normed, normal, scale_one = norm_forward(hidden.astype(F32) + attn, gain_one, shift_one)
        normed_ref[...] = normed
        normal_ref[...] = normal
        low_ref[...] = normed.astype(BF16)
    with jax.named_scope("two_late"):
        rest_c(two, 1, 0)
        rest_c(two, 1, 1)
    for h in range(2):
        with jax.named_scope(f"inner_{h}"):
            span = slice(h * FF_HALF, (h + 1) * FF_HALF)
            inner = dot(low_ref[...], weight(one_all, h, in_cols), NN) + b_inner[:, span]
            value, slope = gelu_both(inner)
            act_ref[:, span] = value.astype(BF16)
            slope_ref[:, span] = slope
    with jax.named_scope("two_all"):
        for k in range(2, n):
            for m in range(2):
                rest_c(two, k, m)
        rest_all(two)
    with jax.named_scope("outer"):
        outer = dot(act_ref[:, :FF_HALF], weight(two_all, 0, all_cols), NT)
        outer += dot(act_ref[:, FF_HALF:], weight(two_all, 1, all_cols), NT) + b_outer
        result, normal_two, scale_two = norm_forward(normed_ref[...] + outer, gain_two, shift_two)
        lay_out[0] = result[:, :HALF].astype(BF16)
        lay_out[1] = result[:, HALF:].astype(BF16)
    to_lay = send(lay_out.at[1 - r], lay_far.at[r], single, 3, place.to_x())
    to_lay.start()
    spot = lax.broadcasted_iota(jnp.int32, (part, 1), 0) + place.block * rows + r * part
    keep = jnp.where(spot < length, 1.0, 0.0)
    with jax.named_scope("cotangent"):
        send(cot.at[other_rows], cot_in.at[1 - r], single, 1, place.to_x()).wait_recv()
    with jax.named_scope("norm_two"):
        seed = jnp.concatenate([cot_in[0], cot_in[1]], axis=1).astype(F32) * keep
        d_two, g_gain_two, g_shift_two = norm_backward(seed, normal_two, scale_two, gain_two)
        d_outer = d_two.astype(BF16)
        small_out[4:5] = g_gain_two
        small_out[5:6] = g_shift_two
        small_out[1:2] = jnp.sum(d_outer.astype(F32), axis=0, keepdims=True)
    d_normed = d_two
    d_outer_t = d_outer.T
    for h in range(2):
        with jax.named_scope(f"d_inner_{h}"):
            span = slice(h * FF_HALF, (h + 1) * FF_HALF)
            d_inner = dot(d_outer, weight(two_all, h, all_cols), NN) * slope_ref[:, span]
            d_inner = d_inner.astype(BF16)
            d_ref[:, span] = d_inner
            sums = jnp.sum(d_inner.astype(F32), axis=0, keepdims=True)
            small_out[6 + 2 * h : 7 + 2 * h] = sums[:, :D]
            small_out[7 + 2 * h : 8 + 2 * h] = sums[:, D:]
            d_normed += dot(d_inner, weight(one_all, h, in_cols), NT)
    with jax.named_scope("all_sent"):
        for gather in (vec, wq, one, two):
            gather.all_sent()
    own_col = pl.ds(pl.multiple_of(r * HALF, HALF), HALF)

    def give(number, ref, h, columns, target):
        return pltpu.make_async_copy(
            ref.at[pl.ds(h * size, size), :, columns],
            g_out.at[pl.ds(h * size, size), :, target],
            local.at[8 + SPAN * PAIRS + number],
        )

    gives = []
    for h in range(2):
        with jax.named_scope(f"g_outer_{h}"):
            span = slice(h * FF_HALF, (h + 1) * FF_HALF)
            term = dot(d_outer_t, act_ref[:, span], NN).astype(BF16)
            two_all[h * size : (h + 1) * size] = term.reshape(size, blk, FF_HALF)
            copy = give(h, two_all, h, pl.ds(0, FF_HALF), pl.ds(FIRST, FF_HALF))
            copy.start()
            gives.append(copy)
    with jax.named_scope("norm_one"):
        d_one, g_gain_one, g_shift_one = norm_backward(d_normed, normal_ref[...], scale_one, gain_one)
        d_attn = d_one.astype(BF16)
        small_out[2:3] = g_gain_one
        small_out[3:4] = g_shift_one
        small_out[0:1] = jnp.sum(d_attn.astype(F32), axis=0, keepdims=True)
        small_out[10:16] = jnp.zeros((6, D), F32)
        for h in range(2):
            low_out[h] = d_attn[:, h * HALF : (h + 1) * HALF]
        normed_ref[...] = d_one
        own_out[...] = normed_ref[:, own_col]
        for number in (4, 5, 7):
            leave(number).start()
    with jax.named_scope("d_context"):
        to_lay.wait_send()
        final_out[own_rows, :] = lay_out[r]
        for h in range(2):
            d_context = dot(d_attn, weight(one_all, h, out_cols), NN) * keep
            lay_out[h] = d_context.astype(BF16)
        to_d = send(lay_out.at[1 - r], d_out.at[own_rows], single, 4, place.to_x())
        to_d.start()
        d_out[own_rows, :] = lay_out[r]
    low_t = low_ref[...].T
    d_attn_t = d_attn.T
    for h in range(2):
        with jax.named_scope(f"g_inner_{h}"):
            span = slice(h * FF_HALF, (h + 1) * FF_HALF)
            term = dot(low_t, d_ref[:, span], NN).astype(BF16)
            one_all[h * size : (h + 1) * size, :, HALF:] = term.reshape(size, blk, FF_HALF)
            term = dot(d_attn_t, ctx_in[h], NN).astype(BF16)
            one_all[h * size : (h + 1) * size, :, :HALF] = term.reshape(size, blk, HALF)
            copy = give(2 + h, one_all, h, pl.ds(0, FIRST), pl.ds(0, FIRST))
            copy.start()
            gives.append(copy)
    for number in range(1, SPAN):
        for p in range(PAIRS):
            kv_move(number, p).wait_send()
    send(lay_far.at[r], lay_far.at[1 - r], single, 3, place.to_x()).wait_recv()
    final_out[other_rows, :] = lay_far[1 - r]
    leave(3).start()
    send(hid, hid, single, 0, place.to_x()).wait_send()
    send(ctx_in.at[0], ctx_in.at[0], single, 1, place.to_x()).wait_send()
    for p in range(PAIRS):
        to_ctx(p).wait_send()
    to_d.wait_send()
    send(lay_out.at[1 - r], d_out.at[other_rows], single, 4, place.to_x()).wait_recv()
    leave(6).start()
    for copy in [hid_local, wq_local, q_local] + gives:
        copy.wait()
    for t in range(SPAN * PAIRS):
        kv_copy(jnp.int32(t)).wait()


def forward_attention(size, lengths, hid, qkv_weights, rest_weights, vec, cot):
    rows = hid.shape[0]
    part = rows // 2
    blk = qkv_weights[0].shape[0]
    n = size // 4
    any_space = pl.BlockSpec(memory_space=pl.ANY)
    vmem = pl.BlockSpec(memory_space=pltpu.VMEM)
    shape = jax.ShapeDtypeStruct
    n_col, n_all = (n - 1) + n + 2 * n, (n - 1) + n + 2 * n + 4 * n
    dma = pltpu.SemaphoreType.DMA
    scratch = pltpu.VMEM
    results = (
        shape((2, rows, HALF), BF16),
        shape((size, blk, QKV), BF16),
        shape((PAIRS, rows, 128), BF16),
        shape((SPAN, 2 * PAIRS, rows, 128), BF16),
        shape((SPAN, 2 * PAIRS, rows, rows), BF16),
        shape((SPAN, 2 * PAIRS, 1, rows), F32),
        shape((2 * PAIRS, 1, rows), F32),
        shape((PAIRS, 128, rows), F32),
        shape((2 * size, blk, REST), BF16),
        shape((rows, HALF), BF16),
        shape((2, part, HALF), BF16),
        shape((part, HALF), F32),
        shape((rows, HALF), BF16),
        shape((16, D), F32),
    )
    picks = (5, 6, 7, 9, 10, 11, 12, 13)
    return pl.pallas_call(
        functools.partial(staged, kernel_a, size, 10, len(results), picks),
        out_shape=results,
        in_specs=[pl.BlockSpec(memory_space=pltpu.SMEM)] + [vmem] * 9,
        out_specs=[any_space] * len(results),
        scratch_shapes=[scratch(results[at].shape, results[at].dtype) for at in picks]
        + [dma((len(picks),))]
        + [
            scratch((2, rows, HALF), BF16),
            scratch((blk, QKV), BF16),
            scratch((size, blk, QKV), BF16),
            scratch((2 * size, 16, 128), BF16),
            scratch((blk, FIRST), BF16),
            scratch((2 * size, blk, FIRST), BF16),
            scratch((2 * size, blk, FF_HALF), BF16),
            scratch((SPAN, 2 * PAIRS, rows, 128), BF16),
            scratch((PAIRS, rows, 128), BF16),
            scratch((2 * PAIRS, rows, 128), BF16),
            scratch((2 * PAIRS, HEAD_DIM, rows), F32),
            scratch((2 * PAIRS, 1, rows), F32),
            scratch((2 * PAIRS, 1, rows), F32),
            scratch((2, 2, rows, rows), BF16),
            scratch((rows, HALF), BF16),
            scratch((2, part, HALF), BF16),
            scratch((2, part, HALF), BF16),
            scratch((2, part, HALF), BF16),
            scratch((2, part, HALF), BF16),
            scratch((part, D), F32),
            scratch((part, D), F32),
            scratch((part, D), BF16),
            scratch((part, 2 * FF_HALF), F32),
            scratch((part, 2 * FF_HALF), BF16),
            scratch((part, 2 * FF_HALF), BF16),
            dma((n_all,)),
            dma((n_all,)),
            dma((n_all,)),
            dma((n_all,)),
            dma((n_col,)),
            dma((n_col,)),
            dma((n_all,)),
            dma((n_all,)),
            dma((SPAN * PAIRS,)),
            dma((SPAN * PAIRS,)),
            dma((7,)),
            dma((7,)),
            dma((12 + SPAN * PAIRS,)),
            dma((2,)),
        ],
        compiler_params=pltpu.CompilerParams(
            collective_id=0, has_side_effects=True, vmem_limit_bytes=62 * 2**20
        ),
        name="forward_attention",
    )(lengths, hid, *qkv_weights, *rest_weights, vec, cot)


def kernel_c(
    size,
    leave,
    d_ctx,
    qs,
    m_in,
    lse_in,
    ctxt,
    hid_all,
    wq_all,
    dres_low,
    dres_own,
    small_in,
    kv_in,
    p_in,
    g_in,
    query_out,
    key_out,
    value_out,
    wo_out,
    wi_out,
    wu_out,
    small_out,
    bias_out,
    grad_out,
    dtot,
    delta,
    qm,
    acc,
    kv,
    pbuf,
    big,
    cb,
    rb,
    st,
    b1,
    b2,
    b3,
    b4,
    d_all,
    hid_t,
    far,
    gq,
    q1,
    q2,
    q3,
    near,
    bias_own,
    bias_got,
    vec_sum,
    vec_got,
    one_send,
    one_recv,
    kv_send,
    kv_recv,
    g_send,
    g_recv,
    q_send,
    q_recv,
    s_send,
    s_recv,
    v_send,
    v_recv,
    load,
    p_sem,
):
    place = Place(size)
    rows = qs.shape[1]
    part = rows // 2
    n = place.planes
    r, y, j = place.r, place.y, place.j
    half = size // 2
    blk = wq_all.shape[1]
    own_rows = pl.ds(pl.multiple_of(r * part, part), part)

    def b_block(i):
        pair, core = lax.div(i, 2), lax.rem(j + 1 + lax.rem(i, 2), 2)
        return place.near_block(1 - lax.div(pair, 2), 1 - lax.rem(pair, 2), core)

    def kv_load(i):
        return pltpu.make_async_copy(kv_in.at[b_block(i)], kv.at[i], load.at[i])

    def p_load(t, slot):
        p, i = lax.div(t, SPAN), lax.rem(t, SPAN)
        return pltpu.make_async_copy(
            p_in.at[b_block(i), pl.ds(2 * p, 2)], pbuf.at[slot], p_sem.at[slot]
        )

    def index(other, k, m):
        return 2 * n * other + 2 * ((k + n - 1) % n) + m

    def g_block(at, core):
        n_at, m = at // (2 * n), at % 2
        k = ((at % (2 * n)) // 2 + 1) % n
        return place.any_block(
            lax.rem(r + 1 + n_at, 2), place.plane(k), lax.rem(y + 1 + m, 2), core
        )

    def g_load(at):
        return pltpu.make_async_copy(g_in.at[g_block(at, j)], st.at[at], load.at[8 + at])

    def loop(count, body):
        def step(at, carry):
            body(at)
            return carry

        lax.fori_loop(0, count, step, jnp.int32(0))

    needed = [(0, 2, 0), (0, 1, 0), (0, 2, 1), (1, 1, 0), (0, 3, 0), (0, 3, 1), (1, 2, 0), (1, 2, 1)]
    needed += [(0, 1, 1), (1, 1, 1), (0, 0, 0), (0, 0, 1), (1, 3, 0), (1, 3, 1), (1, 0, 0), (1, 0, 1)]
    needed = [index(*at) for at in needed]
    p_load(jnp.int32(0), 0).start()
    for at in needed[:4]:
        g_load(at).start()
    loop(SPAN, lambda i: kv_load(i).start())
    for at in needed[4:]:
        g_load(at).start()
    lane = lax.broadcasted_iota(jnp.int32, (rows, 128), 1)
    for p in range(PAIRS):
        piece = qs[p]
        qm[2 * p] = jnp.where(lane < HEAD_DIM, piece, jnp.zeros_like(piece))
        qm[2 * p + 1] = jnp.where(lane >= HEAD_DIM, piece, jnp.zeros_like(piece))
    acc[...] = jnp.zeros_like(acc)
    for which in range(2):
        hid_t[which] = hid_all[which].T
    far[...] = jnp.zeros_like(far)
    far[own_rows, :] = dres_low[1 - r].astype(F32)
    grad_out[...] = jnp.zeros_like(grad_out)
    grad_out[own_rows, :] = dres_own[...]
    upper = lax.broadcasted_iota(jnp.int32, (128, rows), 0) < HEAD_DIM
    for p in range(PAIRS):
        turned = d_ctx[:, p * 128 : (p + 1) * 128].astype(F32).T
        product = turned * ctxt[p]
        delta[2 * p] = jnp.sum(product[:HEAD_DIM], axis=0, keepdims=True)
        delta[2 * p + 1] = jnp.sum(product[HEAD_DIM:], axis=0, keepdims=True)
        dtot[2 * p] = jnp.where(upper, turned, 0.0)
        dtot[2 * p + 1] = jnp.where(upper, 0.0, turned)
    with jax.named_scope("meet"):
        meet(place)
    single = (one_send, one_recv)
    gs = (g_send, g_recv)
    ks = (kv_send, kv_recv)
    at_x, at_y, at_z = 4 * n, 6 * n, 8 * n

    send(small_in, vec_got.at[0], (v_send, v_recv), 0, place.to_x()).start()

    def c_move(at):
        return send(g_in.at[g_block(at, 1 - j)], b1.at[at], gs, at, place.to_core())

    for at in needed:
        c_move(at).start()

    def fold(target, source, at):
        total = target[at].astype(F32) + source.astype(F32)
        target[at] = total.astype(BF16)

    def pieces(p):
        return pl.ds(2 * p, 2)

    def core_send(p, pair):
        return send(
            big.at[2 * pair, pieces(p)], cb.at[pair, pieces(p)], ks, 4 * p + pair, place.to_core()
        )

    def core_add(p, pair):
        core_send(p, pair).wait_recv()
        for piece in (2 * p, 2 * p + 1):
            fold(big, cb[pair, piece], (2 * pair + 1, piece))

    def hop(p, pair):
        peer = place.to_y() if pair == 2 else place.to_z_near()
        number = 4 * PAIRS + 3 * p + pair
        return send(big.at[2 * pair + 1, pieces(p)], rb.at[pair, pieces(p)], ks, number, peer)

    def hop_add(p):
        hop(p, 0).wait_recv()
        for piece in (2 * p, 2 * p + 1):
            fold(big, rb[0, piece], (5, piece))

    def g_core_add(other, k, m):
        at = index(other, k, m)
        c_move(at).wait_recv()
        g_load(at).wait()
        fold(st, b1[at], at)

    def gx(k, m):
        at = index(0, k, m)
        return send(st.at[at], b2.at[at], gs, at_x + at, place.to_x())

    def gx_add(k, m):
        gx(k, m).wait_recv()
        fold(st, b2[index(0, k, m)], index(1, k, m))

    def gy(k, other):
        slot = 2 * k + other
        return send(st.at[index(other, k, 0)], b3.at[slot], gs, at_y + slot, place.to_y())

    def gy_add(k, other):
        gy(k, other).wait_recv()
        fold(st, b3[2 * k + other], index(other, k, 1))

    def gz(k):
        return send(st.at[index(1, k, 1)], b4.at[k - 1], gs, at_z + k - 1, place.to_z(k))

    vz = (v_send, v_recv)

    def vector(number):
        level = min(number, 3)
        step = max(number - 2, 1)
        peer = (place.to_x(), place.to_core(), place.to_y(), place.to_z(step))[level]
        source = small_in if level == 0 else vec_sum.at[level - 1]
        return send(source, vec_got.at[number], vz, number, peer)

    def vector_add(level):
        vector(level).wait_recv()
        before = small_in[...] if level == 0 else vec_sum[level - 1]
        vec_sum[level] = before + vec_got[level]

    qz = (q_send, q_recv)

    def q_core(p):
        return send(gq.at[p, 1 - j], q1.at[p], qz, (n + 1) * p, place.to_core())

    def q_side(p):
        return send(gq.at[p, j, 1 - y], q2.at[p], qz, (n + 1) * p + 1, place.to_y())

    def q_plane(p, k):
        return send(
            gq.at[p, j, y, place.plane(k)], q3.at[p, k - 1], qz, (n + 1) * p + 1 + k, place.to_z(k)
        )

    def q_core_add(p):
        q_core(p).wait_recv()
        for side in range(2):
            fold(gq, q1[p, side], (p, j, side))

    def q_side_add(p):
        q_side(p).wait_recv()
        fold(gq, q2[p], (p, j, y))

    def q_planes(p):
        for k in range(1, n):
            q_plane(p, k).start()

    def settle(p):
        core_send(p, 3).wait_recv()
        hop(p, 1).wait_recv()
        hop(p, 2).wait_recv()
        both = jnp.concatenate([acc[2 * p], acc[2 * p + 1]], axis=0)
        d_query = (both.T * 0.125).astype(BF16)
        d_all[p, :, 0:128] = d_query
        lanes = slice(p * 128, (p + 1) * 128)
        bias_own[0, 0:1, lanes] = jnp.sum(d_query.astype(F32), axis=0, keepdims=True)
        for at in range(2):
            piece = 2 * p + at
            total = big[7, piece].astype(F32) + cb[3, piece].astype(F32)
            total += rb[1, piece].astype(F32) + rb[2, piece].astype(F32)
            low = total.astype(BF16)
            d_all[p, :, (at + 1) * 128 : (at + 2) * 128] = low
        bias_own[0, 1:2, lanes] = jnp.sum(low.astype(F32), axis=0, keepdims=True)

    def input_term(p, which):
        parts = []
        for at in range(3):
            columns = slice(at * HALF + p * 128, at * HALF + (p + 1) * 128)
            parts.append(wq_all[pl.ds(which * half, half), :, columns].reshape(HALF, 128))
        return dot(d_all[p], jnp.concatenate(parts, axis=1), NT)

    def far_term(p):
        far[...] = far[...] + input_term(p, 1 - r)

    def own_term(p):
        grad_out[...] = grad_out[...] + input_term(p, r)

    def grads(p):
        for which in range(2):
            term = dot(hid_t[which], d_all[p], NN).astype(BF16)
            for b in range(half):
                c = which * half + b
                gq[p, c % 2, (c // 2) % 2, c // 4] = term[b * blk : (b + 1) * blk]

    events = {}

    def add(step, what, *inputs):
        events.setdefault(step, []).append(functools.partial(what, *inputs))

    def start(step, what, *inputs):
        add(step, lambda: what(*inputs).start())

    bias_own[0, 2:8] = jnp.zeros((6, HALF), F32)
    add(0, g_core_add, 0, 2, 0)
    start(0, gx, 2, 0)
    add(0, g_core_add, 0, 1, 0)
    start(0, gy, 1, 0)
    add(1, g_core_add, 0, 2, 1)
    add(1, g_core_add, 1, 1, 0)
    start(2, gx, 2, 1)
    start(2, gy, 1, 1)
    add(2, g_core_add, 0, 3, 0)
    add(3, vector_add, 0)
    start(3, vector, 1)
    start(3, gx, 3, 0)
    add(3, g_core_add, 0, 3, 1)
    late = [(1, 2, 0), (1, 2, 1), (0, 1, 1), (1, 1, 1), (0, 0, 0), (0, 0, 1), (1, 3, 0), (1, 3, 1)]
    for at, what in enumerate(late + [(1, 0, 0), (1, 0, 1)]):
        add(4 + at, g_core_add, *what)
    add(6, vector_add, 1)
    start(6, vector, 2)
    add(8, gx_add, 2, 0)
    add(8, gy_add, 1, 0)
    add(9, gx_add, 2, 1)
    start(9, gy, 2, 1)
    add(9, gy_add, 1, 1)
    start(10, gx, 1, 1)
    start(10, gx, 3, 1)
    start(10, gx, 0, 0)
    start(11, gx, 0, 1)
    add(11, vector_add, 2)
    for step in range(1, n):
        start(11, vector, 2 + step)
    add(15, gy_add, 2, 1)
    start(15, gz, 2)
    add(18, gx_add, 1, 1)
    add(19, gx_add, 3, 0)
    add(19, gx_add, 3, 1)
    start(19, gy, 3, 1)
    for p in range(PAIRS):
        base = SPAN * p
        late = 7 if p == PAIRS - 1 else 8
        start(base + 2, core_send, p, 0)
        add(base + 3, core_add, p, 0)
        start(base + 3, hop, p, 0)
        start(base + 4, core_send, p, 1)
        add(base + 5, core_add, p, 1)
        start(base + 5, hop, p, 1)
        start(base + 6, core_send, p, 2)
        add(base + 7, core_add, p, 2)
        add(base + late, hop_add, p)
        start(base + late, hop, p, 2)
        start(base + 8, core_send, p, 3)
        if p < PAIRS - 1:
            add(base + 14, settle, p)
            add(base + 14, grads, p)
            start(base + 14, q_core, p)
            add(base + 15, far_term, p)
            add(base + 15, own_term, p)
            add(base + 15, q_core_add, p)

    steps = SPAN * PAIRS

    def back(t, carry):
        p, i = lax.div(t, SPAN), lax.rem(t, SPAN)
        for step, calls in sorted(events.items()):
            if step < steps:

                @pl.when(t == step)
                def _(calls=calls):
                    with jax.named_scope(f"step_{step}"):
                        for call in calls:
                            call()

        slot = lax.rem(t, 2)

        @pl.when(t + 1 < steps)
        def _():
            p_load(t + 1, 1 - slot).start()

        @pl.when(p == 0)
        def _():
            kv_load(i).wait()

        p_load(t, slot).wait()
        where = b_block(i)
        key = kv[i, 2 * p]
        value = kv[i, 2 * p + 1]
        key_t = key.T
        d_key = d_value = None
        for h in range(2):
            g = 2 * p + h
            factor = jnp.exp(m_in[where, g] - lse_in[g])
            d_rows = (dtot[g] * factor).astype(BF16)
            weights = pbuf[slot, h]
            d_probs = dot(value, d_rows, NN)
            d_scores = (weights.astype(F32) * (d_probs - delta[g] * factor)).astype(BF16)
            value_term = dot(weights, d_rows, NT)
            key_term = dot(d_scores, qm[g], NN)
            acc[g] += dot(key_t[h * HEAD_DIM : (h + 1) * HEAD_DIM], d_scores, NN)
            d_key = key_term if d_key is None else d_key + key_term
            d_value = value_term if d_value is None else d_value + value_term
        big[i, 2 * p] = d_key.astype(BF16)
        big[i, 2 * p + 1] = d_value.astype(BF16)
        return carry

    lax.fori_loop(0, steps, back, jnp.int32(0))

    last = PAIRS - 1
    for call in events[steps]:
        call()
    gz(1).start()
    q_side(0).start()
    q_side(1).start()
    with jax.named_scope("settle"):
        settle(last)
    with jax.named_scope("far"):
        far_term(last)
        near[0] = far[...].astype(BF16)
    to_near = send(near.at[0], near.at[1], single, 0, place.to_x())
    with jax.named_scope("grads"):
        grads(last)
    to_near.start()
    q_core(last).start()
    sz = (s_send, s_recv)

    def small(number):
        level = min(number, 2)
        peer = (place.to_core(), place.to_y(), place.to_z(max(number - 1, 1)))[level]
        return send(bias_own.at[level], bias_got.at[number], sz, number, peer)

    small(0).start()
    with jax.named_scope("own"):
        own_term(last)
    with jax.named_scope("q_core"):
        q_core_add(last)
        small(0).wait_recv()
        bias_own[1] = bias_own[0] + bias_got[0]
    q_side(last).start()
    small(1).start()
    with jax.named_scope("g_x_0"):
        gx_add(0, 0)
        gx_add(0, 1)
    gy(0, 1).start()
    with jax.named_scope("g_y_3"):
        gy_add(3, 1)
    gz(3).start()
    with jax.named_scope("q_side_0"):
        q_side_add(0)
        q_planes(0)
    with jax.named_scope("q_side_1"):
        q_side_add(1)
        q_planes(1)
    with jax.named_scope("q_side_2"):
        q_side_add(last)
        q_planes(last)
        small(1).wait_recv()
        bias_own[2] = bias_own[1] + bias_got[1]
    for step in range(1, n):
        small(1 + step).start()
    with jax.named_scope("vectors"):
        total = vec_sum[2]
        for step in range(1, n):
            vector(2 + step).wait_recv()
            total = total + vec_got[2 + step]
        small_out[...] = total
        leave(6).start()

    def q_out(p):
        total = gq[p, j, y, place.z].astype(F32)
        for k in range(1, n):
            q_plane(p, k).wait_recv()
            total = total + q3[p, k - 1].astype(F32)
        lanes = slice(p * 128, (p + 1) * 128)
        query_out[:, lanes] = total[:, :128]
        key_out[:, lanes] = total[:, 128:256]
        value_out[:, lanes] = total[:, 256:]

    with jax.named_scope("q_out_0"):
        q_out(0)
    with jax.named_scope("near_wait"):
        to_near.wait_recv()
        grad_out[...] = grad_out[...] + near[1].astype(F32)
        leave(8).start()
    with jax.named_scope("g_z"):
        total = None
        for k in range(1, n):
            gz(k).wait_recv()
            got = b4[k - 1].astype(F32)
            total = got if total is None else total + got
    with jax.named_scope("g_y_0"):
        gy_add(0, 1)
        total = total + st[index(1, 0, 1)].astype(F32)
        wo_out[...] = total[:, :HALF]
        wi_out[...] = total[:, HALF:FIRST]
        wu_out[...] = total[:, FIRST:]
        for number in (3, 4, 5):
            leave(number).start()
    with jax.named_scope("q_out"):
        q_out(1)
        q_out(last)
        for number in range(3):
            leave(number).start()
        total = bias_own[2]
        for step in range(1, n):
            small(1 + step).wait_recv()
            total = total + bias_got[1 + step]
        bias_out[...] = total
        leave(7).start()

    for at in range(4 * n):
        c_move(at).wait_send()
    for k in range(n):
        first = k == 1
        for m in range(2):
            if not first or m == 1:
                gx(k, m).wait_send()
            if first or m == 1:
                gy(k, m).wait_send()
    for k in range(1, n):
        gz(k).wait_send()
        small(1 + k).wait_send()
        for p in range(PAIRS):
            q_plane(p, k).wait_send()
    small(0).wait_send()
    small(1).wait_send()
    for number in range(n + 2):
        vector(number).wait_send()
    for p in range(PAIRS):
        q_core(p).wait_send()
        q_side(p).wait_send()
        for pair in range(4):
            core_send(p, pair).wait_send()
        for pair in range(3):
            hop(p, pair).wait_send()
    to_near.wait_send()


def backward_attention(
    size, dctx, qs, m_in, lse_in, ctxt, hid_all, wq_all, dres_low, dres_own, small_in, kv_in, p_in, g_in
):
    rows = qs.shape[1]
    part = rows // 2
    blk = wq_all.shape[1]
    n = size // 4
    any_space = pl.BlockSpec(memory_space=pl.ANY)
    vmem = pl.BlockSpec(memory_space=pltpu.VMEM)
    shape = jax.ShapeDtypeStruct
    dma = pltpu.SemaphoreType.DMA
    scratch = pltpu.VMEM
    g_count, q_count = 4 * n + 2 * n + 2 * n + n - 1, PAIRS * (n + 1)
    results = (
        shape((blk, HALF), F32),
        shape((blk, HALF), F32),
        shape((blk, HALF), F32),
        shape((blk, HALF), F32),
        shape((blk, FF_HALF), F32),
        shape((blk, FF_HALF), F32),
        shape((16, D), F32),
        shape((8, HALF), F32),
        shape((rows, HALF), F32),
    )
    return pl.pallas_call(
        functools.partial(staged, kernel_c, size, 13, len(results), range(len(results))),
        out_shape=results,
        in_specs=[vmem] * 10 + [any_space] * 3,
        out_specs=[any_space] * len(results),
        scratch_shapes=[scratch(a.shape, a.dtype) for a in results]
        + [dma((len(results),))]
        + [
            scratch((2 * PAIRS, 128, rows), F32),
            scratch((2 * PAIRS, 1, rows), F32),
            scratch((2 * PAIRS, rows, 128), BF16),
            scratch((2 * PAIRS, HEAD_DIM, rows), F32),
            scratch((SPAN, 2 * PAIRS, rows, 128), BF16),
            scratch((2, 2, rows, rows), BF16),
            scratch((SPAN, 2 * PAIRS, rows, 128), BF16),
            scratch((4, 2 * PAIRS, rows, 128), BF16),
            scratch((3, 2 * PAIRS, rows, 128), BF16),
            scratch((4 * n, blk, REST), BF16),
            scratch((4 * n, blk, REST), BF16),
            scratch((2 * n, blk, REST), BF16),
            scratch((2 * n, blk, REST), BF16),
            scratch((n - 1, blk, REST), BF16),
            scratch((PAIRS, rows, HALF), BF16),
            scratch((2, HALF, rows), BF16),
            scratch((rows, HALF), F32),
            scratch((PAIRS, 2, 2, n, blk, HALF), BF16),
            scratch((PAIRS, 2, n, blk, HALF), BF16),
            scratch((PAIRS, n, blk, HALF), BF16),
            scratch((PAIRS, n - 1, blk, HALF), BF16),
            scratch((2, rows, HALF), BF16),
            scratch((3, 8, HALF), F32),
            scratch((n + 1, 8, HALF), F32),
            scratch((3, 16, D), F32),
            scratch((n + 2, 16, D), F32),
            dma((1,)),
            dma((1,)),
            dma((7 * PAIRS,)),
            dma((7 * PAIRS,)),
            dma((g_count,)),
            dma((g_count,)),
            dma((q_count,)),
            dma((q_count,)),
            dma((n + 1,)),
            dma((n + 1,)),
            dma((n + 2,)),
            dma((n + 2,)),
            dma((9 + 4 * n,)),
            dma((2,)),
        ],
        compiler_params=pltpu.CompilerParams(
            collective_id=1, has_side_effects=True, vmem_limit_bytes=63 * 2**20
        ),
        name="backward_attention",
    )(dctx, qs, m_in, lse_in, ctxt, hid_all, wq_all, dres_low, dres_own, small_in, kv_in, p_in, g_in)


def kernel_d(size, per, count, *refs):
    sources, targets = refs[:count], refs[count : 2 * count - 2]
    vectors = refs[2 * count - 2 : 2 * count + 7]
    held, come, go = refs[2 * count + 7 : 3 * count + 7], refs[-2], refs[-1]
    small, bias = held[0], held[1]
    loads = [pltpu.make_async_copy(s, h, come.at[at]) for at, (s, h) in enumerate(zip(sources, held))]
    stores = [pltpu.make_async_copy(h, t, go.at[at]) for at, (h, t) in enumerate(zip(held[2:], targets))]
    for copy in loads:
        copy.start()
    loads[0].wait()
    loads[1].wait()
    row = lax.axis_index("row")
    inside = lax.rem(lax.axis_index("col"), size)
    start = row * HALF + inside * per
    lines = small[...]
    turned = pltpu.roll(lines, D - start, 1)
    for at in range(6):
        vectors[at][...] = turned[at, :per]
    spot = inside * 4 * per
    hidden = pltpu.roll(lines, D - lax.rem(spot, D), 1)[:, :128]
    wanted = 6 + 2 * row + lax.div(spot, D)
    line = lax.broadcasted_iota(jnp.int32, hidden.shape, 0)
    vectors[6][...] = jnp.sum(jnp.where(line == wanted, hidden, 0.0), axis=0)[: 4 * per]
    turned = pltpu.roll(bias[...], HALF - inside * per, 1)
    for at in range(2):
        vectors[7 + at][...] = turned[at, :per]
    for load, store in zip(loads[2:], stores):
        load.wait()
        store.start()
    for store in stores:
        store.wait()


def finish(size, small, bias, arrays):
    space = pl.BlockSpec(memory_space=pl.ANY)
    shapes = [jax.ShapeDtypeStruct(a.shape, a.dtype) for a in arrays]
    arrays = [small, bias] + arrays
    count = len(arrays)
    return pl.pallas_call(
        functools.partial(kernel_d, size, HALF // size, count),
        out_shape=shapes
        + [jax.ShapeDtypeStruct((HALF // size * (4 if at == 6 else 1),), F32) for at in range(9)],
        in_specs=[space] * count,
        out_specs=[space] * (count - 2) + [pl.BlockSpec(memory_space=pltpu.VMEM)] * 9,
        scratch_shapes=[pltpu.VMEM(a.shape, a.dtype) for a in arrays]
        + [pltpu.SemaphoreType.DMA((count,))] * 2,
        compiler_params=pltpu.CompilerParams(vmem_limit_bytes=63 * 2**20),
        name="finish",
    )(*arrays)


def per_device(group, hidden_in, cotangent, lengths, *params):
    w_query, w_key, w_value, w_output, w_inner, w_outer = params[:6]
    b_query, b_value, b_output, b_inner, b_outer = params[6:11]
    gain_one, shift_one, gain_two, shift_two = params[11:]
    cols = lax.axis_size("col")
    size = group
    ways = cols // size
    inside = lax.axis_index("col") % size
    row = lax.axis_index("row")

    def regroup(block):
        if ways == 1:
            return block
        whole = lax.all_gather(block, "col", axis=0, tiled=True)
        count = block.shape[0] * ways
        return lax.dynamic_slice_in_dim(whole, inside * count, count, axis=0)

    vec = jnp.zeros((16, 128), BF16)
    vectors = (b_query, b_value, b_output, b_outer, gain_one, shift_one, gain_two, shift_two)
    for at, vector in enumerate(vectors + (b_inner,)):
        line = regroup(vector)
        vec += jnp.pad(line[None, :], ((at, 15 - at), (0, 128 - line.shape[0])))
    qkv_weights = [regroup(w) for w in (w_query, w_key, w_value)]
    rest_weights = [regroup(w) for w in (w_output.T, w_inner, w_outer.T)]
    (hid_all, wq_all, qs, kv, probs, m_all, lse, ctxt, g_parts, layer_out, low, own, d_context, small) = (
        forward_attention(size, lengths, hidden_in, qkv_weights, rest_weights, vec, cotangent)
    )
    (g_query, g_key, g_value, g_output, g_inner, g_outer, g_small, g_bias, grad_in) = (
        backward_attention(
            size,
            d_context,
            qs,
            m_all,
            lse,
            ctxt,
            hid_all,
            wq_all,
            low,
            own,
            small,
            kv,
            probs,
            g_parts,
        )
    )

    def spread(block):
        if ways == 1:
            return block
        count = block.shape[0]
        whole = jnp.zeros((count * size,) + block.shape[1:], block.dtype)
        whole = lax.dynamic_update_slice_in_dim(whole, block, inside * count, axis=0)
        return lax.psum_scatter(whole, "col", scatter_dimension=0, tiled=True)

    arrays = [g_query, g_key, g_value, g_output, g_inner, g_outer, grad_in, layer_out]
    arrays = finish(size, g_small, g_bias, arrays)
    g_query, g_key, g_value, g_output, g_inner, g_outer, grad_in, layer_out = arrays[:8]
    pieces = [spread(piece) for piece in arrays[8:]]
    g_b_output, g_b_outer, g_gain_one, g_shift_one, g_gain_two, g_shift_two = pieces[:6]
    g_b_inner, g_b_query, g_b_value = pieces[6:]
    return (
        layer_out,
        grad_in,
        spread(g_query),
        spread(g_key),
        spread(g_value),
        spread(g_output).T,
        spread(g_inner),
        spread(g_outer).T,
        g_b_query,
        g_b_value,
        g_b_output,
        g_b_inner,
        g_b_outer,
        g_gain_one,
        g_shift_one,
        g_gain_two,
        g_shift_two,
    )


def solution(mesh):
    cols = mesh.shape["col"]
    group = max(s for s in range(SPAN, cols + 1, 4) if cols % s == 0 and D // s % 16 == 0)
    token, weight, turned = P("col", "row"), P("col", "row"), P("row", "col")
    vector = P(("row", "col"))
    return jax.shard_map(
        functools.partial(per_device, group),
        mesh=mesh,
        in_specs=(token, token, P()) + (weight,) * 3 + (turned, weight, turned) + (vector,) * 9,
        out_specs=(token, token) + (weight,) * 3 + (turned, weight, turned) + (vector,) * 9,
        check_vma=False,
    )
```

```python
import functools

import jax
import jax.numpy as jnp
from jax import lax
from jax.experimental import pallas as pl
from jax.experimental.pallas import tpu as pltpu
from jax.sharding import PartitionSpec as P

D = 768
HALF = 384
HEAD_DIM = 64
FF_HALF = 1536
PAIRS = 3
SPAN = 8
EPSILON = 1e-12
MASKED = -1e30
MESH = pl.DeviceIdType.MESH
F32 = jnp.float32
BF16 = jnp.bfloat16
FIRST = HALF + FF_HALF
REST = HALF + 2 * FF_HALF
QKV = 3 * HALF


def dot(left, right, contract):
    return lax.dot_general(left, right, (contract, ((), ())), preferred_element_type=F32)


NN = ((1,), (0,))
NT = ((1,), (1,))
TN = ((0,), (0,))


class Place:
    def __init__(self, size):
        self.size = size
        self.planes = size // 4
        self.r = lax.axis_index("row")
        col = lax.axis_index("col")
        self.base = lax.div(col, size) * size
        inner = lax.rem(col, size)
        self.slot = lax.div(col, SPAN)
        self.block = lax.rem(col, SPAN)
        self.z = lax.div(inner, 4)
        self.y = lax.rem(lax.div(inner, 2), 2)
        self.j = lax.rem(inner, 2)
        self.zl = lax.rem(self.z, 2)

    def plane(self, step):
        return lax.rem(self.z + step + self.planes, self.planes)

    def device(self, r, z, y, j):
        return (r, self.base + z * 4 + y * 2 + j)

    def to_z(self, step):
        return self.device(self.r, self.plane(step), self.y, self.j)

    def to_z_near(self):
        return self.device(self.r, self.z - self.zl + (1 - self.zl), self.y, self.j)

    def to_y(self):
        return self.device(self.r, self.z, 1 - self.y, self.j)

    def to_x(self):
        return self.device(1 - self.r, self.z, self.y, self.j)

    def to_core(self):
        return self.device(self.r, self.z, self.y, 1 - self.j)

    def col_block(self, z, y, j):
        return z * 4 + y * 2 + j

    def any_block(self, r, z, y, j):
        return r * self.size + z * 4 + y * 2 + j

    def near_block(self, dz, dy, j):
        return lax.rem(self.zl + dz, 2) * 4 + lax.rem(self.y + dy, 2) * 2 + j


def meet(place):
    barrier = pltpu.get_barrier_semaphore()
    peers = [place.to_z(step) for step in range(1, place.planes)]
    peers += [place.to_y(), place.to_x(), place.to_core()]
    for peer in peers:
        pl.semaphore_signal(barrier, inc=1, device_id=peer, device_id_type=MESH)
    pl.semaphore_wait(barrier, len(peers))


def send(src, dst, sems, index, peer):
    return pltpu.make_async_remote_copy(
        src_ref=src,
        dst_ref=dst,
        send_sem=sems[0].at[index],
        recv_sem=sems[1].at[index],
        device_id=peer,
        device_id_type=MESH,
    )


class Gather:
    def __init__(self, place, own, full, sems, with_rows):
        self.place, self.own, self.full, self.sems = place, own, full, sems
        self.rows = 2 if with_rows else 1
        self.with_rows = with_rows
        n = place.planes
        self.at_y = n - 1
        self.at_x = self.at_y + n
        self.at_c = self.at_x + (2 * n if with_rows else 0)
        self.total = self.at_c + 2 * n * self.rows

    def index(self, n, k, m, j):
        p = self.place
        z, y = p.plane(-k), lax.rem(p.y + m, 2)
        if self.with_rows:
            return p.any_block(lax.rem(p.r + n, 2), z, y, j)
        return p.col_block(z, y, j)

    def move(self, number, peer, n, k, m, j, local):
        where = self.index(n, k, m, j)
        src = self.own if local else self.full.at[where]
        return send(src, self.full.at[where], self.sems, number, peer)

    def z_sends(self):
        p = self.place
        for step in range(1, p.planes):
            self.move(step - 1, p.to_z(step), 0, 0, 0, p.j, True).start()

    def z_done(self, k):
        p = self.place
        self.move(k - 1, p.to_z(k), 0, k, 0, p.j, False).wait_recv()

    def y_send(self, k):
        p = self.place
        self.move(self.at_y + k, p.to_y(), 0, k, 0, p.j, k == 0).start()

    def y_done(self, k):
        p = self.place
        self.move(self.at_y + k, p.to_y(), 0, k, 1, p.j, False).wait_recv()

    def x_send(self, k, m):
        p = self.place
        self.move(self.at_x + 2 * k + m, p.to_x(), 0, k, m, p.j, k + m == 0).start()

    def x_done(self, k, m):
        p = self.place
        self.move(self.at_x + 2 * k + m, p.to_x(), 1, k, m, p.j, False).wait_recv()

    def c_number(self, n, k, m):
        return self.at_c + (2 * k + m) * self.rows + n

    def c_send(self, n, k, m):
        p = self.place
        number = self.c_number(n, k, m)
        self.move(number, p.to_core(), n, k, m, p.j, n + k + m == 0).start()

    def c_done(self, n, k, m):
        p = self.place
        self.move(self.c_number(n, k, m), p.to_core(), n, k, m, 1 - p.j, False).wait_recv()

    def all_sent(self):
        for number in range(self.total):
            send(self.own, self.own, self.sems, number, self.place.to_core()).wait_send()


def spread_rows(tiles, picks, per, width):
    blocks = tiles.shape[0]
    flat = tiles.reshape(blocks * 16, 128)
    total = len(picks) * blocks
    line = lax.broadcasted_iota(jnp.int32, (total, blocks * 16), 0)
    at = lax.broadcasted_iota(jnp.int32, (total, blocks * 16), 1)
    wanted = jnp.zeros((total, blocks * 16), F32)
    for spot, pick in enumerate(picks):
        hit = at == (line - spot * blocks) * 16 + pick
        inside = (line >= spot * blocks) & (line < (spot + 1) * blocks)
        wanted = jnp.where(hit & inside, 1.0, wanted)
    taken = dot(wanted.astype(BF16), flat, NN).astype(BF16)
    lane = lax.broadcasted_iota(jnp.int32, (128, width), 1).astype(F32)
    group = jnp.floor((lane + 0.5) * (1.0 / per))
    place = lax.broadcasted_iota(jnp.int32, (128, width), 0).astype(F32)
    copies = jnp.where(lane - group * per == place, 1.0, 0.0).astype(BF16)
    wide = dot(taken, copies, NN)
    first = lax.broadcasted_iota(jnp.int32, (blocks, width), 0) * per
    column = lax.broadcasted_iota(jnp.int32, (blocks, width), 1)
    mask = (column >= first) & (column < first + per)
    rows = []
    for spot in range(len(picks)):
        part = jnp.where(mask, wide[spot * blocks : (spot + 1) * blocks], 0.0)
        rows.append(jnp.sum(part, axis=0, keepdims=True))
    return rows


def gelu_both(argument):
    spread = 1.0 + lax.erf(argument * 0.7071067811865476)
    bell = jnp.exp(argument * argument * -0.5) * 0.3989422804014327
    return 0.5 * argument * spread, 0.5 * spread + argument * bell


def norm_forward(resid, gain, shift):
    center = resid - jnp.mean(resid, axis=1, keepdims=True)
    scale = lax.rsqrt(jnp.mean(center * center, axis=1, keepdims=True) + EPSILON)
    normal = center * scale
    return normal * gain + shift, normal, scale


def norm_backward(incoming, normal, scale, gain):
    scaled = incoming * gain
    first = jnp.mean(scaled, axis=1, keepdims=True)
    second = jnp.mean(scaled * normal, axis=1, keepdims=True)
    result = scale * (scaled - first - normal * second)
    sums = jnp.sum(incoming * normal, axis=0, keepdims=True)
    return result, sums, jnp.sum(incoming, axis=0, keepdims=True)


def staged(kernel, size, inputs, outputs, picks, *refs):
    results, rest = list(refs[inputs : inputs + outputs]), refs[inputs + outputs :]
    held, sems, rest = rest[: len(picks)], rest[len(picks)], rest[len(picks) + 1 :]
    targets = [results[at] for at in picks]
    for at, ref in zip(picks, held):
        results[at] = ref

    def leave(number):
        return pltpu.make_async_copy(held[number], targets[number], sems.at[number])

    kernel(size, leave, *refs[:inputs], *results, *rest)
    for number in range(len(picks)):
        leave(number).wait()


def kernel_a(
    size,
    leave,
    lengths,
    hid,
    w_query,
    w_key,
    w_value,
    w_output,
    w_inner,
    w_outer,
    vec_in,
    cot,
    hid_out,
    wq_out,
    q_out,
    kv_out,
    p_out,
    m_out,
    lse_out,
    ctxt_out,
    g_out,
    final_out,
    low_out,
    own_out,
    d_out,
    small_out,
    hid_all,
    wq_own,
    wq_all,
    vec_all,
    one_own,
    one_all,
    two_all,
    kv,
    qs,
    qm,
    acc,
    high,
    low,
    pbuf,
    ctx_tp,
    ctx_in,
    cot_in,
    lay_out,
    lay_far,
    normed_ref,
    normal_ref,
    low_ref,
    slope_ref,
    act_ref,
    d_ref,
    one_send,
    one_recv,
    two_send,
    two_recv,
    wq_send,
    wq_recv,
    vec_send,
    vec_recv,
    kv_send,
    kv_recv,
    lone_send,
    lone_recv,
    local,
    p_sem,
):
    place = Place(size)
    rows = hid.shape[0]
    part = rows // 2
    n = place.planes
    r, y, j = place.r, place.y, place.j
    blk = w_query.shape[0]
    for at, source in enumerate((w_query, w_key, w_value)):
        wq_own[:, at * HALF : (at + 1) * HALF] = source[...]
    one_own[:, :HALF] = w_output[...]
    one_own[:, HALF:] = w_inner[...]
    with jax.named_scope("meet"):
        meet(place)

    single = (lone_send, lone_recv)
    own_rows = pl.ds(pl.multiple_of(r * part, part), part)
    other_rows = pl.ds(pl.multiple_of((1 - r) * part, part), part)
    to_hid = send(hid, hid_all.at[r], single, 0, place.to_x())
    to_hid.start()
    vec = Gather(place, vec_in, vec_all, (vec_send, vec_recv), True)
    wq = Gather(place, wq_own, wq_all, (wq_send, wq_recv), False)
    one = Gather(place, one_own, one_all, (one_send, one_recv), True)
    two = Gather(place, w_outer, two_all, (two_send, two_recv), True)
    for gather in (vec, wq):
        gather.z_sends()
        gather.y_send(0)
        gather.c_send(0, 0, 0)
    vec.x_send(0, 0)
    one.x_send(0, 0)
    one.y_send(0)
    two.x_send(0, 0)
    to_cot = send(cot.at[other_rows], cot_in.at[r], single, 1, place.to_x())
    to_cot.start()
    one.c_send(0, 0, 0)
    two.c_send(0, 0, 0)
    hid_all[r] = hid[...]
    mine = place.any_block(r, place.z, y, j)
    wq_all[place.col_block(place.z, y, j)] = wq_own[...]
    vec_all[mine] = vec_in[...]
    one_all[mine] = one_own[...]
    two_all[mine] = w_outer[...]
    cot_in[r] = cot[own_rows, :]
    for k in range(1, n):
        with jax.named_scope(f"qkv_plane_{k}"):
            for gather in (vec, wq):
                gather.z_done(k)
                gather.y_send(k)
                gather.c_send(0, k, 0)
            vec.x_send(k, 0)
    one.z_sends()
    two.y_send(0)
    for k in range(n):
        with jax.named_scope(f"qkv_side_{k}"):
            for gather in (vec, wq):
                gather.y_done(k)
                gather.c_send(0, k, 1)
            vec.x_send(k, 1)
    with jax.named_scope("qkv_core"):
        for k in range(n):
            for m in range(2):
                for gather in (vec, wq):
                    gather.c_done(0, k, m)
    with jax.named_scope("hidden"):
        send(hid, hid_all.at[1 - r], single, 0, place.to_x()).wait_recv()

    def rest_y(gather, k):
        gather.z_done(k)
        gather.y_send(k)
        gather.x_send(k, 0)
        gather.c_send(0, k, 0)

    def rest_x(gather, k):
        gather.y_done(k)
        gather.x_send(k, 1)
        gather.c_send(0, k, 1)

    def rest_c(gather, k, m):
        gather.x_done(k, m)
        gather.c_send(1, k, m)

    def rest_all(gather):
        for n_at in range(2):
            for k in range(n):
                for m in range(2):
                    if gather is not vec or n_at:
                        gather.c_done(n_at, k, m)

    hid_local = pltpu.make_async_copy(hid_all, hid_out, local.at[2])
    hid_local.start()
    wq_local = pltpu.make_async_copy(wq_all, wq_out, local.at[3])
    wq_local.start()

    kvs = (kv_send, kv_recv)

    def kv_block(i):
        pair, core = lax.div(i, 2), lax.rem(j + lax.rem(i, 2), 2)
        return place.near_block(lax.div(pair, 2), lax.rem(pair, 2), core)

    def kv_move(number, p):
        what = (0, 0, 0, 2, 0, 4, 2, 6)[number]
        if number % 2:
            peer = place.to_core()
        else:
            peer = place.to_y() if number == 2 else place.to_z_near()
        where = kv_block(jnp.int32(what))
        block = kv.at[where, pl.ds(2 * p, 2)]
        return send(block, block, kvs, SPAN * p + number, peer)

    def kv_start(number, p):
        kv_move(number, p).start()

    def kv_here(number, p):
        where = kv_block(jnp.int32(number))
        block = kv.at[where, pl.ds(2 * p, 2)]
        send(block, block, kvs, SPAN * p + number, place.to_core()).wait_recv()

    own_tiles = vec_all[pl.ds(r * size, size)]
    b_query, b_value = spread_rows(own_tiles, (0, 1), HALF // size, HALF)
    own = place.near_block(0, 0, j)
    half = size // 2
    for which in (1, 2, 0):
        columns = slice(which * HALF, (which + 1) * HALF)
        total = dot(hid_all[0], wq_all[:half, :, columns].reshape(HALF, HALF), NN)
        total += dot(hid_all[1], wq_all[half:, :, columns].reshape(HALF, HALF), NN)
        if which == 0:
            total += b_query
        if which == 2:
            total += b_value
        total = total.astype(BF16)
        for p in range(PAIRS):
            piece = total[:, p * 128 : (p + 1) * 128]
            if which == 0:
                lane = lax.broadcasted_iota(jnp.int32, (rows, 128), 1)
                piece = piece * jnp.asarray(0.125, BF16)
                qs[p] = piece
                qm[2 * p] = jnp.where(lane < HEAD_DIM, piece, jnp.zeros_like(piece))
                qm[2 * p + 1] = jnp.where(lane >= HEAD_DIM, piece, jnp.zeros_like(piece))
            else:
                kv[own, 2 * p + which - 1] = piece
        if which == 1:
            with jax.named_scope("after_key"):
                rest_x(one, 0)
        if which == 2:
            with jax.named_scope("after_value"):
                for number in (2, 4, 1):
                    kv_start(number, 0)
                rest_y(one, 1)
    acc[...] = jnp.zeros_like(acc)
    high[...] = jnp.full_like(high, MASKED)
    low[...] = jnp.zeros_like(low)

    q_local = pltpu.make_async_copy(qs, q_out, local.at[4])
    q_local.start()

    def vec_rows():
        for k in range(n):
            for m in range(2):
                rest_c(vec, k, m)

    def two_start():
        two.z_sends()

    events = {}

    def add(step, what, *inputs):
        events.setdefault(step, []).append(functools.partial(what, *inputs))

    add(1, kv_here, 1, 0)
    add(2, kv_here, 2, 0)
    add(2, kv_start, 3, 0)
    add(2, kv_start, 6, 0)
    add(3, kv_here, 3, 0)
    add(3, rest_x, one, 1)
    add(3, rest_y, one, 2)
    add(3, two_start)
    add(4, kv_here, 4, 0)
    add(4, kv_start, 5, 0)
    add(4, rest_y, one, 3)
    add(5, kv_here, 5, 0)
    add(5, kv_start, 2, 1)
    add(5, kv_start, 4, 1)
    add(5, kv_start, 1, 1)
    add(5, vec_rows)
    add(6, kv_here, 6, 0)
    add(6, kv_start, 7, 0)
    add(6, rest_x, two, 0)
    add(7, kv_here, 7, 0)
    add(7, rest_x, one, 2)
    add(8, rest_x, one, 3)
    add(8, rest_c, one, 0, 0)
    add(9, kv_here, 1, 1)
    add(9, rest_c, one, 1, 0)
    add(10, kv_here, 2, 1)
    add(10, kv_start, 3, 1)
    add(10, kv_start, 6, 1)
    add(11, kv_here, 3, 1)
    add(11, rest_y, two, 1)
    add(11, kv_start, 2, 2)
    add(11, kv_start, 4, 2)
    add(11, kv_start, 1, 2)
    add(12, kv_here, 4, 1)
    add(12, kv_start, 5, 1)
    add(13, kv_here, 5, 1)
    add(13, rest_c, one, 0, 1)
    add(13, rest_c, one, 1, 1)
    add(13, rest_y, two, 2)
    add(14, kv_here, 6, 1)
    add(14, kv_start, 7, 1)
    add(14, rest_x, two, 1)
    add(15, kv_here, 7, 1)
    add(15, rest_y, two, 3)
    add(16, rest_c, one, 2, 0)
    add(17, kv_here, 1, 2)
    add(17, rest_c, one, 3, 0)
    add(17, rest_x, two, 2)
    add(18, kv_here, 2, 2)
    add(18, kv_start, 3, 2)
    add(18, kv_start, 6, 2)
    add(19, kv_here, 3, 2)
    add(19, rest_c, one, 2, 1)
    add(20, kv_here, 4, 2)
    add(20, kv_start, 5, 2)
    add(20, rest_x, two, 3)
    add(21, kv_here, 5, 2)
    add(21, rest_c, one, 3, 1)
    add(22, kv_here, 6, 2)
    add(22, kv_start, 7, 2)
    add(22, rest_c, two, 0, 0)
    add(23, kv_here, 7, 2)
    add(23, rest_c, two, 0, 1)

    length = lengths[place.slot]

    def p_copy(t, slot):
        p, i = lax.div(t, SPAN), lax.rem(t, SPAN)
        return pltpu.make_async_copy(
            pbuf.at[slot], p_out.at[kv_block(i), pl.ds(2 * p, 2)], p_sem.at[slot]
        )

    def kv_copy(t):
        p, i = lax.div(t, SPAN), lax.rem(t, SPAN)
        where, both = kv_block(i), pl.ds(2 * p, 2)
        return pltpu.make_async_copy(
            kv.at[where, both], kv_out.at[where, both], local.at[8 + t]
        )

    steps = SPAN * PAIRS
    column = lax.broadcasted_iota(jnp.int32, (1, rows), 1) + place.block * rows
    keep_row = jnp.where(column < length, 1.0, 0.0)

    def to_ctx(p):
        lanes = pl.ds(p * 128, 128)
        return send(
            ctx_tp.at[other_rows, lanes], ctx_in.at[r, :, lanes], single, (2, 5, 6)[p], place.to_x()
        )

    def context(p):
        parts = []
        for h in range(2):
            g = 2 * p + h
            lse_out[g] = high[g] + jnp.log(low[g])
            parts.append(acc[g] / low[g])
        both = jnp.concatenate(parts, axis=0)
        ctxt_out[p] = both
        ctx_tp[:, p * 128 : (p + 1) * 128] = (both * keep_row).T.astype(BF16)
        to_ctx(p).start()
        ctx_in[r, :, p * 128 : (p + 1) * 128] = ctx_tp[own_rows, p * 128 : (p + 1) * 128]

    for p in range(PAIRS - 1):
        add(SPAN * (p + 1), context, p)

    def attend(t, carry):
        p, i = lax.div(t, SPAN), lax.rem(t, SPAN)
        for step, calls in sorted(events.items()):

            @pl.when(t == step)
            def _(calls=calls):
                for call in calls:
                    with jax.named_scope(f"at_{step}"):
                        call()

        kv_copy(t).start()

        slot = lax.rem(t, 2)

        @pl.when(t >= 2)
        def _():
            p_copy(t - 2, slot).wait()

        where = kv_block(i)
        place_of = lax.broadcasted_iota(jnp.int32, (rows, 128), 0) + where * rows
        bias = jnp.where(place_of < length, 0.0, MASKED)
        bias = jnp.concatenate([bias] * (rows // 128), axis=1)
        key = kv[where, 2 * p]
        value_t = kv[where, 2 * p + 1].T
        for h in range(2):
            g = 2 * p + h
            scores = dot(key, qm[g], NT) + bias
            top = jnp.max(scores, axis=0, keepdims=True)
            weights = jnp.exp(scores - top)
            below = jnp.sum(weights, axis=0, keepdims=True)
            rounded = weights.astype(BF16)
            pbuf[slot, h] = rounded
            term = dot(value_t[h * HEAD_DIM : (h + 1) * HEAD_DIM], rounded, NN)
            old = high[g]
            new = jnp.maximum(old, top)
            keep_old, keep_new = jnp.exp(old - new), jnp.exp(top - new)
            high[g] = new
            low[g] = low[g] * keep_old + below * keep_new
            acc[g] = acc[g] * keep_old + term * keep_new
            m_out[where, g] = top
        p_copy(t, slot).start()
        return carry

    lax.fori_loop(0, steps, attend, jnp.int32(0))

    context(PAIRS - 1)
    for number in range(3):
        leave(number).start()
    for t in (steps - 2, steps - 1):
        p_copy(jnp.int32(t), t % 2).wait()
    with jax.named_scope("one_all"):
        rest_all(vec)
        rest_all(one)
    six = spread_rows(vec_all[...], (2, 3, 4, 5, 6, 7), HALF // size, D)
    b_output, b_outer, gain_one, shift_one, gain_two, shift_two = six
    (b_inner,) = spread_rows(vec_all[...], (8,), FF_HALF // size, 2 * FF_HALF)
    hidden = jnp.concatenate([hid_all[0, own_rows, :], hid_all[1, own_rows, :]], axis=1)
    with jax.named_scope("context"):
        for p in range(PAIRS):
            lanes = pl.ds(p * 128, 128)
            send(
                ctx_tp.at[other_rows, lanes], ctx_in.at[1 - r, :, lanes], single, (2, 5, 6)[p], place.to_x()
            ).wait_recv()

    def weight(ref, h, columns):
        block = ref[h * size : (h + 1) * size, :, columns]
        return block.reshape(D, block.shape[2])

    out_cols, in_cols, all_cols = slice(0, HALF), slice(HALF, FIRST), slice(0, FF_HALF)
    with jax.named_scope("middle_one"):
        attn = dot(ctx_in[0], weight(one_all, 0, out_cols), NT)
        attn += dot(ctx_in[1], weight(one_all, 1, out_cols), NT) + b_output
        normed, normal, scale_one = norm_forward(hidden.astype(F32) + attn, gain_one, shift_one)
        normed_ref[...] = normed
        normal_ref[...] = normal
        low_ref[...] = normed.astype(BF16)
    with jax.named_scope("two_late"):
        rest_c(two, 1, 0)
        rest_c(two, 1, 1)
    for h in range(2):
        with jax.named_scope(f"inner_{h}"):
            span = slice(h * FF_HALF, (h + 1) * FF_HALF)
            inner = dot(low_ref[...], weight(one_all, h, in_cols), NN) + b_inner[:, span]
            value, slope = gelu_both(inner)
            act_ref[:, span] = value.astype(BF16)
            slope_ref[:, span] = slope
    with jax.named_scope("two_all"):
        for k in range(2, n):
            for m in range(2):
                rest_c(two, k, m)
        rest_all(two)
    with jax.named_scope("outer"):
        outer = dot(act_ref[:, :FF_HALF], weight(two_all, 0, all_cols), NT)
        outer += dot(act_ref[:, FF_HALF:], weight(two_all, 1, all_cols), NT) + b_outer
        result, normal_two, scale_two = norm_forward(normed_ref[...] + outer, gain_two, shift_two)
        lay_out[0] = result[:, :HALF].astype(BF16)
        lay_out[1] = result[:, HALF:].astype(BF16)
    to_lay = send(lay_out.at[1 - r], lay_far.at[r], single, 3, place.to_x())
    to_lay.start()
    spot = lax.broadcasted_iota(jnp.int32, (part, 1), 0) + place.block * rows + r * part
    keep = jnp.where(spot < length, 1.0, 0.0)
    with jax.named_scope("cotangent"):
        send(cot.at[other_rows], cot_in.at[1 - r], single, 1, place.to_x()).wait_recv()
    with jax.named_scope("norm_two"):
        seed = jnp.concatenate([cot_in[0], cot_in[1]], axis=1).astype(F32) * keep
        d_two, g_gain_two, g_shift_two = norm_backward(seed, normal_two, scale_two, gain_two)
        d_outer = d_two.astype(BF16)
        small_out[4:5] = g_gain_two
        small_out[5:6] = g_shift_two
        small_out[1:2] = jnp.sum(d_outer.astype(F32), axis=0, keepdims=True)
    d_normed = d_two
    d_outer_t = d_outer.T
    for h in range(2):
        with jax.named_scope(f"d_inner_{h}"):
            span = slice(h * FF_HALF, (h + 1) * FF_HALF)
            d_inner = dot(d_outer, weight(two_all, h, all_cols), NN) * slope_ref[:, span]
            d_inner = d_inner.astype(BF16)
            d_ref[:, span] = d_inner
            sums = jnp.sum(d_inner.astype(F32), axis=0, keepdims=True)
            small_out[6 + 2 * h : 7 + 2 * h] = sums[:, :D]
            small_out[7 + 2 * h : 8 + 2 * h] = sums[:, D:]
            d_normed += dot(d_inner, weight(one_all, h, in_cols), NT)
    with jax.named_scope("all_sent"):
        for gather in (vec, wq, one, two):
            gather.all_sent()
    own_col = pl.ds(pl.multiple_of(r * HALF, HALF), HALF)

    def give(number, ref, h, columns, target):
        return pltpu.make_async_copy(
            ref.at[pl.ds(h * size, size), :, columns],
            g_out.at[pl.ds(h * size, size), :, target],
            local.at[8 + SPAN * PAIRS + number],
        )

    gives = []
    for h in range(2):
        with jax.named_scope(f"g_outer_{h}"):
            span = slice(h * FF_HALF, (h + 1) * FF_HALF)
            term = dot(d_outer_t, act_ref[:, span], NN).astype(BF16)
            two_all[h * size : (h + 1) * size] = term.reshape(size, blk, FF_HALF)
            copy = give(h, two_all, h, pl.ds(0, FF_HALF), pl.ds(FIRST, FF_HALF))
            copy.start()
            gives.append(copy)
    with jax.named_scope("norm_one"):
        d_one, g_gain_one, g_shift_one = norm_backward(d_normed, normal_ref[...], scale_one, gain_one)
        d_attn = d_one.astype(BF16)
        small_out[2:3] = g_gain_one
        small_out[3:4] = g_shift_one
        small_out[0:1] = jnp.sum(d_attn.astype(F32), axis=0, keepdims=True)
        small_out[10:16] = jnp.zeros((6, D), F32)
        for h in range(2):
            low_out[h] = d_attn[:, h * HALF : (h + 1) * HALF]
        normed_ref[...] = d_one
        own_out[...] = normed_ref[:, own_col]
        for number in (4, 5, 7):
            leave(number).start()
    with jax.named_scope("d_context"):
        to_lay.wait_send()
        final_out[own_rows, :] = lay_out[r]
        for h in range(2):
            d_context = dot(d_attn, weight(one_all, h, out_cols), NN) * keep
            lay_out[h] = d_context.astype(BF16)
        to_d = send(lay_out.at[1 - r], d_out.at[own_rows], single, 4, place.to_x())
        to_d.start()
        d_out[own_rows, :] = lay_out[r]
    low_t = low_ref[...].T
    d_attn_t = d_attn.T
    for h in range(2):
        with jax.named_scope(f"g_inner_{h}"):
            span = slice(h * FF_HALF, (h + 1) * FF_HALF)
            term = dot(low_t, d_ref[:, span], NN).astype(BF16)
            one_all[h * size : (h + 1) * size, :, HALF:] = term.reshape(size, blk, FF_HALF)
            term = dot(d_attn_t, ctx_in[h], NN).astype(BF16)
            one_all[h * size : (h + 1) * size, :, :HALF] = term.reshape(size, blk, HALF)
            copy = give(2 + h, one_all, h, pl.ds(0, FIRST), pl.ds(0, FIRST))
            copy.start()
            gives.append(copy)
    for number in range(1, SPAN):
        for p in range(PAIRS):
            kv_move(number, p).wait_send()
    send(lay_far.at[r], lay_far.at[1 - r], single, 3, place.to_x()).wait_recv()
    final_out[other_rows, :] = lay_far[1 - r]
    leave(3).start()
    send(hid, hid, single, 0, place.to_x()).wait_send()
    send(ctx_in.at[0], ctx_in.at[0], single, 1, place.to_x()).wait_send()
    for p in range(PAIRS):
        to_ctx(p).wait_send()
    to_d.wait_send()
    send(lay_out.at[1 - r], d_out.at[other_rows], single, 4, place.to_x()).wait_recv()
    leave(6).start()
    for copy in [hid_local, wq_local, q_local] + gives:
        copy.wait()
    for t in range(SPAN * PAIRS):
        kv_copy(jnp.int32(t)).wait()


def forward_attention(size, lengths, hid, qkv_weights, rest_weights, vec, cot):
    rows = hid.shape[0]
    part = rows // 2
    blk = qkv_weights[0].shape[0]
    n = size // 4
    any_space = pl.BlockSpec(memory_space=pl.ANY)
    vmem = pl.BlockSpec(memory_space=pltpu.VMEM)
    shape = jax.ShapeDtypeStruct
    n_col, n_all = (n - 1) + n + 2 * n, (n - 1) + n + 2 * n + 4 * n
    dma = pltpu.SemaphoreType.DMA
    scratch = pltpu.VMEM
    results = (
        shape((2, rows, HALF), BF16),
        shape((size, blk, QKV), BF16),
        shape((PAIRS, rows, 128), BF16),
        shape((SPAN, 2 * PAIRS, rows, 128), BF16),
        shape((SPAN, 2 * PAIRS, rows, rows), BF16),
        shape((SPAN, 2 * PAIRS, 1, rows), F32),
        shape((2 * PAIRS, 1, rows), F32),
        shape((PAIRS, 128, rows), F32),
        shape((2 * size, blk, REST), BF16),
        shape((rows, HALF), BF16),
        shape((2, part, HALF), BF16),
        shape((part, HALF), F32),
        shape((rows, HALF), BF16),
        shape((16, D), F32),
    )
    picks = (5, 6, 7, 9, 10, 11, 12, 13)
    return pl.pallas_call(
        functools.partial(staged, kernel_a, size, 10, len(results), picks),
        out_shape=results,
        in_specs=[pl.BlockSpec(memory_space=pltpu.SMEM)] + [vmem] * 9,
        out_specs=[any_space] * len(results),
        scratch_shapes=[scratch(results[at].shape, results[at].dtype) for at in picks]
        + [dma((len(picks),))]
        + [
            scratch((2, rows, HALF), BF16),
            scratch((blk, QKV), BF16),
            scratch((size, blk, QKV), BF16),
            scratch((2 * size, 16, 128), BF16),
            scratch((blk, FIRST), BF16),
            scratch((2 * size, blk, FIRST), BF16),
            scratch((2 * size, blk, FF_HALF), BF16),
            scratch((SPAN, 2 * PAIRS, rows, 128), BF16),
            scratch((PAIRS, rows, 128), BF16),
            scratch((2 * PAIRS, rows, 128), BF16),
            scratch((2 * PAIRS, HEAD_DIM, rows), F32),
            scratch((2 * PAIRS, 1, rows), F32),
            scratch((2 * PAIRS, 1, rows), F32),
            scratch((2, 2, rows, rows), BF16),
            scratch((rows, HALF), BF16),
            scratch((2, part, HALF), BF16),
            scratch((2, part, HALF), BF16),
            scratch((2, part, HALF), BF16),
            scratch((2, part, HALF), BF16),
            scratch((part, D), F32),
            scratch((part, D), F32),
            scratch((part, D), BF16),
            scratch((part, 2 * FF_HALF), F32),
            scratch((part, 2 * FF_HALF), BF16),
            scratch((part, 2 * FF_HALF), BF16),
            dma((n_all,)),
            dma((n_all,)),
            dma((n_all,)),
            dma((n_all,)),
            dma((n_col,)),
            dma((n_col,)),
            dma((n_all,)),
            dma((n_all,)),
            dma((SPAN * PAIRS,)),
            dma((SPAN * PAIRS,)),
            dma((7,)),
            dma((7,)),
            dma((12 + SPAN * PAIRS,)),
            dma((2,)),
        ],
        compiler_params=pltpu.CompilerParams(
            collective_id=0, has_side_effects=True, vmem_limit_bytes=62 * 2**20
        ),
        name="forward_attention",
    )(lengths, hid, *qkv_weights, *rest_weights, vec, cot)


def kernel_c(
    size,
    leave,
    d_ctx,
    qs,
    m_in,
    lse_in,
    ctxt,
    hid_all,
    wq_in,
    dres_low,
    dres_own,
    small_in,
    kv_in,
    p_in,
    g_in,
    query_out,
    key_out,
    value_out,
    wo_out,
    wi_out,
    wu_out,
    small_out,
    bias_out,
    grad_out,
    wq_all,
    dtot,
    delta,
    qm,
    acc,
    kv,
    pbuf,
    big,
    cb,
    rb,
    st,
    b1,
    b2,
    b3,
    b4,
    d_all,
    hid_t,
    far,
    gq,
    q1,
    q2,
    q3,
    near,
    bias_own,
    bias_got,
    vec_sum,
    vec_got,
    one_send,
    one_recv,
    kv_send,
    kv_recv,
    g_send,
    g_recv,
    q_send,
    q_recv,
    s_send,
    s_recv,
    v_send,
    v_recv,
    load,
    p_sem,
):
    place = Place(size)
    rows = qs.shape[1]
    part = rows // 2
    n = place.planes
    r, y, j = place.r, place.y, place.j
    half = size // 2
    blk = wq_all.shape[1]
    own_rows = pl.ds(pl.multiple_of(r * part, part), part)

    def b_block(i):
        pair, core = lax.div(i, 2), lax.rem(j + 1 + lax.rem(i, 2), 2)
        return place.near_block(1 - lax.div(pair, 2), 1 - lax.rem(pair, 2), core)

    def kv_load(i):
        return pltpu.make_async_copy(kv_in.at[b_block(i)], kv.at[i], load.at[i])

    def p_load(t, slot):
        p, i = lax.div(t, SPAN), lax.rem(t, SPAN)
        return pltpu.make_async_copy(
            p_in.at[b_block(i), pl.ds(2 * p, 2)], pbuf.at[slot], p_sem.at[slot]
        )

    def index(other, k, m):
        return 2 * n * other + 2 * ((k + n - 1) % n) + m

    def g_block(at, core):
        n_at, m = at // (2 * n), at % 2
        k = ((at % (2 * n)) // 2 + 1) % n
        return place.any_block(
            lax.rem(r + 1 + n_at, 2), place.plane(k), lax.rem(y + 1 + m, 2), core
        )

    def g_load(at):
        return pltpu.make_async_copy(g_in.at[g_block(at, j)], st.at[at], load.at[8 + at])

    def loop(count, body):
        def step(at, carry):
            body(at)
            return carry

        lax.fori_loop(0, count, step, jnp.int32(0))

    needed = [(0, 2, 0), (0, 1, 0), (0, 2, 1), (1, 1, 0), (0, 3, 0), (0, 3, 1), (1, 2, 0), (1, 2, 1)]
    needed += [(0, 1, 1), (1, 1, 1), (0, 0, 0), (0, 0, 1), (1, 3, 0), (1, 3, 1), (1, 0, 0), (1, 0, 1)]
    needed = [index(*at) for at in needed]
    p_load(jnp.int32(0), 0).start()
    for at in needed[:4]:
        g_load(at).start()
    loop(SPAN, lambda i: kv_load(i).start())
    for at in needed[4:]:
        g_load(at).start()
    wq_load = pltpu.make_async_copy(wq_in, wq_all, load.at[8 + 4 * n])
    wq_load.start()
    lane = lax.broadcasted_iota(jnp.int32, (rows, 128), 1)
    for p in range(PAIRS):
        piece = qs[p]
        qm[2 * p] = jnp.where(lane < HEAD_DIM, piece, jnp.zeros_like(piece))
        qm[2 * p + 1] = jnp.where(lane >= HEAD_DIM, piece, jnp.zeros_like(piece))
    acc[...] = jnp.zeros_like(acc)
    for which in range(2):
        hid_t[which] = hid_all[which].T
    far[...] = jnp.zeros_like(far)
    far[own_rows, :] = dres_low[1 - r].astype(F32)
    grad_out[...] = jnp.zeros_like(grad_out)
    grad_out[own_rows, :] = dres_own[...]
    upper = lax.broadcasted_iota(jnp.int32, (128, rows), 0) < HEAD_DIM
    for p in range(PAIRS):
        turned = d_ctx[:, p * 128 : (p + 1) * 128].astype(F32).T
        product = turned * ctxt[p]
        delta[2 * p] = jnp.sum(product[:HEAD_DIM], axis=0, keepdims=True)
        delta[2 * p + 1] = jnp.sum(product[HEAD_DIM:], axis=0, keepdims=True)
        dtot[2 * p] = jnp.where(upper, turned, 0.0)
        dtot[2 * p + 1] = jnp.where(upper, 0.0, turned)
    with jax.named_scope("meet"):
        meet(place)
    single = (one_send, one_recv)
    gs = (g_send, g_recv)
    ks = (kv_send, kv_recv)
    at_x, at_y, at_z = 4 * n, 6 * n, 8 * n

    send(small_in, vec_got.at[0], (v_send, v_recv), 0, place.to_x()).start()

    def c_move(at):
        return send(g_in.at[g_block(at, 1 - j)], b1.at[at], gs, at, place.to_core())

    for at in needed:
        c_move(at).start()

    def fold(target, source, at):
        total = target[at].astype(F32) + source.astype(F32)
        target[at] = total.astype(BF16)

    def pieces(p):
        return pl.ds(2 * p, 2)

    def core_send(p, pair):
        return send(
            big.at[2 * pair, pieces(p)], cb.at[pair, pieces(p)], ks, 4 * p + pair, place.to_core()
        )

    def core_add(p, pair):
        core_send(p, pair).wait_recv()
        for piece in (2 * p, 2 * p + 1):
            fold(big, cb[pair, piece], (2 * pair + 1, piece))

    def hop(p, pair):
        peer = place.to_y() if pair == 2 else place.to_z_near()
        number = 4 * PAIRS + 3 * p + pair
        return send(big.at[2 * pair + 1, pieces(p)], rb.at[pair, pieces(p)], ks, number, peer)

    def hop_add(p):
        hop(p, 0).wait_recv()
        for piece in (2 * p, 2 * p + 1):
            fold(big, rb[0, piece], (5, piece))

    def g_core_add(other, k, m):
        at = index(other, k, m)
        c_move(at).wait_recv()
        g_load(at).wait()
        fold(st, b1[at], at)

    def gx(k, m):
        at = index(0, k, m)
        return send(st.at[at], b2.at[at], gs, at_x + at, place.to_x())

    def gx_add(k, m):
        gx(k, m).wait_recv()
        fold(st, b2[index(0, k, m)], index(1, k, m))

    def gy(k, other):
        slot = 2 * k + other
        return send(st.at[index(other, k, 0)], b3.at[slot], gs, at_y + slot, place.to_y())

    def gy_add(k, other):
        gy(k, other).wait_recv()
        fold(st, b3[2 * k + other], index(other, k, 1))

    def gz(k):
        return send(st.at[index(1, k, 1)], b4.at[k - 1], gs, at_z + k - 1, place.to_z(k))

    vz = (v_send, v_recv)

    def vector(number):
        level = min(number, 3)
        step = max(number - 2, 1)
        peer = (place.to_x(), place.to_core(), place.to_y(), place.to_z(step))[level]
        source = small_in if level == 0 else vec_sum.at[level - 1]
        return send(source, vec_got.at[number], vz, number, peer)

    def vector_add(level):
        vector(level).wait_recv()
        before = small_in[...] if level == 0 else vec_sum[level - 1]
        vec_sum[level] = before + vec_got[level]

    qz = (q_send, q_recv)

    def q_core(p):
        return send(gq.at[p, 1 - j], q1.at[p], qz, (n + 1) * p, place.to_core())

    def q_side(p):
        return send(gq.at[p, j, 1 - y], q2.at[p], qz, (n + 1) * p + 1, place.to_y())

    def q_plane(p, k):
        return send(
            gq.at[p, j, y, place.plane(k)], q3.at[p, k - 1], qz, (n + 1) * p + 1 + k, place.to_z(k)
        )

    def q_core_add(p):
        q_core(p).wait_recv()
        for side in range(2):
            fold(gq, q1[p, side], (p, j, side))

    def q_side_add(p):
        q_side(p).wait_recv()
        fold(gq, q2[p], (p, j, y))

    def q_planes(p):
        for k in range(1, n):
            q_plane(p, k).start()

    def settle(p):
        core_send(p, 3).wait_recv()
        hop(p, 1).wait_recv()
        hop(p, 2).wait_recv()
        both = jnp.concatenate([acc[2 * p], acc[2 * p + 1]], axis=0)
        d_query = (both.T * 0.125).astype(BF16)
        d_all[p, :, 0:128] = d_query
        lanes = slice(p * 128, (p + 1) * 128)
        bias_own[0, 0:1, lanes] = jnp.sum(d_query.astype(F32), axis=0, keepdims=True)
        for at in range(2):
            piece = 2 * p + at
            total = big[7, piece].astype(F32) + cb[3, piece].astype(F32)
            total += rb[1, piece].astype(F32) + rb[2, piece].astype(F32)
            low = total.astype(BF16)
            d_all[p, :, (at + 1) * 128 : (at + 2) * 128] = low
        bias_own[0, 1:2, lanes] = jnp.sum(low.astype(F32), axis=0, keepdims=True)

    def input_term(p, which):
        parts = []
        for at in range(3):
            columns = slice(at * HALF + p * 128, at * HALF + (p + 1) * 128)
            parts.append(wq_all[pl.ds(which * half, half), :, columns].reshape(HALF, 128))
        return dot(d_all[p], jnp.concatenate(parts, axis=1), NT)

    def far_term(p):
        far[...] = far[...] + input_term(p, 1 - r)

    def own_term(p):
        grad_out[...] = grad_out[...] + input_term(p, r)

    def grads(p):
        for which in range(2):
            term = dot(hid_t[which], d_all[p], NN).astype(BF16)
            for b in range(half):
                c = which * half + b
                gq[p, c % 2, (c // 2) % 2, c // 4] = term[b * blk : (b + 1) * blk]

    events = {}

    def add(step, what, *inputs):
        events.setdefault(step, []).append(functools.partial(what, *inputs))

    def start(step, what, *inputs):
        add(step, lambda: what(*inputs).start())

    bias_own[0, 2:8] = jnp.zeros((6, HALF), F32)
    add(14, wq_load.wait)
    add(0, g_core_add, 0, 2, 0)
    start(0, gx, 2, 0)
    add(0, g_core_add, 0, 1, 0)
    start(0, gy, 1, 0)
    add(1, g_core_add, 0, 2, 1)
    add(1, g_core_add, 1, 1, 0)
    start(2, gx, 2, 1)
    start(2, gy, 1, 1)
    add(2, g_core_add, 0, 3, 0)
    add(3, vector_add, 0)
    start(3, vector, 1)
    start(3, gx, 3, 0)
    add(3, g_core_add, 0, 3, 1)
    late = [(1, 2, 0), (1, 2, 1), (0, 1, 1), (1, 1, 1), (0, 0, 0), (0, 0, 1), (1, 3, 0), (1, 3, 1)]
    for at, what in enumerate(late + [(1, 0, 0), (1, 0, 1)]):
        add(4 + at, g_core_add, *what)
    add(6, vector_add, 1)
    start(6, vector, 2)
    add(8, gx_add, 2, 0)
    add(8, gy_add, 1, 0)
    add(9, gx_add, 2, 1)
    start(9, gy, 2, 1)
    add(9, gy_add, 1, 1)
    start(10, gx, 1, 1)
    start(10, gx, 3, 1)
    start(10, gx, 0, 0)
    start(11, gx, 0, 1)
    add(11, vector_add, 2)
    for step in range(1, n):
        start(11, vector, 2 + step)
    add(15, gy_add, 2, 1)
    start(15, gz, 2)
    add(18, gx_add, 1, 1)
    add(19, gx_add, 3, 0)
    add(19, gx_add, 3, 1)
    start(19, gy, 3, 1)
    for p in range(PAIRS):
        base = SPAN * p
        late = 7 if p == PAIRS - 1 else 8
        start(base + 2, core_send, p, 0)
        add(base + 3, core_add, p, 0)
        start(base + 3, hop, p, 0)
        start(base + 4, core_send, p, 1)
        add(base + 5, core_add, p, 1)
        start(base + 5, hop, p, 1)
        start(base + 6, core_send, p, 2)
        add(base + 7, core_add, p, 2)
        add(base + late, hop_add, p)
        start(base + late, hop, p, 2)
        start(base + 8, core_send, p, 3)
        if p < PAIRS - 1:
            add(base + 14, settle, p)
            add(base + 14, grads, p)
            start(base + 14, q_core, p)
            add(base + 15, far_term, p)
            add(base + 15, own_term, p)
            add(base + 15, q_core_add, p)

    steps = SPAN * PAIRS

    def back(t, carry):
        p, i = lax.div(t, SPAN), lax.rem(t, SPAN)
        for step, calls in sorted(events.items()):
            if step < steps:

                @pl.when(t == step)
                def _(calls=calls):
                    with jax.named_scope(f"step_{step}"):
                        for call in calls:
                            call()

        slot = lax.rem(t, 2)

        @pl.when(t + 1 < steps)
        def _():
            p_load(t + 1, 1 - slot).start()

        @pl.when(p == 0)
        def _():
            kv_load(i).wait()

        p_load(t, slot).wait()
        where = b_block(i)
        key = kv[i, 2 * p]
        value = kv[i, 2 * p + 1]
        key_t = key.T
        d_key = d_value = None
        for h in range(2):
            g = 2 * p + h
            factor = jnp.exp(m_in[where, g] - lse_in[g])
            d_rows = (dtot[g] * factor).astype(BF16)
            weights = pbuf[slot, h]
            d_probs = dot(value, d_rows, NN)
            d_scores = (weights.astype(F32) * (d_probs - delta[g] * factor)).astype(BF16)
            value_term = dot(weights, d_rows, NT)
            key_term = dot(d_scores, qm[g], NN)
            acc[g] += dot(key_t[h * HEAD_DIM : (h + 1) * HEAD_DIM], d_scores, NN)
            d_key = key_term if d_key is None else d_key + key_term
            d_value = value_term if d_value is None else d_value + value_term
        big[i, 2 * p] = d_key.astype(BF16)
        big[i, 2 * p + 1] = d_value.astype(BF16)
        return carry

    lax.fori_loop(0, steps, back, jnp.int32(0))

    last = PAIRS - 1
    for call in events[steps]:
        call()
    gz(1).start()
    q_side(0).start()
    q_side(1).start()
    with jax.named_scope("settle"):
        settle(last)
    with jax.named_scope("far"):
        far_term(last)
        near[0] = far[...].astype(BF16)
    to_near = send(near.at[0], near.at[1], single, 0, place.to_x())
    with jax.named_scope("grads"):
        grads(last)
    to_near.start()
    q_core(last).start()
    sz = (s_send, s_recv)

    def small(number):
        level = min(number, 2)
        peer = (place.to_core(), place.to_y(), place.to_z(max(number - 1, 1)))[level]
        return send(bias_own.at[level], bias_got.at[number], sz, number, peer)

    small(0).start()
    with jax.named_scope("own"):
        own_term(last)
    with jax.named_scope("q_core"):
        q_core_add(last)
        small(0).wait_recv()
        bias_own[1] = bias_own[0] + bias_got[0]
    q_side(last).start()
    small(1).start()
    with jax.named_scope("g_x_0"):
        gx_add(0, 0)
        gx_add(0, 1)
    gy(0, 1).start()
    with jax.named_scope("g_y_3"):
        gy_add(3, 1)
    gz(3).start()
    with jax.named_scope("q_side_0"):
        q_side_add(0)
        q_planes(0)
    with jax.named_scope("q_side_1"):
        q_side_add(1)
        q_planes(1)
    with jax.named_scope("q_side_2"):
        q_side_add(last)
        q_planes(last)
        small(1).wait_recv()
        bias_own[2] = bias_own[1] + bias_got[1]
    for step in range(1, n):
        small(1 + step).start()
    with jax.named_scope("vectors"):
        total = vec_sum[2]
        for step in range(1, n):
            vector(2 + step).wait_recv()
            total = total + vec_got[2 + step]
        small_out[...] = total
        leave(6).start()

    def q_out(p):
        total = gq[p, j, y, place.z].astype(F32)
        for k in range(1, n):
            q_plane(p, k).wait_recv()
            total = total + q3[p, k - 1].astype(F32)
        lanes = slice(p * 128, (p + 1) * 128)
        query_out[:, lanes] = total[:, :128]
        key_out[:, lanes] = total[:, 128:256]
        value_out[:, lanes] = total[:, 256:]

    with jax.named_scope("q_out_0"):
        q_out(0)
    with jax.named_scope("near_wait"):
        to_near.wait_recv()
        grad_out[...] = grad_out[...] + near[1].astype(F32)
        leave(8).start()
    with jax.named_scope("g_z"):
        total = None
        for k in range(1, n):
            gz(k).wait_recv()
            got = b4[k - 1].astype(F32)
            total = got if total is None else total + got
    with jax.named_scope("g_y_0"):
        gy_add(0, 1)
        total = total + st[index(1, 0, 1)].astype(F32)
        wo_out[...] = total[:, :HALF]
        wi_out[...] = total[:, HALF:FIRST]
        wu_out[...] = total[:, FIRST:]
        for number in (3, 4, 5):
            leave(number).start()
    with jax.named_scope("q_out"):
        q_out(1)
        q_out(last)
        for number in range(3):
            leave(number).start()
        total = bias_own[2]
        for step in range(1, n):
            small(1 + step).wait_recv()
            total = total + bias_got[1 + step]
        bias_out[...] = total
        leave(7).start()

    for at in range(4 * n):
        c_move(at).wait_send()
    for k in range(n):
        first = k == 1
        for m in range(2):
            if not first or m == 1:
                gx(k, m).wait_send()
            if first or m == 1:
                gy(k, m).wait_send()
    for k in range(1, n):
        gz(k).wait_send()
        small(1 + k).wait_send()
        for p in range(PAIRS):
            q_plane(p, k).wait_send()
    small(0).wait_send()
    small(1).wait_send()
    for number in range(n + 2):
        vector(number).wait_send()
    for p in range(PAIRS):
        q_core(p).wait_send()
        q_side(p).wait_send()
        for pair in range(4):
            core_send(p, pair).wait_send()
        for pair in range(3):
            hop(p, pair).wait_send()
    to_near.wait_send()


def backward_attention(
    size, dctx, qs, m_in, lse_in, ctxt, hid_all, wq_all, dres_low, dres_own, small_in, kv_in, p_in, g_in
):
    rows = qs.shape[1]
    part = rows // 2
    blk = wq_all.shape[1]
    n = size // 4
    any_space = pl.BlockSpec(memory_space=pl.ANY)
    vmem = pl.BlockSpec(memory_space=pltpu.VMEM)
    shape = jax.ShapeDtypeStruct
    dma = pltpu.SemaphoreType.DMA
    scratch = pltpu.VMEM
    g_count, q_count = 4 * n + 2 * n + 2 * n + n - 1, PAIRS * (n + 1)
    results = (
        shape((blk, HALF), F32),
        shape((blk, HALF), F32),
        shape((blk, HALF), F32),
        shape((blk, HALF), F32),
        shape((blk, FF_HALF), F32),
        shape((blk, FF_HALF), F32),
        shape((16, D), F32),
        shape((8, HALF), F32),
        shape((rows, HALF), F32),
    )
    return pl.pallas_call(
        functools.partial(staged, kernel_c, size, 13, len(results), range(len(results))),
        out_shape=results,
        in_specs=[vmem] * 6 + [any_space] + [vmem] * 3 + [any_space] * 3,
        out_specs=[any_space] * len(results),
        scratch_shapes=[scratch(a.shape, a.dtype) for a in results]
        + [dma((len(results),))]
        + [
            scratch(wq_all.shape, BF16),
            scratch((2 * PAIRS, 128, rows), F32),
            scratch((2 * PAIRS, 1, rows), F32),
            scratch((2 * PAIRS, rows, 128), BF16),
            scratch((2 * PAIRS, HEAD_DIM, rows), F32),
            scratch((SPAN, 2 * PAIRS, rows, 128), BF16),
            scratch((2, 2, rows, rows), BF16),
            scratch((SPAN, 2 * PAIRS, rows, 128), BF16),
            scratch((4, 2 * PAIRS, rows, 128), BF16),
            scratch((3, 2 * PAIRS, rows, 128), BF16),
            scratch((4 * n, blk, REST), BF16),
            scratch((4 * n, blk, REST), BF16),
            scratch((2 * n, blk, REST), BF16),
            scratch((2 * n, blk, REST), BF16),
            scratch((n - 1, blk, REST), BF16),
            scratch((PAIRS, rows, HALF), BF16),
            scratch((2, HALF, rows), BF16),
            scratch((rows, HALF), F32),
            scratch((PAIRS, 2, 2, n, blk, HALF), BF16),
            scratch((PAIRS, 2, n, blk, HALF), BF16),
            scratch((PAIRS, n, blk, HALF), BF16),
            scratch((PAIRS, n - 1, blk, HALF), BF16),
            scratch((2, rows, HALF), BF16),
            scratch((3, 8, HALF), F32),
            scratch((n + 1, 8, HALF), F32),
            scratch((3, 16, D), F32),
            scratch((n + 2, 16, D), F32),
            dma((1,)),
            dma((1,)),
            dma((7 * PAIRS,)),
            dma((7 * PAIRS,)),
            dma((g_count,)),
            dma((g_count,)),
            dma((q_count,)),
            dma((q_count,)),
            dma((n + 1,)),
            dma((n + 1,)),
            dma((n + 2,)),
            dma((n + 2,)),
            dma((9 + 4 * n,)),
            dma((2,)),
        ],
        compiler_params=pltpu.CompilerParams(
            collective_id=1, has_side_effects=True, vmem_limit_bytes=63 * 2**20
        ),
        name="backward_attention",
    )(dctx, qs, m_in, lse_in, ctxt, hid_all, wq_all, dres_low, dres_own, small_in, kv_in, p_in, g_in)


def kernel_d(size, per, count, *refs):
    sources, targets = refs[:count], refs[count : 2 * count - 2]
    vectors = refs[2 * count - 2 : 2 * count + 7]
    held, come, go = refs[2 * count + 7 : 3 * count + 7], refs[-2], refs[-1]
    small, bias = held[0], held[1]
    loads = [pltpu.make_async_copy(s, h, come.at[at]) for at, (s, h) in enumerate(zip(sources, held))]
    stores = [pltpu.make_async_copy(h, t, go.at[at]) for at, (h, t) in enumerate(zip(held[2:], targets))]
    for copy in loads:
        copy.start()
    loads[0].wait()
    loads[1].wait()
    row = lax.axis_index("row")
    inside = lax.rem(lax.axis_index("col"), size)
    start = row * HALF + inside * per
    lines = small[...]
    turned = pltpu.roll(lines, D - start, 1)
    for at in range(6):
        vectors[at][...] = turned[at, :per]
    spot = inside * 4 * per
    hidden = pltpu.roll(lines, D - lax.rem(spot, D), 1)[:, :128]
    wanted = 6 + 2 * row + lax.div(spot, D)
    line = lax.broadcasted_iota(jnp.int32, hidden.shape, 0)
    vectors[6][...] = jnp.sum(jnp.where(line == wanted, hidden, 0.0), axis=0)[: 4 * per]
    turned = pltpu.roll(bias[...], HALF - inside * per, 1)
    for at in range(2):
        vectors[7 + at][...] = turned[at, :per]
    for load, store in zip(loads[2:], stores):
        load.wait()
        store.start()
    for store in stores:
        store.wait()


def finish(size, small, bias, arrays):
    space = pl.BlockSpec(memory_space=pl.ANY)
    shapes = [jax.ShapeDtypeStruct(a.shape, a.dtype) for a in arrays]
    arrays = [small, bias] + arrays
    count = len(arrays)
    return pl.pallas_call(
        functools.partial(kernel_d, size, HALF // size, count),
        out_shape=shapes
        + [jax.ShapeDtypeStruct((HALF // size * (4 if at == 6 else 1),), F32) for at in range(9)],
        in_specs=[space] * count,
        out_specs=[space] * (count - 2) + [pl.BlockSpec(memory_space=pltpu.VMEM)] * 9,
        scratch_shapes=[pltpu.VMEM(a.shape, a.dtype) for a in arrays]
        + [pltpu.SemaphoreType.DMA((count,))] * 2,
        compiler_params=pltpu.CompilerParams(vmem_limit_bytes=63 * 2**20),
        name="finish",
    )(*arrays)


def per_device(group, hidden_in, cotangent, lengths, *params):
    w_query, w_key, w_value, w_output, w_inner, w_outer = params[:6]
    b_query, b_value, b_output, b_inner, b_outer = params[6:11]
    gain_one, shift_one, gain_two, shift_two = params[11:]
    cols = lax.axis_size("col")
    size = group
    ways = cols // size
    inside = lax.axis_index("col") % size
    row = lax.axis_index("row")

    def regroup(block):
        if ways == 1:
            return block
        whole = lax.all_gather(block, "col", axis=0, tiled=True)
        count = block.shape[0] * ways
        return lax.dynamic_slice_in_dim(whole, inside * count, count, axis=0)

    vec = jnp.zeros((16, 128), BF16)
    vectors = (b_query, b_value, b_output, b_outer, gain_one, shift_one, gain_two, shift_two)
    for at, vector in enumerate(vectors + (b_inner,)):
        line = regroup(vector)
        vec += jnp.pad(line[None, :], ((at, 15 - at), (0, 128 - line.shape[0])))
    qkv_weights = [regroup(w) for w in (w_query, w_key, w_value)]
    rest_weights = [regroup(w) for w in (w_output.T, w_inner, w_outer.T)]
    (hid_all, wq_all, qs, kv, probs, m_all, lse, ctxt, g_parts, layer_out, low, own, d_context, small) = (
        forward_attention(size, lengths, hidden_in, qkv_weights, rest_weights, vec, cotangent)
    )
    (g_query, g_key, g_value, g_output, g_inner, g_outer, g_small, g_bias, grad_in) = (
        backward_attention(
            size,
            d_context,
            qs,
            m_all,
            lse,
            ctxt,
            hid_all,
            wq_all,
            low,
            own,
            small,
            kv,
            probs,
            g_parts,
        )
    )

    def spread(block):
        if ways == 1:
            return block
        count = block.shape[0]
        whole = jnp.zeros((count * size,) + block.shape[1:], block.dtype)
        whole = lax.dynamic_update_slice_in_dim(whole, block, inside * count, axis=0)
        return lax.psum_scatter(whole, "col", scatter_dimension=0, tiled=True)

    arrays = [g_query, g_key, g_value, g_output, g_inner, g_outer, grad_in, layer_out]
    arrays = finish(size, g_small, g_bias, arrays)
    g_query, g_key, g_value, g_output, g_inner, g_outer, grad_in, layer_out = arrays[:8]
    pieces = [spread(piece) for piece in arrays[8:]]
    g_b_output, g_b_outer, g_gain_one, g_shift_one, g_gain_two, g_shift_two = pieces[:6]
    g_b_inner, g_b_query, g_b_value = pieces[6:]
    return (
        layer_out,
        grad_in,
        spread(g_query),
        spread(g_key),
        spread(g_value),
        spread(g_output).T,
        spread(g_inner),
        spread(g_outer).T,
        g_b_query,
        g_b_value,
        g_b_output,
        g_b_inner,
        g_b_outer,
        g_gain_one,
        g_shift_one,
        g_gain_two,
        g_shift_two,
    )


def solution(mesh):
    cols = mesh.shape["col"]
    group = max(s for s in range(SPAN, cols + 1, 4) if cols % s == 0 and D // s % 16 == 0)
    token, weight, turned = P("col", "row"), P("col", "row"), P("row", "col")
    vector = P(("row", "col"))
    return jax.shard_map(
        functools.partial(per_device, group),
        mesh=mesh,
        in_specs=(token, token, P()) + (weight,) * 3 + (turned, weight, turned) + (vector,) * 9,
        out_specs=(token, token) + (weight,) * 3 + (turned, weight, turned) + (vector,) * 9,
        check_vma=False,
    )
```
